512 devices in a mesh: rows: 8 (over y), mp: 64 (over z, x, core).
Axes of the slice: x: 4, y: 8, z: 8, core: 2. Of those that a mesh axis runs over, the one named last changes fastest.
Arguments:
- lam_out: bfloat16 [1024, 64, 1024], P('mp', 'rows'), may hold values from -6 to 6
- q_down: bfloat16 [1024, 4096], P(None, 'rows'), may hold values from -127 to 127, as said below
- down_scale: float32 [1024], replicated, may hold values from 0.0001 to 0.001
- q_up: bfloat16 [4096, 1024], P('rows'), may hold values from -127 to 127, as said below
- up_scale: float32 [4096], P('rows'), may hold values from 5e-05 to 0.0005
- chan_slopes: bfloat16 [2, 1024, 8, 4096], P(None, 'mp', 'rows'), may hold values from -0.14941406 to 1.09375
- chan_icpt: bfloat16 [2, 1024, 8, 4096], P(None, 'mp', 'rows')
- tok_in_blocks: bfloat16 [16, 128, 128], replicated, may hold values from -0.25 to 0.25
- tok_out_blocks: bfloat16 [16, 128, 128], replicated, may hold values from -0.25 to 0.25
- block_cells: int32 [16], replicated, may hold values from 0 to 31, as said below
- tok_slopes: bfloat16 [2, 512, 8, 1024], P(None, None, 'rows', 'mp'), may hold values from -0.14941406 to 1.09375
- tok_icpt: bfloat16 [2, 512, 8, 1024], P(None, None, 'rows', 'mp')
Outputs:
- lam_in: bfloat16 [1024, 64, 1024], P(None, 'rows', 'mp')
- bias: float32 [64], P('rows')
The draws below stay inside these ranges and needn't reach their ends.
Inputs may be any that keep to these rules, and one draw needn't show every extreme that they name: `q_down`: integer values, 8-bit signed codes; a program may carry them across devices in any exact packed form, several codes to an element. `q_up`: integer values, 8-bit signed codes; a program may carry them across devices in any exact packed form, several codes to an element. `block_cells`: 16 distinct cells; cell h * 8 + u is hidden block h and token block u.
All inputs are finite; a program needn't handle non-finite values.
Results may differ from the reference program's by a relative error of at most 0.012.
Values may be sent and summed in bfloat16 or wider, within the bound.
No kernel may reach another device: no remote copies, remote signals or barrier semaphores. Data moves between devices by JAX's collectives and lax.ppermute only.
A program may use at most 64 MiB of HBM per device.

```python
import math
import jax
import jax.numpy as jnp
from jax import lax

D = 1024
CH = 4096
TH = 512
TOK = 1024
BLK = 128
NB = 16
SPEC = 8
IMAGES = 8
ROWS = 64
NHB = 4
NTB = 8


def draw_q_down(key, part):
    return jax.random.randint(jax.random.fold_in(key, 3), (D, CH), -127, 128).astype(jnp.bfloat16)


def draw_q_up(key, part):
    return jax.random.randint(jax.random.fold_in(key, 5), (CH, D), -127, 128).astype(jnp.bfloat16)


def draw_block_cells(key, part):
    return jax.random.permutation(jax.random.fold_in(key, 11), NHB * NTB)[:NB].astype(jnp.int32)


def draw_chan_icpt(key, part):
    inner = jax.random.fold_in(key, 7)
    noise = jax.random.normal(inner, (2, TOK, IMAGES, CH), jnp.float32)
    along_tok = 1.0 + 2.0 * jnp.arange(TOK, dtype=jnp.float32) / TOK
    along_hid = 1.0 + 2.0 * jnp.arange(CH, dtype=jnp.float32) / CH
    return (0.002 * noise * along_tok[None, :, None, None] * along_hid).astype(jnp.bfloat16)


def draw_tok_icpt(key, part):
    inner = jax.random.fold_in(key, 13)
    noise = jax.random.normal(inner, (2, TH, IMAGES, D), jnp.float32)
    along_chan = 1.0 + 2.0 * jnp.arange(D, dtype=jnp.float32) / D
    return (0.008 * noise * along_chan).astype(jnp.bfloat16)


def level_of(own_key, shape, pieces, least, largest):
    def one(axis_at, parts):
        draws = jax.random.uniform(jax.random.fold_in(jax.random.fold_in(own_key, 6), axis_at), (parts,), jnp.float32, least / len(pieces), largest / len(pieces))
        return jnp.repeat(jnp.exp(draws), shape[axis_at] // parts).reshape((-1,) + (1,) * (len(shape) - axis_at - 1))

    gain = one(*pieces[0])
    for cut in pieces[1:]:
        gain = gain * one(*cut)
    return gain


def normal_values(rng, extent, width, bound, pieces=(), kind=jnp.bfloat16):
    gain = level_of(rng, extent, pieces, -0.22, 0.18) if pieces else 1.0
    values = jax.random.normal(rng, extent, jnp.float32) * width * gain
    return jnp.minimum(jnp.maximum(values, -bound), bound).astype(kind)


def setup_inputs(seed: int = 0) -> dict:
    arg_keys = jax.random.split(jax.random.key(seed), 13)
    return {
        "lam_out": normal_values(arg_keys[0], (TOK, ROWS, D), 1.0, 6.0, ((0, 64), (1, 8))),
        "q_down": draw_q_down(jax.random.fold_in(arg_keys[12], 71), 0),
        "down_scale": jnp.clip(jnp.exp(jax.random.uniform(arg_keys[2], (D,), jnp.float32, math.log(0.0001), math.log(0.001))), 0.0001, 0.001),
        "q_up": draw_q_up(jax.random.fold_in(arg_keys[12], 71), 0),
        "up_scale": jnp.clip(jnp.exp(math.log(0.0005) - 2.3025852 * jax.random.uniform(arg_keys[4], (CH,), jnp.float32) ** level_of(arg_keys[4], (CH,), ((0, 8),), -0.2, 0.2)), 4.999999873689376e-05, 0.0005),
        "chan_slopes": jnp.clip(-0.14941406 + 1.2431641 * jax.random.uniform(arg_keys[5], (2, TOK, IMAGES, CH), jnp.float32) ** level_of(arg_keys[5], (2, TOK, IMAGES, CH), ((1, 64), (2, 8)), -0.2, 0.2), -0.14941406, 1.09375).astype(jnp.bfloat16),
        "chan_icpt": draw_chan_icpt(jax.random.fold_in(arg_keys[12], 71), 0),
        "tok_in_blocks": normal_values(arg_keys[7], (NB, BLK, BLK), (TOK // 2) ** -0.5, 0.25),
        "tok_out_blocks": normal_values(arg_keys[8], (NB, BLK, BLK), (TOK // 2) ** -0.5, 0.25),
        "block_cells": draw_block_cells(jax.random.fold_in(arg_keys[12], 71), 0),
        "tok_slopes": jnp.clip(-0.14941406 + 1.2431641 * jax.random.uniform(arg_keys[10], (2, TH, IMAGES, D), jnp.float32) ** level_of(arg_keys[10], (2, TH, IMAGES, D), ((2, 8), (3, 64)), -0.2, 0.2), -0.14941406, 1.09375).astype(jnp.bfloat16),
        "tok_icpt": draw_tok_icpt(jax.random.fold_in(arg_keys[12], 71), 0),
    }


def dense_blocks(blocks, cells, count_rows, count_cols):
    row_hot = (cells[:, None] // count_cols == jnp.arange(count_rows, dtype=jnp.int32)[None, :]).astype(jnp.float32)
    col_hot = (cells[:, None] % count_cols == jnp.arange(count_cols, dtype=jnp.int32)[None, :]).astype(jnp.float32)
    dense = jnp.einsum("bh,bt,bij->hitj", row_hot, col_hot, blocks.astype(jnp.float32))
    return dense.reshape(count_rows * BLK, count_cols * BLK).astype(jnp.bfloat16)


def reference(lam_out, q_down, down_scale, q_up, up_scale, chan_slopes, chan_icpt, tok_in_blocks, tok_out_blocks, block_cells, tok_slopes, tok_icpt):
    def channel_block(items):
        lam_blk, slope_blk, icpt_blk = items
        scaled = (lam_blk.astype(jnp.float32) * down_scale).astype(jnp.bfloat16)
        pre = jnp.dot(scaled.reshape(-1, D), q_down, preferred_element_type=jnp.float32)
        pre = pre.reshape(BLK, IMAGES, SPEC, CH)
        pos = jnp.maximum(pre, 0.0)
        neg = jnp.minimum(pre, 0.0)
        lower = slope_blk[0].astype(jnp.float32)[:, :, None, :]
        upper = slope_blk[1].astype(jnp.float32)[:, :, None, :]
        mid = pos * lower + neg * upper
        icpt_low = icpt_blk[0].astype(jnp.float32)[:, :, None, :]
        icpt_high = icpt_blk[1].astype(jnp.float32)[:, :, None, :]
        part_bias = jnp.sum(pos * icpt_low + neg * icpt_high, axis=(0, 3)).reshape(ROWS)
        mid_scaled = (mid * up_scale).astype(jnp.bfloat16).reshape(-1, CH)
        back = jnp.dot(mid_scaled, q_up, preferred_element_type=jnp.float32).reshape(BLK, ROWS, D)
        result = (lam_blk.astype(jnp.float32) + back).astype(jnp.bfloat16)
        return result, part_bias

    lam_blocks = lam_out.reshape(NTB, BLK, ROWS, D)
    slope_blocks = jnp.moveaxis(chan_slopes.reshape(2, NTB, BLK, IMAGES, CH), 1, 0)
    icpt_blocks = jnp.moveaxis(chan_icpt.reshape(2, NTB, BLK, IMAGES, CH), 1, 0)
    res_blocks, bias_parts = lax.map(channel_block, (lam_blocks, slope_blocks, icpt_blocks))
    lam_res = res_blocks.reshape(TOK, ROWS, D)
    bias_chan = jnp.sum(bias_parts, axis=0)

    tok_in = dense_blocks(tok_in_blocks, block_cells, NHB, NTB)
    swapped = (block_cells % NTB) * NHB + block_cells // NTB
    tok_out = dense_blocks(tok_out_blocks, swapped, NTB, NHB)
    columns = lam_res.reshape(TOK, ROWS * D)
    tpre = lax.dot_general(tok_out, columns, (((0,), (0,)), ((), ())), preferred_element_type=jnp.float32)
    tpre = tpre.reshape(TH, IMAGES, SPEC, D)
    pos = jnp.maximum(tpre, 0.0)
    neg = jnp.minimum(tpre, 0.0)
    lower = tok_slopes[0].astype(jnp.float32)[:, :, None, :]
    upper = tok_slopes[1].astype(jnp.float32)[:, :, None, :]
    tmid = (pos * lower + neg * upper).astype(jnp.bfloat16)
    icpt_low = tok_icpt[0].astype(jnp.float32)[:, :, None, :]
    icpt_high = tok_icpt[1].astype(jnp.float32)[:, :, None, :]
    bias_tok = jnp.sum(pos * icpt_low + neg * icpt_high, axis=(0, 3)).reshape(ROWS)
    back = lax.dot_general(tok_in, tmid.reshape(TH, ROWS * D), (((0,), (0,)), ((), ())), preferred_element_type=jnp.float32)
    lam_in = (lam_res.astype(jnp.float32) + back.reshape(TOK, ROWS, D)).astype(jnp.bfloat16)
    return lam_in, bias_chan + bias_tok
```

```python
import functools

import jax
import jax.numpy as jnp
from jax import lax
from jax.experimental import pallas as pl
from jax.experimental.pallas import tpu as pltpu
from jax.sharding import Mesh
from jax.sharding import PartitionSpec as P

D = 1024
CH = 4096
TH = 512
TOK = 1024
BLK = 128
NB = 16
SPEC = 8
NHB = 4
NTB = 8
F32 = jnp.float32
BF16 = jnp.bfloat16
I32 = jnp.int32
MP = ("z", "x", "core")
SWAP = [(0, 1), (1, 0)]
VMEM = 32 * 1024 * 1024

PART = 256
PACKED = 136
SCALE_ONE = float(2**38)


def pack_codes(parts):
    a, b, c, d = (p.astype(F32).astype(I32) for p in parts)
    return (a & 255) | ((b & 255) << 8) | ((c & 255) << 16) | (d << 24)


def unpack_codes(words, m):
    shifted = words << (24 - 8 * m) if m < 3 else words
    return (shifted >> 24).astype(F32).astype(BF16)


def pack_kernel(core_ref, down_ref, up_ref, scale_ref, out_ref):
    down = pack_codes([down_ref[m * 256 : (m + 1) * 256, :] for m in range(4)])
    for k in range(4):
        out_ref[0:64, k * PART : (k + 1) * PART] = down[k * 64 : (k + 1) * 64, :]
    out_ref[64:128, :] = pack_codes([up_ref[m * 64 : (m + 1) * 64, :] for m in range(4)])
    scale = (scale_ref[...] * SCALE_ONE).astype(I32)
    out_ref[128:136, :] = jnp.zeros((8, D), I32)
    out_ref[128:136, 0:PART] = jnp.broadcast_to(scale, (8, PART))


def pack(core, q_down, q_up, up_scale):
    return pl.pallas_call(
        pack_kernel,
        out_shape=jax.ShapeDtypeStruct((PACKED, D), I32),
        grid_spec=pltpu.PrefetchScalarGridSpec(
            num_scalar_prefetch=1,
            grid=(1,),
            in_specs=[
                pl.BlockSpec((D, PART), lambda i, c: (0, c[0])),
                pl.BlockSpec((PART, D), lambda i, c: (c[0], 0)),
                pl.BlockSpec((1, PART), lambda i, c: (0, c[0])),
            ],
            out_specs=pl.BlockSpec((PACKED, D), lambda i, c: (0, 0)),
        ),
        compiler_params=pltpu.CompilerParams(vmem_limit_bytes=VMEM),
        name="pack",
    )(core, q_down, q_up, up_scale.reshape(1, -1))


def dense_kernel(cells_ref, in_ref, out_ref, dense_in_ref, dense_out_ref):
    dense_in_ref[...] = jnp.zeros_like(dense_in_ref)
    dense_out_ref[...] = jnp.zeros_like(dense_out_ref)
    for b in range(NB):
        h = pl.multiple_of(cells_ref[b] // NTB * BLK, BLK)
        u = pl.multiple_of(cells_ref[b] % NTB * BLK, BLK)
        dense_in_ref[pl.ds(h, BLK), pl.ds(u, BLK)] = in_ref[b]
        dense_out_ref[pl.ds(u, BLK), pl.ds(h, BLK)] = out_ref[b]


def dense_blocks(cells, in_blocks, out_blocks):
    return pl.pallas_call(
        dense_kernel,
        out_shape=(
            jax.ShapeDtypeStruct((TH, TOK), BF16),
            jax.ShapeDtypeStruct((TOK, TH), BF16),
        ),
        in_specs=[
            pl.BlockSpec(memory_space=pltpu.SMEM),
            pl.BlockSpec(memory_space=pltpu.VMEM),
            pl.BlockSpec(memory_space=pltpu.VMEM),
        ],
        out_specs=(
            pl.BlockSpec(memory_space=pltpu.VMEM),
            pl.BlockSpec(memory_space=pltpu.VMEM),
        ),
        compiler_params=pltpu.CompilerParams(vmem_limit_bytes=VMEM),
        name="dense",
    )(cells, in_blocks, out_blocks)


def relaxed(pre, lower, upper, icpt_low, icpt_high):
    pos = jnp.maximum(pre, 0.0)
    neg = jnp.minimum(pre, 0.0)
    mid = pos * lower.astype(F32) + neg * upper.astype(F32)
    return mid, pos * icpt_low.astype(F32) + neg * icpt_high.astype(F32)


def channel_kernel(
    core_ref, words_ref, lam_ref, scaled_ref, relax_ref, keep_ref, send_ref, bias_ref, acc, down, up
):
    step = pl.program_id(0)
    for m in range(4):
        codes = unpack_codes(words_ref[0:64, :], m)
        for k in range(4):
            down[m * 256 + k * 64 : m * 256 + (k + 1) * 64, :] = codes[:, k * PART : (k + 1) * PART]
        up[m * 64 : (m + 1) * 64, :] = unpack_codes(words_ref[64:128, :], m)
    pre = jnp.dot(scaled_ref[...], down[...], preferred_element_type=F32)
    pre = pre.reshape(SPEC, 32, PART)
    mid, terms = relaxed(pre, relax_ref[0, 0], relax_ref[0, 1], relax_ref[0, 2], relax_ref[0, 3])
    terms = jnp.sum(terms.reshape(SPEC, 4, 8, PART), axis=1)
    terms = terms[:, :, 0:128] + terms[:, :, 128:256]
    scale = words_ref[128:129, 0:PART].astype(F32) * (1.0 / SCALE_ONE)
    weighted = (mid.reshape(SPEC * 32, PART) * scale).astype(BF16)
    part = jnp.dot(weighted, up[...], preferred_element_type=F32)

    @pl.when(step == 0)
    def _():
        acc[...] = part + 0.5 * lam_ref[...].astype(F32)
        bias_ref[...] = terms

    @pl.when(step > 0)
    def _():
        acc[...] += part
        bias_ref[...] += terms

    @pl.when(step == pl.num_programs(0) - 1)
    def _():
        own = core_ref[0] == 0
        turned = acc[...].T.reshape(32, 2, 16, 256)
        keep_ref[...] = jnp.where(own, turned[:, 0], turned[:, 1])
        send_ref[...] = jnp.where(own, turned[:, 1], turned[:, 0]).astype(BF16)


def channel_mlp(core, words, lam, scaled, relax):
    slices = words.shape[0] // PACKED
    whole = lambda *shape: pl.BlockSpec(shape, lambda i, c: (0,) * len(shape))
    return pl.pallas_call(
        channel_kernel,
        out_shape=(
            jax.ShapeDtypeStruct((32, 16, 256), F32),
            jax.ShapeDtypeStruct((32, 16, 256), BF16),
            jax.ShapeDtypeStruct((SPEC, 8, 128), F32),
        ),
        grid_spec=pltpu.PrefetchScalarGridSpec(
            num_scalar_prefetch=1,
            grid=(slices,),
            in_specs=[
                pl.BlockSpec((PACKED, D), lambda i, c: (i, 0)),
                whole(256, D),
                whole(256, D),
                pl.BlockSpec((1, 4, 32, PART), lambda i, c: (i, 0, 0, 0)),
            ],
            out_specs=(whole(32, 16, 256), whole(32, 16, 256), whole(SPEC, 8, 128)),
            scratch_shapes=[
                pltpu.VMEM((256, D), F32),
                pltpu.VMEM((D, PART), BF16),
                pltpu.VMEM((PART, D), BF16),
            ],
        ),
        compiler_params=pltpu.CompilerParams(vmem_limit_bytes=VMEM),
        name="channel",
    )(core, words, lam, scaled, relax)


def token_kernel(got_ref, dense_ref, slopes_ref, icpt_ref, columns_ref, mid_ref, bias_ref):
    lane = lax.broadcasted_iota(I32, (16, 128), 1) // 32
    for u in range(NTB):
        for a in range(2):
            v = [got_ref[4 * u + p, :, a * 128 : (a + 1) * 128].astype(F32) for p in range(4)]
            for bit in (1, 2):
                low = (lane & bit) == 0
                new = list(v)
                for p in range(4):
                    if p & bit == 0:
                        q = p + bit
                        new[p] = jnp.where(low, v[p], pltpu.roll(v[q], 32 * bit, 1))
                        new[q] = jnp.where(low, pltpu.roll(v[p], 128 - 32 * bit, 1), v[q])
                v = new
            for q in range(4):
                r = 4 * a + q
                columns_ref[r * 16 : (r + 1) * 16, u * 128 : (u + 1) * 128] = v[q].astype(BF16)
    pre = jnp.dot(columns_ref[...], dense_ref[...], preferred_element_type=F32)
    pre = pre.reshape(SPEC, 16, TH)
    mid, terms = relaxed(pre, slopes_ref[0], slopes_ref[1], icpt_ref[0], icpt_ref[1])
    mid_ref[...] = mid.reshape(SPEC * 16, TH).astype(BF16)
    terms = terms[:, 0:8, :] + terms[:, 8:16, :]
    bias_ref[...] = sum(terms[:, :, k * 128 : (k + 1) * 128] for k in range(NHB))


def token_mlp(got, dense_out, slopes, icpt):
    return pl.pallas_call(
        token_kernel,
        out_shape=(
            jax.ShapeDtypeStruct((SPEC * 16, TOK), BF16),
            jax.ShapeDtypeStruct((SPEC * 16, TH), BF16),
            jax.ShapeDtypeStruct((SPEC, 8, 128), F32),
        ),
        compiler_params=pltpu.CompilerParams(vmem_limit_bytes=VMEM),
        name="token",
    )(got, dense_out, slopes, icpt)


def back_kernel(columns_ref, mid_ref, dense_ref, out_ref):
    back = jnp.dot(mid_ref[...], dense_ref[...], preferred_element_type=F32)
    out_ref[...] = (columns_ref[...].astype(F32) + back).astype(BF16)


def token_back(columns, mid, dense_in):
    return pl.pallas_call(
        back_kernel,
        out_shape=jax.ShapeDtypeStruct((SPEC * 16, TOK), BF16),
        compiler_params=pltpu.CompilerParams(vmem_limit_bytes=VMEM),
        name="back",
    )(columns, mid, dense_in)


def on_device(
    lam_out,
    q_down,
    down_scale,
    q_up,
    up_scale,
    chan_slopes,
    chan_icpt,
    tok_in_blocks,
    tok_out_blocks,
    block_cells,
    tok_slopes,
    tok_icpt,
):
    core = lax.axis_index("core")
    first = core == 0
    core_arg = core.astype(I32).reshape(1)
    tok_dev = lam_out.shape[0]
    slices = lax.axis_size("rows")

    packed = pack(core_arg, q_down, q_up, up_scale)
    words = lax.all_gather(packed, "rows", axis=0, tiled=True)

    def paired(own, other, axis):
        return jnp.where(
            first,
            jnp.concatenate([own, other], axis),
            jnp.concatenate([other, own], axis),
        )

    by_row = jnp.swapaxes(lam_out, 0, 1)
    lam = paired(by_row, lax.ppermute(by_row, "core", SWAP), 1).reshape(-1, D)
    scaled = (lam.astype(F32) * down_scale).astype(BF16)
    relax = jnp.concatenate([chan_slopes, chan_icpt], 0).reshape(4, tok_dev, slices, 2, PART)
    relax = jnp.transpose(relax, (3, 2, 0, 1, 4))
    own = jnp.where(first, relax[0], relax[1])
    other = lax.ppermute(jnp.where(first, relax[1], relax[0]), "core", SWAP)
    relax = paired(own, other, 2)

    dense_in, dense_out = dense_blocks(block_cells, tok_in_blocks, tok_out_blocks)
    slopes = jnp.transpose(tok_slopes, (0, 2, 3, 1)).reshape(2, 16, TH)
    icpt = jnp.transpose(tok_icpt, (0, 2, 3, 1)).reshape(2, 16, TH)

    keep, send, chan_bias = channel_mlp(core_arg, words, lam, scaled, relax)
    summed = (keep + lax.ppermute(send, "core", SWAP).astype(F32)).astype(BF16)
    got = lax.all_to_all(summed, ("z", "x"), 0, 0, tiled=True)
    columns, mid, tok_bias = token_mlp(got, dense_out, slopes, icpt)
    own_bias = jnp.sum(chan_bias + tok_bias, axis=(1, 2))
    all_bias = lax.all_to_all(
        jnp.broadcast_to(own_bias[None, :], (64, SPEC)), MP, 0, 0, tiled=True
    )
    lam_in = token_back(columns, mid, dense_in)
    lam_in = jnp.transpose(lam_in.reshape(SPEC, 16, TOK), (2, 0, 1))
    return (lam_in, jnp.sum(all_bias, axis=0))


def solution(mesh):
    axes = Mesh(mesh.devices.reshape(8, 8, 4, 2), ("rows", "z", "x", "core"))
    return jax.shard_map(
        on_device,
        mesh=axes,
        in_specs=(
            P(MP, "rows", None),
            P(None, "rows"),
            P(),
            P("rows", None),
            P("rows"),
            P(None, MP, "rows", None),
            P(None, MP, "rows", None),
            P(),
            P(),
            P(),
            P(None, None, "rows", MP),
            P(None, None, "rows", MP),
        ),
        out_specs=(P(None, "rows", MP), P("rows")),
        check_vma=False,
    )
```

```python
import functools

import jax
import jax.numpy as jnp
from jax import lax
from jax.experimental import pallas as pl
from jax.experimental.pallas import tpu as pltpu
from jax.sharding import Mesh
from jax.sharding import PartitionSpec as P

D = 1024
CH = 4096
TH = 512
TOK = 1024
BLK = 128
NB = 16
SPEC = 8
NHB = 4
NTB = 8
F32 = jnp.float32
BF16 = jnp.bfloat16
I32 = jnp.int32
MP = ("z", "x", "core")
SWAP = [(0, 1), (1, 0)]
VMEM = 32 * 1024 * 1024

PART = 256
PACKED = 136
SCALE_ONE = float(2**38)


def pack_codes(parts):
    a, b, c, d = (p.astype(F32).astype(I32) for p in parts)
    return (a & 255) | ((b & 255) << 8) | ((c & 255) << 16) | (d << 24)


def unpack_codes(words, m):
    shifted = words << (24 - 8 * m) if m < 3 else words
    return (shifted >> 24).astype(F32).astype(BF16)


def pack_kernel(core_ref, down_hbm, up_hbm, scale_hbm, out_ref, down_ref, up_ref, scale_ref, sems):
    start = pl.multiple_of(core_ref[0] * PART, PART)
    copies = [
        pltpu.make_async_copy(down_hbm.at[:, pl.ds(start, PART)], down_ref, sems.at[0]),
        pltpu.make_async_copy(up_hbm.at[pl.ds(start, PART), :], up_ref, sems.at[1]),
        pltpu.make_async_copy(scale_hbm.at[:, pl.ds(start, PART)], scale_ref, sems.at[2]),
    ]
    for copy in copies:
        copy.start()
    out_ref[128:136, :] = jnp.zeros((8, D), I32)
    copies[0].wait()
    down = pack_codes([down_ref[m * 256 : (m + 1) * 256, :] for m in range(4)])
    for k in range(4):
        out_ref[0:64, k * PART : (k + 1) * PART] = down[k * 64 : (k + 1) * 64, :]
    copies[1].wait()
    out_ref[64:128, :] = pack_codes([up_ref[m * 64 : (m + 1) * 64, :] for m in range(4)])
    copies[2].wait()
    scale = (scale_ref[...] * SCALE_ONE).astype(I32)
    out_ref[128:136, 0:PART] = jnp.broadcast_to(scale, (8, PART))


def pack(core, q_down, q_up, up_scale):
    return pl.pallas_call(
        pack_kernel,
        out_shape=jax.ShapeDtypeStruct((PACKED, D), I32),
        in_specs=[pl.BlockSpec(memory_space=pltpu.SMEM)]
        + [pl.BlockSpec(memory_space=pltpu.HBM)] * 3,
        out_specs=pl.BlockSpec(memory_space=pltpu.VMEM),
        scratch_shapes=[
            pltpu.VMEM((D, PART), BF16),
            pltpu.VMEM((PART, D), BF16),
            pltpu.VMEM((1, PART), F32),
            pltpu.SemaphoreType.DMA((3,)),
        ],
        compiler_params=pltpu.CompilerParams(vmem_limit_bytes=60 * 1024 * 1024),
        name="pack",
    )(core, q_down, q_up, up_scale.reshape(1, -1))


def dense_kernel(cells_ref, in_ref, out_ref, dense_in_ref, dense_out_ref):
    dense_in_ref[...] = jnp.zeros_like(dense_in_ref)
    dense_out_ref[...] = jnp.zeros_like(dense_out_ref)
    for b in range(NB):
        h = pl.multiple_of(cells_ref[b] // NTB * BLK, BLK)
        u = pl.multiple_of(cells_ref[b] % NTB * BLK, BLK)
        dense_in_ref[pl.ds(h, BLK), pl.ds(u, BLK)] = in_ref[b]
        dense_out_ref[pl.ds(u, BLK), pl.ds(h, BLK)] = out_ref[b]


def dense_blocks(cells, in_blocks, out_blocks):
    return pl.pallas_call(
        dense_kernel,
        out_shape=(
            jax.ShapeDtypeStruct((TH, TOK), BF16),
            jax.ShapeDtypeStruct((TOK, TH), BF16),
        ),
        in_specs=[
            pl.BlockSpec(memory_space=pltpu.SMEM),
            pl.BlockSpec(memory_space=pltpu.VMEM),
            pl.BlockSpec(memory_space=pltpu.VMEM),
        ],
        out_specs=(
            pl.BlockSpec(memory_space=pltpu.VMEM),
            pl.BlockSpec(memory_space=pltpu.VMEM),
        ),
        compiler_params=pltpu.CompilerParams(vmem_limit_bytes=VMEM),
        name="dense",
    )(cells, in_blocks, out_blocks)


def relaxed(pre, lower, upper, icpt_low, icpt_high):
    pos = jnp.maximum(pre, 0.0)
    neg = jnp.minimum(pre, 0.0)
    mid = pos * lower.astype(F32) + neg * upper.astype(F32)
    return mid, pos * icpt_low.astype(F32) + neg * icpt_high.astype(F32)


def channel_kernel(count, split, first, last, *refs):
    where_ref, core_ref, lam_ref, scaled_ref, relax_ref = refs[:5]
    refs = refs[5:]
    if split:
        words, refs = [(refs[0], refs[1])], refs[2:]
    else:
        words, refs = [(w.at[0:64], w.at[64:PACKED]) for w in refs[:count]], refs[count:]
    if not first:
        acc_in, bias_in, *refs = refs
    *outs, down, up = refs
    total = bias = None
    for k, (down_words, up_words) in enumerate(words):
        for m in range(4):
            codes = unpack_codes(down_words[...], m)
            for q in range(4):
                rows = m * 256 + q * 64
                down[k, rows : rows + 64, :] = codes[:, q * PART : (q + 1) * PART]
            up[k, m * 64 : (m + 1) * 64, :] = unpack_codes(up_words[0:64, :], m)
        pre = jnp.dot(scaled_ref[...], down[k], preferred_element_type=F32)
        pre = pre.reshape(SPEC, 32, PART)
        bounds = relax_ref.at[where_ref[k]]
        mid, terms = relaxed(pre, bounds[0], bounds[1], bounds[2], bounds[3])
        terms = jnp.sum(terms.reshape(SPEC, 4, 8, PART), axis=1)
        terms = terms[:, :, 0:128] + terms[:, :, 128:256]
        scale = up_words[64:65, 0:PART].astype(F32) * (1.0 / SCALE_ONE)
        weighted = (mid.reshape(SPEC * 32, PART) * scale).astype(BF16)
        part = jnp.dot(weighted, up[k], preferred_element_type=F32)
        total = part if total is None else total + part
        bias = terms if bias is None else bias + terms
    if first:
        total = total + 0.5 * lam_ref[...].astype(F32)
    else:
        total = total + acc_in[...]
        bias = bias + bias_in[...]
    if last:
        keep_ref, send_ref, bias_ref = outs
        own = core_ref[0] == 0
        turned = total.T.reshape(32, 2, 16, 256)
        keep_ref[...] = jnp.where(own, turned[:, 0], turned[:, 1])
        send_ref[...] = jnp.where(own, turned[:, 1], turned[:, 0]).astype(BF16)
        bias_ref[...] = bias
    else:
        acc_ref, bias_ref = outs
        acc_ref[...] = total
        bias_ref[...] = bias


def channel_part(where, core, lam, scaled, relax, words, carried, last=False):
    split = isinstance(words, tuple)
    count = 1 if split else len(words)
    first = carried is None
    bias_shape = jax.ShapeDtypeStruct((SPEC, 8, 128), F32)
    if last:
        out_shape = (
            jax.ShapeDtypeStruct((32, 16, 256), F32),
            jax.ShapeDtypeStruct((32, 16, 256), BF16),
            bias_shape,
        )
    else:
        out_shape = (jax.ShapeDtypeStruct((256, D), F32), bias_shape)
    operands = [where.astype(I32), core, lam, scaled, relax, *words]
    aliases = {}
    if not first:
        if not last:
            aliases = {len(operands): 0, len(operands) + 1: 1}
        operands += list(carried)
    smem, vmem = pl.BlockSpec(memory_space=pltpu.SMEM), pl.BlockSpec(memory_space=pltpu.VMEM)
    return pl.pallas_call(
        functools.partial(channel_kernel, count, split, first, last),
        out_shape=out_shape,
        in_specs=[smem, smem] + [vmem] * (len(operands) - 2),
        out_specs=(vmem,) * len(out_shape),
        scratch_shapes=[
            pltpu.VMEM((count, D, PART), BF16),
            pltpu.VMEM((count, PART, D), BF16),
        ],
        input_output_aliases=aliases,
        compiler_params=pltpu.CompilerParams(vmem_limit_bytes=VMEM),
        cost_estimate=pl.CostEstimate(
            flops=count * 4 * 256 * PART * D,
            bytes_accessed=count * PACKED * D * 4 + 3 * 256 * D * 4,
            transcendentals=0,
        ),
        name="channel",
    )(*operands)


def token_kernel(got_ref, dense_ref, slopes_ref, icpt_ref, columns_ref, mid_ref, bias_ref):
    lane = lax.broadcasted_iota(I32, (16, 128), 1) // 32
    for u in range(NTB):
        for a in range(2):
            v = [got_ref[4 * u + p, :, a * 128 : (a + 1) * 128].astype(F32) for p in range(4)]
            for bit in (1, 2):
                low = (lane & bit) == 0
                new = list(v)
                for p in range(4):
                    if p & bit == 0:
                        q = p + bit
                        new[p] = jnp.where(low, v[p], pltpu.roll(v[q], 32 * bit, 1))
                        new[q] = jnp.where(low, pltpu.roll(v[p], 128 - 32 * bit, 1), v[q])
                v = new
            for q in range(4):
                r = 4 * a + q
                columns_ref[r * 16 : (r + 1) * 16, u * 128 : (u + 1) * 128] = v[q].astype(BF16)
    pre = jnp.dot(columns_ref[...], dense_ref[...], preferred_element_type=F32)
    pre = pre.reshape(SPEC, 16, TH)
    mid, terms = relaxed(pre, slopes_ref[0], slopes_ref[1], icpt_ref[0], icpt_ref[1])
    mid_ref[...] = mid.reshape(SPEC * 16, TH).astype(BF16)
    terms = terms[:, 0:8, :] + terms[:, 8:16, :]
    bias_ref[...] = sum(terms[:, :, k * 128 : (k + 1) * 128] for k in range(NHB))


def token_mlp(got, dense_out, slopes, icpt):
    return pl.pallas_call(
        token_kernel,
        out_shape=(
            jax.ShapeDtypeStruct((SPEC * 16, TOK), BF16),
            jax.ShapeDtypeStruct((SPEC * 16, TH), BF16),
            jax.ShapeDtypeStruct((SPEC, 8, 128), F32),
        ),
        compiler_params=pltpu.CompilerParams(vmem_limit_bytes=VMEM),
        name="token",
    )(got, dense_out, slopes, icpt)


def back_kernel(columns_ref, mid_ref, dense_ref, out_ref):
    back = jnp.dot(mid_ref[...], dense_ref[...], preferred_element_type=F32)
    out_ref[...] = (columns_ref[...].astype(F32) + back).astype(BF16)


def token_back(columns, mid, dense_in):
    return pl.pallas_call(
        back_kernel,
        out_shape=jax.ShapeDtypeStruct((SPEC * 16, TOK), BF16),
        compiler_params=pltpu.CompilerParams(vmem_limit_bytes=VMEM),
        name="back",
    )(columns, mid, dense_in)


def on_device(
    lam_out,
    q_down,
    down_scale,
    q_up,
    up_scale,
    chan_slopes,
    chan_icpt,
    tok_in_blocks,
    tok_out_blocks,
    block_cells,
    tok_slopes,
    tok_icpt,
):
    core = lax.axis_index("core")
    first = core == 0
    core_arg = core.astype(I32).reshape(1)
    tok_dev = lam_out.shape[0]
    slices = lax.axis_size("rows")

    packed = pack(core_arg, q_down, q_up, up_scale)

    ahead = [(i, (i + 1) % slices) for i in range(slices)]
    behind = [(i, (i - 1) % slices) for i in range(slices)]
    me = lax.axis_index("rows")
    near = (lax.ppermute(packed, "rows", ahead), lax.ppermute(packed, "rows", behind))

    def paired(own, other, axis):
        return jnp.where(
            first,
            jnp.concatenate([own, other], axis),
            jnp.concatenate([other, own], axis),
        )

    by_row = jnp.swapaxes(lam_out, 0, 1)
    lam = paired(by_row, lax.ppermute(by_row, "core", SWAP), 1).reshape(-1, D)
    scaled = (lam.astype(F32) * down_scale).astype(BF16)
    relax = jnp.concatenate([chan_slopes, chan_icpt], 0).reshape(4, tok_dev, slices, 2, PART)
    relax = jnp.transpose(relax, (3, 2, 0, 1, 4))
    own = jnp.where(first, relax[0], relax[1])
    other = lax.ppermute(jnp.where(first, relax[1], relax[0]), "core", SWAP)
    relax = paired(own, other, 2)

    dense_in, dense_out = dense_blocks(block_cells, tok_in_blocks, tok_out_blocks)
    slopes = jnp.transpose(tok_slopes, (0, 2, 3, 1)).reshape(2, 16, TH)
    icpt = jnp.transpose(tok_icpt, (0, 2, 3, 1)).reshape(2, 16, TH)

    common = (core_arg, lam, scaled, relax)

    def two(k, words, carried):
        return channel_part(jnp.stack([me - k, me + k]) % slices, *common, list(words), carried)

    def forward(words, carried):
        (a, b), carried = lax.optimization_barrier((words, carried))
        return (lax.ppermute(a, "rows", ahead), lax.ppermute(b, "rows", behind)), carried

    second = (lax.ppermute(near[0], "rows", ahead), lax.ppermute(near[1], "rows", behind))
    carried = channel_part(me.reshape(1), *common, [packed], None)
    third, carried = forward(second, carried)
    carried = two(1, near, carried)
    (a, b), carried = lax.optimization_barrier((third, carried))
    far = (lax.ppermute(a[0:64], "rows", ahead), lax.ppermute(b[64:PACKED], "rows", behind))
    carried = two(2, second, carried)
    carried = two(3, third, carried)
    at = ((me + slices // 2) % slices).reshape(1)
    keep, send, chan_bias = channel_part(at, *common, far, carried, last=True)
    summed = (keep + lax.ppermute(send, "core", SWAP).astype(F32)).astype(BF16)
    got = lax.all_to_all(summed, ("z", "x"), 0, 0, tiled=True)
    columns, mid, tok_bias = token_mlp(got, dense_out, slopes, icpt)
    own_bias = jnp.sum(chan_bias + tok_bias, axis=(1, 2))
    all_bias = lax.all_to_all(
        jnp.broadcast_to(own_bias[None, :], (64, SPEC)), MP, 0, 0, tiled=True
    )
    lam_in = token_back(columns, mid, dense_in)
    lam_in = jnp.transpose(lam_in.reshape(SPEC, 16, TOK), (2, 0, 1))
    return (lam_in, jnp.sum(all_bias, axis=0))


def solution(mesh):
    axes = Mesh(mesh.devices.reshape(8, 8, 4, 2), ("rows", "z", "x", "core"))
    return jax.shard_map(
        on_device,
        mesh=axes,
        in_specs=(
            P(MP, "rows", None),
            P(None, "rows"),
            P(),
            P("rows", None),
            P("rows"),
            P(None, MP, "rows", None),
            P(None, MP, "rows", None),
            P(),
            P(),
            P(),
            P(None, None, "rows", MP),
            P(None, None, "rows", MP),
        ),
        out_specs=(P(None, "rows", MP), P("rows")),
        check_vma=False,
    )
```

```python
import functools

import jax
import jax.numpy as jnp
from jax import lax
from jax.experimental import pallas as pl
from jax.experimental.pallas import tpu as pltpu
from jax.sharding import Mesh
from jax.sharding import PartitionSpec as P

D = 1024
CH = 4096
TH = 512
TOK = 1024
BLK = 128
NB = 16
SPEC = 8
NHB = 4
NTB = 8
F32 = jnp.float32
BF16 = jnp.bfloat16
I32 = jnp.int32
MP = ("z", "xh", "xl", "core")
TEAM = ("xl", "core")
SWAP = [(0, 1), (1, 0)]
VMEM = 32 * 1024 * 1024

PART = 128
SHARED = 64
ROWS_DEV = SPEC * SHARED
PACKED = 72
LAM_TILES = SPEC * (D // 128)
SCALE_ONE = float(2**38)


def pack_codes(parts):
    a, b, c, d = (p.astype(F32).astype(I32) for p in parts)
    return (a & 255) | ((b & 255) << 8) | ((c & 255) << 16) | (d << 24)


def unpack_codes(words, m):
    shifted = words << (24 - 8 * m) if m < 3 else words
    return (shifted >> 24).astype(F32).astype(BF16)


def pack_kernel(quarter_ref, down_hbm, up_hbm, scale_hbm, out_ref, down_ref, up_ref, scale_ref, sems):
    start = pl.multiple_of(quarter_ref[0] * PART, PART)
    copies = [
        pltpu.make_async_copy(down_hbm.at[:, pl.ds(start, PART)], down_ref, sems.at[0]),
        pltpu.make_async_copy(up_hbm.at[pl.ds(start, PART), :], up_ref, sems.at[1]),
        pltpu.make_async_copy(scale_hbm.at[:, pl.ds(start, PART)], scale_ref, sems.at[2]),
    ]
    for copy in copies:
        copy.start()
    out_ref[64:72, :] = jnp.zeros((8, D), I32)
    copies[0].wait()
    down = pack_codes([down_ref[m * 256 : (m + 1) * 256, :] for m in range(4)])
    for k in range(8):
        out_ref[0:32, k * PART : (k + 1) * PART] = down[k * 32 : (k + 1) * 32, :]
    copies[1].wait()
    out_ref[32:64, :] = pack_codes([up_ref[m * 32 : (m + 1) * 32, :] for m in range(4)])
    copies[2].wait()
    scale = (scale_ref[...] * SCALE_ONE).astype(I32)
    out_ref[64:72, 0:PART] = jnp.broadcast_to(scale, (8, PART))


def pack(quarter, q_down, q_up, up_scale):
    return pl.pallas_call(
        pack_kernel,
        out_shape=jax.ShapeDtypeStruct((PACKED, D), I32),
        in_specs=[pl.BlockSpec(memory_space=pltpu.SMEM)]
        + [pl.BlockSpec(memory_space=pltpu.HBM)] * 3,
        out_specs=pl.BlockSpec(memory_space=pltpu.VMEM),
        scratch_shapes=[
            pltpu.VMEM((D, PART), BF16),
            pltpu.VMEM((PART, D), BF16),
            pltpu.VMEM((1, PART), F32),
            pltpu.SemaphoreType.DMA((3,)),
        ],
        compiler_params=pltpu.CompilerParams(vmem_limit_bytes=60 * 1024 * 1024),
        name="pack",
    )(quarter, q_down, q_up, up_scale.reshape(1, -1))


def dense_kernel(cells_ref, in_ref, out_ref, dense_in_ref, dense_out_ref):
    dense_in_ref[...] = jnp.zeros_like(dense_in_ref)
    dense_out_ref[...] = jnp.zeros_like(dense_out_ref)
    for b in range(NB):
        h = pl.multiple_of(cells_ref[b] // NTB * BLK, BLK)
        u = pl.multiple_of(cells_ref[b] % NTB * BLK, BLK)
        dense_in_ref[pl.ds(h, BLK), pl.ds(u, BLK)] = in_ref[b]
        dense_out_ref[pl.ds(u, BLK), pl.ds(h, BLK)] = out_ref[b]


def dense_blocks(cells, in_blocks, out_blocks):
    return pl.pallas_call(
        dense_kernel,
        out_shape=(
            jax.ShapeDtypeStruct((TH, TOK), BF16),
            jax.ShapeDtypeStruct((TOK, TH), BF16),
        ),
        in_specs=[
            pl.BlockSpec(memory_space=pltpu.SMEM),
            pl.BlockSpec(memory_space=pltpu.VMEM),
            pl.BlockSpec(memory_space=pltpu.VMEM),
        ],
        out_specs=(
            pl.BlockSpec(memory_space=pltpu.VMEM),
            pl.BlockSpec(memory_space=pltpu.VMEM),
        ),
        compiler_params=pltpu.CompilerParams(vmem_limit_bytes=VMEM),
        name="dense",
    )(cells, in_blocks, out_blocks)


def relaxed(pre, lower, upper, icpt_low, icpt_high):
    pos = jnp.maximum(pre, 0.0)
    neg = jnp.minimum(pre, 0.0)
    mid = pos * lower.astype(F32) + neg * upper.astype(F32)
    return mid, pos * icpt_low.astype(F32) + neg * icpt_high.astype(F32)


def share_kernel(quarter_ref, lam_ref, slopes_ref, icpt_ref, *out_refs):
    for r in range(SPEC):
        for k in range(D // 128):
            tile = lam_ref[r, :, k * 128 : (k + 1) * 128]
            for out_ref in out_refs:
                out_ref[r * (D // 128) + k] = tile
    for k, out_ref in enumerate(out_refs):
        for y in range(CH // TH):
            start = pl.multiple_of(y * TH + (quarter_ref[0] ^ k) * PART, PART)
            for kind in range(2):
                out_ref[LAM_TILES + y * 4 + kind] = slopes_ref[kind, :, pl.ds(start, PART)]
                out_ref[LAM_TILES + y * 4 + 2 + kind] = icpt_ref[kind, :, pl.ds(start, PART)]


def share(quarter, by_row, slopes, icpt):
    tiles = LAM_TILES + 4 * (CH // TH)
    return pl.pallas_call(
        share_kernel,
        out_shape=(jax.ShapeDtypeStruct((tiles, 16, 128), BF16),) * 4,
        in_specs=[pl.BlockSpec(memory_space=pltpu.SMEM)]
        + [pl.BlockSpec(memory_space=pltpu.VMEM)] * 3,
        compiler_params=pltpu.CompilerParams(vmem_limit_bytes=60 * 1024 * 1024),
        name="share",
    )(quarter, by_row, slopes, icpt)


def channel_kernel(count, first, last, *refs):
    where_ref, place_ref = refs[:2]
    refs = refs[2:]
    words, refs = refs[:count], refs[count:]
    if first:
        down_scale_ref, *team, acc_ref, bias_ref, scaled_ref, bounds_ref, down, up = refs
        for j, got_ref in enumerate(team):
            start = (place_ref[0] ^ j) * 16
            for r in range(SPEC):
                rows = pl.ds(pl.multiple_of(r * SHARED + start, 16), 16)
                for k in range(D // 128):
                    cut = slice(k * 128, (k + 1) * 128)
                    lam = got_ref[r * (D // 128) + k].astype(F32)
                    scaled_ref[rows, cut] = (lam * down_scale_ref[:, cut]).astype(BF16)
                    acc_ref[rows, cut] = 0.25 * lam
            rows = pl.ds(pl.multiple_of(start, 16), 16)
            for y in range(CH // TH):
                for kind in range(4):
                    bounds_ref[y, kind, rows, :] = got_ref[LAM_TILES + y * 4 + kind]
        acc_in, bias_in = acc_ref, None
    else:
        scaled_ref, bounds_ref, acc_in, bias_in, *outs, down, up = refs
    scales, bounds = [], []
    for k, words_ref in enumerate(words):
        for m in range(4):
            codes = unpack_codes(words_ref[0:32, :], m)
            for q in range(8):
                rows = m * 256 + q * 32
                cut = slice(q * PART, (q + 1) * PART)
                down[rows : rows + 32, k * PART : (k + 1) * PART] = codes[:, cut]
            rows = k * PART + m * 32
            up[rows : rows + 32, :] = unpack_codes(words_ref[32:64, :], m)
        scales.append(words_ref[64:65, 0:PART].astype(F32) * (1.0 / SCALE_ONE))
        bounds.append(bounds_ref.at[where_ref[k]])
    scale = jnp.concatenate(scales, axis=1)
    bounds = [jnp.concatenate([b[kind] for b in bounds], axis=1) for kind in range(4)]
    pre = jnp.dot(scaled_ref[...], down[...], preferred_element_type=F32)
    pre = pre.reshape(SPEC, SHARED, count * PART)
    mid, terms = relaxed(pre, *bounds)
    terms = jnp.sum(terms.reshape(SPEC, SHARED // 8, 8, count * PART), axis=1)
    bias = sum(terms[:, :, k * PART : (k + 1) * PART] for k in range(count))
    weighted = (mid.reshape(ROWS_DEV, count * PART) * scale).astype(BF16)
    part = jnp.dot(weighted, up[...], preferred_element_type=F32)
    total = acc_in[...] + part
    if not first:
        bias = bias + bias_in[...]
    if last:
        keep_ref, send_ref, bias_ref = outs
        own = place_ref[0] % 2 == 0
        turned = total.T.reshape(32, 2, 16, ROWS_DEV)
        keep_ref[...] = jnp.where(own, turned[:, 0], turned[:, 1])
        send_ref[...] = jnp.where(own, turned[:, 1], turned[:, 0]).astype(BF16)
    else:
        if not first:
            acc_ref, bias_ref = outs
        acc_ref[...] = total
    bias_ref[...] = bias


def channel_part(where, place, words, rest, first=False, last=False):
    count = len(words)
    acc_shape = jax.ShapeDtypeStruct((ROWS_DEV, D), F32)
    bias_shape = jax.ShapeDtypeStruct((SPEC, 8, 128), F32)
    operands = [where.astype(I32), place, *words, *rest]
    aliases = {}
    if first:
        scaled_shape = jax.ShapeDtypeStruct((ROWS_DEV, D), BF16)
        bounds_shape = jax.ShapeDtypeStruct((CH // TH, 4, SHARED, PART), BF16)
        out_shape = (acc_shape, bias_shape, scaled_shape, bounds_shape)
    elif last:
        out_shape = (
            jax.ShapeDtypeStruct((32, 16, ROWS_DEV), F32),
            jax.ShapeDtypeStruct((32, 16, ROWS_DEV), BF16),
            bias_shape,
        )
    else:
        out_shape = (acc_shape, bias_shape)
        aliases = {len(operands) - 2: 0, len(operands) - 1: 1}
    smem, vmem = pl.BlockSpec(memory_space=pltpu.SMEM), pl.BlockSpec(memory_space=pltpu.VMEM)
    return pl.pallas_call(
        functools.partial(channel_kernel, count, first, last),
        out_shape=out_shape,
        in_specs=[smem, smem] + [vmem] * (len(operands) - 2),
        out_specs=(vmem,) * len(out_shape),
        scratch_shapes=[
            pltpu.VMEM((D, count * PART), BF16),
            pltpu.VMEM((count * PART, D), BF16),
        ],
        input_output_aliases=aliases,
        compiler_params=pltpu.CompilerParams(vmem_limit_bytes=VMEM),
        cost_estimate=pl.CostEstimate(
            flops=count * 4 * ROWS_DEV * PART * D,
            bytes_accessed=count * PACKED * D * 4 + 3 * ROWS_DEV * D * 4,
            transcendentals=0,
        ),
        name="channel",
    )(*operands)


def token_kernel(got_ref, dense_ref, slopes_ref, icpt_ref, columns_ref, mid_ref, bias_ref):
    low = lax.broadcasted_iota(I32, (16, 128), 1) < SHARED
    for u in range(NTB):
        for a in range(SPEC // 2):
            cut = slice(a * 128, (a + 1) * 128)
            v = [
                got_ref[s, :, cut].astype(F32) + got_ref[s + 1, :, cut].astype(F32)
                for s in (4 * u, 4 * u + 2)
            ]
            even = jnp.where(low, v[0], pltpu.roll(v[1], SHARED, 1))
            odd = jnp.where(low, pltpu.roll(v[0], SHARED, 1), v[1])
            for r, value in ((2 * a, even), (2 * a + 1, odd)):
                columns_ref[r * 16 : (r + 1) * 16, u * 128 : (u + 1) * 128] = value.astype(BF16)
    pre = jnp.dot(columns_ref[...], dense_ref[...], preferred_element_type=F32)
    pre = pre.reshape(SPEC, 16, TH)
    mid, terms = relaxed(pre, slopes_ref[0], slopes_ref[1], icpt_ref[0], icpt_ref[1])
    mid_ref[...] = mid.reshape(SPEC * 16, TH).astype(BF16)
    terms = terms[:, 0:8, :] + terms[:, 8:16, :]
    bias_ref[...] = sum(terms[:, :, k * 128 : (k + 1) * 128] for k in range(NHB))


def token_mlp(got, dense_out, slopes, icpt):
    return pl.pallas_call(
        token_kernel,
        out_shape=(
            jax.ShapeDtypeStruct((SPEC * 16, TOK), BF16),
            jax.ShapeDtypeStruct((SPEC * 16, TH), BF16),
            jax.ShapeDtypeStruct((SPEC, 8, 128), F32),
        ),
        compiler_params=pltpu.CompilerParams(vmem_limit_bytes=VMEM),
        name="token",
    )(got, dense_out, slopes, icpt)


def back_kernel(columns_ref, mid_ref, dense_ref, out_ref):
    back = jnp.dot(mid_ref[...], dense_ref[...], preferred_element_type=F32)
    out_ref[...] = (columns_ref[...].astype(F32) + back).astype(BF16)


def token_back(columns, mid, dense_in):
    return pl.pallas_call(
        back_kernel,
        out_shape=jax.ShapeDtypeStruct((SPEC * 16, TOK), BF16),
        compiler_params=pltpu.CompilerParams(vmem_limit_bytes=VMEM),
        name="back",
    )(columns, mid, dense_in)


def on_device(
    lam_out,
    q_down,
    down_scale,
    q_up,
    up_scale,
    chan_slopes,
    chan_icpt,
    tok_in_blocks,
    tok_out_blocks,
    block_cells,
    tok_slopes,
    tok_icpt,
):
    quarter = lax.axis_index(TEAM).astype(I32).reshape(1)
    tok_dev = lam_out.shape[0]
    slices = lax.axis_size("rows")
    ahead = [(i, (i + 1) % slices) for i in range(slices)]
    behind = [(i, (i - 1) % slices) for i in range(slices)]

    own = pack(quarter, q_down, q_up, up_scale)
    near = (lax.ppermute(own, "rows", ahead), lax.ppermute(own, "rows", behind))
    own_part, *parts = share(
        quarter,
        jnp.swapaxes(lam_out, 0, 1),
        chan_slopes.reshape(2, tok_dev, CH),
        chan_icpt.reshape(2, tok_dev, CH),
    )
    onward, parts = lax.optimization_barrier((near[1], parts))
    team = [own_part] + [
        lax.ppermute(part, TEAM, [(i, i ^ k) for i in range(4)]) for k, part in enumerate(parts, 1)
    ]
    second = (lax.ppermute(near[0], "rows", ahead), lax.ppermute(onward, "rows", behind))
    onward, team[2] = lax.optimization_barrier((second[0], team[2]))
    back, team[3] = lax.optimization_barrier((second[1], team[3]))
    third = (lax.ppermute(onward, "rows", ahead), lax.ppermute(back, "rows", behind))
    far = lax.ppermute(third[0], "rows", ahead)

    dense_in, dense_out = dense_blocks(block_cells, tok_in_blocks, tok_out_blocks)
    slopes = jnp.transpose(tok_slopes, (0, 2, 3, 1)).reshape(2, 16, TH)
    icpt = jnp.transpose(tok_icpt, (0, 2, 3, 1)).reshape(2, 16, TH)

    me = lax.axis_index("rows")
    acc, chan_bias, *given = channel_part(
        me.reshape(1), quarter, [own], [down_scale.reshape(1, D), *team], first=True
    )
    for k, words in enumerate((near, second, third), 1):
        at = jnp.stack([me - k, me + k]) % slices
        acc, chan_bias = channel_part(at, quarter, words, [*given, acc, chan_bias])
    at = ((me + slices // 2) % slices).reshape(1)
    keep, send, chan_bias = channel_part(
        at, quarter, [far], [*given, acc, chan_bias], last=True
    )
    summed = (keep + lax.ppermute(send, "core", SWAP).astype(F32)).astype(BF16)
    got = lax.all_to_all(summed, ("z", "xh", "xl"), 0, 0, tiled=True)
    columns, mid, tok_bias = token_mlp(got, dense_out, slopes, icpt)
    own_bias = jnp.sum(chan_bias + tok_bias, axis=(1, 2))
    all_bias = lax.all_to_all(
        jnp.broadcast_to(own_bias[None, :], (64, SPEC)), MP, 0, 0, tiled=True
    )
    lam_in = token_back(columns, mid, dense_in)
    lam_in = jnp.transpose(lam_in.reshape(SPEC, 16, TOK), (2, 0, 1))
    return (lam_in, jnp.sum(all_bias, axis=0))


def solution(mesh):
    axes = Mesh(mesh.devices.reshape(8, 8, 2, 2, 2), ("rows",) + MP)
    return jax.shard_map(
        on_device,
        mesh=axes,
        in_specs=(
            P(MP, "rows", None),
            P(None, "rows"),
            P(),
            P("rows", None),
            P("rows"),
            P(None, MP, "rows", None),
            P(None, MP, "rows", None),
            P(),
            P(),
            P(),
            P(None, None, "rows", MP),
            P(None, None, "rows", MP),
        ),
        out_specs=(P(None, "rows", MP), P("rows")),
        check_vma=False,
    )
```

```python
import functools

import jax
import jax.numpy as jnp
from jax import lax
from jax.experimental import pallas as pl
from jax.experimental.pallas import tpu as pltpu
from jax.sharding import Mesh
from jax.sharding import PartitionSpec as P

D = 1024
CH = 4096
TH = 512
TOK = 1024
BLK = 128
NB = 16
SPEC = 8
NHB = 4
NTB = 8
F32 = jnp.float32
BF16 = jnp.bfloat16
I32 = jnp.int32
MP = ("z", "xh", "xl", "core")
TEAM = ("xl", "core")
SWAP = [(0, 1), (1, 0)]
VMEM = 32 * 1024 * 1024

PART = 256
STEPS = 4
SHARED = 64
ROWS_DEV = SPEC * SHARED
PACKED = 136
LAM_TILES = SPEC * (D // 128)
SCALE_ONE = float(2**38)


def pack_codes(parts):
    a, b, c, d = (p.astype(F32).astype(I32) for p in parts)
    return (a & 255) | ((b & 255) << 8) | ((c & 255) << 16) | (d << 24)


def unpack_codes(words, m):
    shifted = words << (24 - 8 * m) if m < 3 else words
    return (shifted >> 24).astype(F32).astype(BF16)


def pack_kernel(half_ref, down_hbm, up_hbm, scale_hbm, out_ref, down_ref, up_ref, scale_ref, sems):
    start = pl.multiple_of(half_ref[0] * PART, PART)
    copies = [
        pltpu.make_async_copy(down_hbm.at[:, pl.ds(start, PART)], down_ref, sems.at[0]),
        pltpu.make_async_copy(up_hbm.at[pl.ds(start, PART), :], up_ref, sems.at[1]),
        pltpu.make_async_copy(scale_hbm.at[:, pl.ds(start, PART)], scale_ref, sems.at[2]),
    ]
    for copy in copies:
        copy.start()
    out_ref[128:136, :] = jnp.zeros((8, D), I32)
    copies[0].wait()
    down = pack_codes([down_ref[m * 256 : (m + 1) * 256, :] for m in range(4)])
    for k in range(4):
        out_ref[0:64, k * PART : (k + 1) * PART] = down[k * 64 : (k + 1) * 64, :]
    copies[1].wait()
    out_ref[64:128, :] = pack_codes([up_ref[m * 64 : (m + 1) * 64, :] for m in range(4)])
    copies[2].wait()
    scale = (scale_ref[...] * SCALE_ONE).astype(I32)
    out_ref[128:136, 0:PART] = jnp.broadcast_to(scale, (8, PART))


def pack(half, q_down, q_up, up_scale):
    return pl.pallas_call(
        pack_kernel,
        out_shape=jax.ShapeDtypeStruct((PACKED, D), I32),
        in_specs=[pl.BlockSpec(memory_space=pltpu.SMEM)]
        + [pl.BlockSpec(memory_space=pltpu.HBM)] * 3,
        out_specs=pl.BlockSpec(memory_space=pltpu.VMEM),
        scratch_shapes=[
            pltpu.VMEM((D, PART), BF16),
            pltpu.VMEM((PART, D), BF16),
            pltpu.VMEM((1, PART), F32),
            pltpu.SemaphoreType.DMA((3,)),
        ],
        compiler_params=pltpu.CompilerParams(vmem_limit_bytes=60 * 1024 * 1024),
        name="pack",
    )(half, q_down, q_up, up_scale.reshape(1, -1))


def dense_kernel(cells_ref, in_ref, out_ref, dense_in_ref, dense_out_ref):
    dense_in_ref[...] = jnp.zeros_like(dense_in_ref)
    dense_out_ref[...] = jnp.zeros_like(dense_out_ref)
    for b in range(NB):
        h = pl.multiple_of(cells_ref[b] // NTB * BLK, BLK)
        u = pl.multiple_of(cells_ref[b] % NTB * BLK, BLK)
        dense_in_ref[pl.ds(h, BLK), pl.ds(u, BLK)] = in_ref[b]
        dense_out_ref[pl.ds(u, BLK), pl.ds(h, BLK)] = out_ref[b]


def dense_blocks(cells, in_blocks, out_blocks):
    return pl.pallas_call(
        dense_kernel,
        out_shape=(
            jax.ShapeDtypeStruct((TH, TOK), BF16),
            jax.ShapeDtypeStruct((TOK, TH), BF16),
        ),
        in_specs=[
            pl.BlockSpec(memory_space=pltpu.SMEM),
            pl.BlockSpec(memory_space=pltpu.VMEM),
            pl.BlockSpec(memory_space=pltpu.VMEM),
        ],
        out_specs=(
            pl.BlockSpec(memory_space=pltpu.VMEM),
            pl.BlockSpec(memory_space=pltpu.VMEM),
        ),
        compiler_params=pltpu.CompilerParams(vmem_limit_bytes=VMEM),
        name="dense",
    )(cells, in_blocks, out_blocks)


def relaxed(pre, lower, upper, icpt_low, icpt_high):
    pos = jnp.maximum(pre, 0.0)
    neg = jnp.minimum(pre, 0.0)
    mid = pos * lower.astype(F32) + neg * upper.astype(F32)
    return mid, pos * icpt_low.astype(F32) + neg * icpt_high.astype(F32)


def share_kernel(place_ref, lam_ref, slopes_ref, icpt_ref, *out_refs):
    for r in range(SPEC):
        for k in range(D // 128):
            tile = lam_ref[r, :, k * 128 : (k + 1) * 128]
            for out_ref in out_refs:
                out_ref[r * (D // 128) + k] = tile
    row = place_ref[1]
    for k, out_ref in enumerate(out_refs):
        to = place_ref[0] ^ k
        sign = 2 * (to & 1) - 1
        for j in range(STEPS):
            if j < STEPS - 1:
                owner = row + sign * (j + 1)
            else:
                owner = row - STEPS * (1 - (to & 1))
            start = pl.multiple_of((owner & 7) * TH + (to >> 1) * PART, PART)
            for kind in range(4):
                ref = slopes_ref if kind < 2 else icpt_ref
                values = ref[kind % 2, :, pl.ds(start, PART)]
                for h in range(2):
                    out_ref[LAM_TILES + (j * 4 + kind) * 2 + h] = values[:, h * 128 : (h + 1) * 128]


def share(place, by_row, slopes, icpt):
    tiles = LAM_TILES + 4 * STEPS * 2
    return pl.pallas_call(
        share_kernel,
        out_shape=(jax.ShapeDtypeStruct((tiles, 16, 128), BF16),) * 4,
        in_specs=[pl.BlockSpec(memory_space=pltpu.SMEM)]
        + [pl.BlockSpec(memory_space=pltpu.VMEM)] * 3,
        compiler_params=pltpu.CompilerParams(vmem_limit_bytes=60 * 1024 * 1024),
        name="share",
    )(place, by_row, slopes, icpt)


def channel_kernel(step, *refs):
    first, last = step == 0, step == STEPS - 1
    place_ref, words_ref, *refs = refs
    if first:
        down_scale_ref, *team, acc_ref, bias_ref, scaled_ref, bounds_ref, down, up = refs
        for k, got_ref in enumerate(team):
            start = (place_ref[0] ^ k) * 16
            for r in range(SPEC):
                rows = pl.ds(pl.multiple_of(r * SHARED + start, 16), 16)
                for c in range(D // 128):
                    cut = slice(c * 128, (c + 1) * 128)
                    lam = got_ref[r * (D // 128) + c].astype(F32)
                    scaled_ref[rows, cut] = (lam * down_scale_ref[:, cut]).astype(BF16)
                    acc_ref[rows, cut] = 0.25 * lam
            rows = pl.ds(pl.multiple_of(start, 16), 16)
            for i in range(STEPS * 4):
                for h in range(2):
                    tile = got_ref[LAM_TILES + i * 2 + h]
                    bounds_ref[i // 4, i % 4, rows, h * 128 : (h + 1) * 128] = tile
        acc_in, bias_in = acc_ref, None
    else:
        if last:
            own_ref, *refs = refs
        scaled_ref, bounds_ref, acc_in, bias_in, *outs, down, up = refs
    words = words_ref[...]
    if last:
        words = jnp.where(place_ref[0] % 2 == 0, words, own_ref[...])
    for m in range(4):
        codes = unpack_codes(words[0:64], m)
        for q in range(4):
            rows = m * 256 + q * 64
            down[rows : rows + 64, :] = codes[:, q * PART : (q + 1) * PART]
        up[m * 64 : (m + 1) * 64, :] = unpack_codes(words[64:128], m)
    scale = words[128:129, 0:PART].astype(F32) * (1.0 / SCALE_ONE)
    pre = jnp.dot(scaled_ref[...], down[...], preferred_element_type=F32)
    pre = pre.reshape(SPEC, SHARED, PART)
    mid, terms = relaxed(pre, *(bounds_ref[step, kind] for kind in range(4)))
    terms = jnp.sum(terms.reshape(SPEC, SHARED // 8, 8, PART), axis=1)
    bias = terms[:, :, 0:128] + terms[:, :, 128:256]
    weighted = (mid.reshape(ROWS_DEV, PART) * scale).astype(BF16)
    part = jnp.dot(weighted, up[...], preferred_element_type=F32)
    total = acc_in[...] + part
    if not first:
        bias = bias + bias_in[...]
    if last:
        keep_ref, send_ref, bias_ref = outs
        own = place_ref[0] % 2 == 0
        turned = total.T.reshape(32, 2, 16, ROWS_DEV)
        keep_ref[...] = jnp.where(own, turned[:, 0], turned[:, 1])
        send_ref[...] = jnp.where(own, turned[:, 1], turned[:, 0]).astype(BF16)
    else:
        if not first:
            acc_ref, bias_ref = outs
        acc_ref[...] = total
    bias_ref[...] = bias


def channel_part(step, place, *rest):
    acc_shape = jax.ShapeDtypeStruct((ROWS_DEV, D), F32)
    bias_shape = jax.ShapeDtypeStruct((SPEC, 8, 128), F32)
    operands = [place, *rest]
    aliases = {}
    if step == 0:
        scaled_shape = jax.ShapeDtypeStruct((ROWS_DEV, D), BF16)
        bounds_shape = jax.ShapeDtypeStruct((STEPS, 4, SHARED, PART), BF16)
        out_shape = (acc_shape, bias_shape, scaled_shape, bounds_shape)
    elif step == STEPS - 1:
        out_shape = (
            jax.ShapeDtypeStruct((32, 16, ROWS_DEV), F32),
            jax.ShapeDtypeStruct((32, 16, ROWS_DEV), BF16),
            bias_shape,
        )
    else:
        out_shape = (acc_shape, bias_shape)
        aliases = {len(operands) - 2: 0, len(operands) - 1: 1}
    smem, vmem = pl.BlockSpec(memory_space=pltpu.SMEM), pl.BlockSpec(memory_space=pltpu.VMEM)
    return pl.pallas_call(
        functools.partial(channel_kernel, step),
        out_shape=out_shape,
        in_specs=[smem] + [vmem] * (len(operands) - 1),
        out_specs=(vmem,) * len(out_shape),
        scratch_shapes=[pltpu.VMEM((D, PART), BF16), pltpu.VMEM((PART, D), BF16)],
        input_output_aliases=aliases,
        compiler_params=pltpu.CompilerParams(vmem_limit_bytes=VMEM),
        cost_estimate=pl.CostEstimate(
            flops=4 * ROWS_DEV * PART * D,
            bytes_accessed=PACKED * D * 4 + 3 * ROWS_DEV * D * 4,
            transcendentals=0,
        ),
        name="channel",
    )(*operands)


def token_kernel(got_ref, dense_ref, slopes_ref, icpt_ref, columns_ref, mid_ref, bias_ref):
    low = lax.broadcasted_iota(I32, (16, 128), 1) < SHARED
    for u in range(NTB):
        for a in range(SPEC // 2):
            cut = slice(a * 128, (a + 1) * 128)
            v = [
                got_ref[s, :, cut].astype(F32) + got_ref[s + 1, :, cut].astype(F32)
                for s in (4 * u, 4 * u + 2)
            ]
            even = jnp.where(low, v[0], pltpu.roll(v[1], SHARED, 1))
            odd = jnp.where(low, pltpu.roll(v[0], SHARED, 1), v[1])
            for r, value in ((2 * a, even), (2 * a + 1, odd)):
                columns_ref[r * 16 : (r + 1) * 16, u * 128 : (u + 1) * 128] = value.astype(BF16)
    pre = jnp.dot(columns_ref[...], dense_ref[...], preferred_element_type=F32)
    pre = pre.reshape(SPEC, 16, TH)
    mid, terms = relaxed(pre, slopes_ref[0], slopes_ref[1], icpt_ref[0], icpt_ref[1])
    mid_ref[...] = mid.reshape(SPEC * 16, TH).astype(BF16)
    terms = terms[:, 0:8, :] + terms[:, 8:16, :]
    bias_ref[...] = sum(terms[:, :, k * 128 : (k + 1) * 128] for k in range(NHB))


def token_mlp(got, dense_out, slopes, icpt):
    return pl.pallas_call(
        token_kernel,
        out_shape=(
            jax.ShapeDtypeStruct((SPEC * 16, TOK), BF16),
            jax.ShapeDtypeStruct((SPEC * 16, TH), BF16),
            jax.ShapeDtypeStruct((SPEC, 8, 128), F32),
        ),
        compiler_params=pltpu.CompilerParams(vmem_limit_bytes=VMEM),
        name="token",
    )(got, dense_out, slopes, icpt)


def back_kernel(columns_ref, mid_ref, dense_ref, out_ref):
    back = jnp.dot(mid_ref[...], dense_ref[...], preferred_element_type=F32)
    out_ref[...] = (columns_ref[...].astype(F32) + back).astype(BF16)


def token_back(columns, mid, dense_in):
    return pl.pallas_call(
        back_kernel,
        out_shape=jax.ShapeDtypeStruct((SPEC * 16, TOK), BF16),
        compiler_params=pltpu.CompilerParams(vmem_limit_bytes=VMEM),
        name="back",
    )(columns, mid, dense_in)


def on_device(
    lam_out,
    q_down,
    down_scale,
    q_up,
    up_scale,
    chan_slopes,
    chan_icpt,
    tok_in_blocks,
    tok_out_blocks,
    block_cells,
    tok_slopes,
    tok_icpt,
):
    quarter, row = lax.axis_index(TEAM).astype(I32), lax.axis_index("rows").astype(I32)
    place = jnp.stack([quarter, row])
    half = (quarter >> 1).reshape(1)
    tok_dev = lam_out.shape[0]
    slices = lax.axis_size("rows")
    ahead = [(i * 2, (i + 1) % slices * 2) for i in range(slices)]
    behind = [(i * 2 + 1, (i - 1) % slices * 2 + 1) for i in range(slices)]

    def forward(words, pairs):
        return lax.ppermute(words, ("rows", "core"), pairs)

    own = pack(half, q_down, q_up, up_scale)
    first = forward(own, ahead + behind)
    own_part, *parts = share(
        place,
        jnp.swapaxes(lam_out, 0, 1),
        chan_slopes.reshape(2, tok_dev, CH),
        chan_icpt.reshape(2, tok_dev, CH),
    )
    words, parts = lax.optimization_barrier((first, parts))
    second = forward(words, ahead + behind)
    team = [own_part] + [
        lax.ppermute(part, TEAM, [(i, i ^ k) for i in range(4)]) for k, part in enumerate(parts, 1)
    ]
    words, team[2] = lax.optimization_barrier((second, team[2]))
    third = forward(words, ahead + behind)
    words, team[1], team[3] = lax.optimization_barrier((third, team[1], team[3]))
    far = forward(words, ahead)

    dense_in, dense_out = dense_blocks(block_cells, tok_in_blocks, tok_out_blocks)
    slopes = jnp.transpose(tok_slopes, (0, 2, 3, 1)).reshape(2, 16, TH)
    icpt = jnp.transpose(tok_icpt, (0, 2, 3, 1)).reshape(2, 16, TH)

    acc, chan_bias, *given = channel_part(0, place, first, down_scale.reshape(1, D), *team)
    acc, chan_bias = channel_part(1, place, second, *given, acc, chan_bias)
    acc, chan_bias = channel_part(2, place, third, *given, acc, chan_bias)
    keep, send, chan_bias = channel_part(3, place, far, own, *given, acc, chan_bias)
    summed = (keep + lax.ppermute(send, "core", SWAP).astype(F32)).astype(BF16)
    got = lax.all_to_all(summed, ("z", "xh", "xl"), 0, 0, tiled=True)
    columns, mid, tok_bias = token_mlp(got, dense_out, slopes, icpt)
    own_bias = jnp.sum(chan_bias + tok_bias, axis=(1, 2))
    all_bias = lax.all_to_all(
        jnp.broadcast_to(own_bias[None, :], (64, SPEC)), MP, 0, 0, tiled=True
    )
    lam_in = token_back(columns, mid, dense_in)
    lam_in = jnp.transpose(lam_in.reshape(SPEC, 16, TOK), (2, 0, 1))
    return (lam_in, jnp.sum(all_bias, axis=0))


def solution(mesh):
    axes = Mesh(mesh.devices.reshape(8, 8, 2, 2, 2), ("rows",) + MP)
    return jax.shard_map(
        on_device,
        mesh=axes,
        in_specs=(
            P(MP, "rows", None),
            P(None, "rows"),
            P(),
            P("rows", None),
            P("rows"),
            P(None, MP, "rows", None),
            P(None, MP, "rows", None),
            P(),
            P(),
            P(),
            P(None, None, "rows", MP),
            P(None, None, "rows", MP),
        ),
        out_specs=(P(None, "rows", MP), P("rows")),
        check_vma=False,
    )
```

```python
import functools

import jax
import jax.numpy as jnp
from jax import lax
from jax.experimental import pallas as pl
from jax.experimental.pallas import tpu as pltpu
from jax.sharding import Mesh
from jax.sharding import PartitionSpec as P

D = 1024
CH = 4096
TH = 512
TOK = 1024
BLK = 128
NB = 16
SPEC = 8
NHB = 4
NTB = 8
F32 = jnp.float32
BF16 = jnp.bfloat16
I32 = jnp.int32
MP = ("z", "xh", "xl", "core")
TEAM = ("xl", "core")
SWAP = [(0, 1), (1, 0)]
VMEM = 32 * 1024 * 1024

PART = 256
STEPS = 4
SHARED = 64
ROWS_DEV = SPEC * SHARED
PACKED = 136
LAM_TILES = SPEC * (D // 128)
SCALE_ONE = float(2**38)


def pack_codes(parts):
    a, b, c, d = (p.astype(F32).astype(I32) for p in parts)
    return (a & 255) | ((b & 255) << 8) | ((c & 255) << 16) | (d << 24)


def unpack_codes(words, m):
    shifted = words << (24 - 8 * m) if m < 3 else words
    return (shifted >> 24).astype(F32).astype(BF16)


def pack_kernel(half_ref, down_hbm, up_hbm, scale_hbm, out_ref, down_ref, up_ref, scale_ref, sems):
    start = pl.multiple_of(half_ref[0] * PART, PART)
    copies = [
        pltpu.make_async_copy(down_hbm.at[:, pl.ds(start, PART)], down_ref, sems.at[0]),
        pltpu.make_async_copy(up_hbm.at[pl.ds(start, PART), :], up_ref, sems.at[1]),
        pltpu.make_async_copy(scale_hbm.at[:, pl.ds(start, PART)], scale_ref, sems.at[2]),
    ]
    for copy in copies:
        copy.start()
    out_ref[128:136, :] = jnp.zeros((8, D), I32)
    copies[0].wait()
    down = pack_codes([down_ref[m * 256 : (m + 1) * 256, :] for m in range(4)])
    for k in range(4):
        out_ref[0:64, k * PART : (k + 1) * PART] = down[k * 64 : (k + 1) * 64, :]
    copies[1].wait()
    out_ref[64:128, :] = pack_codes([up_ref[m * 64 : (m + 1) * 64, :] for m in range(4)])
    copies[2].wait()
    scale = (scale_ref[...] * SCALE_ONE).astype(I32)
    out_ref[128:136, 0:PART] = jnp.broadcast_to(scale, (8, PART))


def pack(half, q_down, q_up, up_scale):
    return pl.pallas_call(
        pack_kernel,
        out_shape=jax.ShapeDtypeStruct((PACKED, D), I32),
        in_specs=[pl.BlockSpec(memory_space=pltpu.SMEM)]
        + [pl.BlockSpec(memory_space=pltpu.HBM)] * 3,
        out_specs=pl.BlockSpec(memory_space=pltpu.VMEM),
        scratch_shapes=[
            pltpu.VMEM((D, PART), BF16),
            pltpu.VMEM((PART, D), BF16),
            pltpu.VMEM((1, PART), F32),
            pltpu.SemaphoreType.DMA((3,)),
        ],
        compiler_params=pltpu.CompilerParams(vmem_limit_bytes=60 * 1024 * 1024),
        name="pack",
    )(half, q_down, q_up, up_scale.reshape(1, -1))


def dense_kernel(cells_ref, in_ref, out_ref, dense_in_ref, dense_out_ref):
    dense_in_ref[...] = jnp.zeros_like(dense_in_ref)
    dense_out_ref[...] = jnp.zeros_like(dense_out_ref)
    for b in range(NB):
        h = pl.multiple_of(cells_ref[b] // NTB * BLK, BLK)
        u = pl.multiple_of(cells_ref[b] % NTB * BLK, BLK)
        dense_in_ref[pl.ds(h, BLK), pl.ds(u, BLK)] = in_ref[b]
        dense_out_ref[pl.ds(u, BLK), pl.ds(h, BLK)] = out_ref[b]


def dense_blocks(cells, in_blocks, out_blocks):
    return pl.pallas_call(
        dense_kernel,
        out_shape=(
            jax.ShapeDtypeStruct((TH, TOK), BF16),
            jax.ShapeDtypeStruct((TOK, TH), BF16),
        ),
        in_specs=[
            pl.BlockSpec(memory_space=pltpu.SMEM),
            pl.BlockSpec(memory_space=pltpu.VMEM),
            pl.BlockSpec(memory_space=pltpu.VMEM),
        ],
        out_specs=(
            pl.BlockSpec(memory_space=pltpu.VMEM),
            pl.BlockSpec(memory_space=pltpu.VMEM),
        ),
        compiler_params=pltpu.CompilerParams(vmem_limit_bytes=VMEM),
        name="dense",
    )(cells, in_blocks, out_blocks)


def relaxed(pre, lower, upper, icpt_low, icpt_high):
    pos = jnp.maximum(pre, 0.0)
    neg = jnp.minimum(pre, 0.0)
    mid = pos * lower.astype(F32) + neg * upper.astype(F32)
    return mid, pos * icpt_low.astype(F32) + neg * icpt_high.astype(F32)


def share_kernel(row_ref, lam_ref, slopes_ref, icpt_ref, out_ref):
    for r in range(SPEC):
        for k in range(D // 128):
            tile = lam_ref[r, :, k * 128 : (k + 1) * 128]
            for to in range(4):
                out_ref[to, r * (D // 128) + k] = tile
    row = row_ref[0]
    for to in range(4):
        half, core = to // 2, to % 2
        for j in range(STEPS):
            owner = row + (j + 1) % STEPS if core else row - (j + 1)
            start = pl.multiple_of((owner & 7) * TH + half * PART, PART)
            for kind in range(4):
                ref = slopes_ref if kind < 2 else icpt_ref
                values = ref[kind % 2, :, pl.ds(start, PART)]
                for h in range(2):
                    tile = LAM_TILES + (j * 4 + kind) * 2 + h
                    out_ref[to, tile] = values[:, h * 128 : (h + 1) * 128]


def share(row, by_row, slopes, icpt):
    tiles = LAM_TILES + 4 * STEPS * 2
    return pl.pallas_call(
        share_kernel,
        out_shape=jax.ShapeDtypeStruct((4, tiles, 16, 128), BF16),
        in_specs=[pl.BlockSpec(memory_space=pltpu.SMEM)]
        + [pl.BlockSpec(memory_space=pltpu.VMEM)] * 3,
        compiler_params=pltpu.CompilerParams(vmem_limit_bytes=60 * 1024 * 1024),
        name="share",
    )(row, by_row, slopes, icpt)


def channel_kernel(step, *refs):
    first, last = step == 0, step == STEPS - 1
    core_ref, words_ref, *refs = refs
    if first:
        down_scale_ref, got_ref, acc_ref, bias_ref, scaled_ref, bounds_ref, down, up = refs
        for q in range(4):
            for r in range(SPEC):
                rows = slice(r * SHARED + q * 16, r * SHARED + (q + 1) * 16)
                for c in range(D // 128):
                    cut = slice(c * 128, (c + 1) * 128)
                    lam = got_ref[q, r * (D // 128) + c].astype(F32)
                    scaled_ref[rows, cut] = (lam * down_scale_ref[:, cut]).astype(BF16)
                    acc_ref[rows, cut] = 0.25 * lam
            for i in range(STEPS * 4):
                for h in range(2):
                    tile = got_ref[q, LAM_TILES + i * 2 + h]
                    bounds_ref[i // 4, i % 4, q * 16 : (q + 1) * 16, h * 128 : (h + 1) * 128] = tile
        acc_in, bias_in = acc_ref, None
    else:
        if last:
            own_ref, *refs = refs
        scaled_ref, bounds_ref, acc_in, bias_in, *outs, down, up = refs
    words = words_ref[...]
    if last:
        words = jnp.where(core_ref[0] == 0, words, own_ref[...])
    for m in range(4):
        codes = unpack_codes(words[0:64], m)
        for q in range(4):
            rows = m * 256 + q * 64
            down[rows : rows + 64, :] = codes[:, q * PART : (q + 1) * PART]
        up[m * 64 : (m + 1) * 64, :] = unpack_codes(words[64:128], m)
    scale = words[128:129, 0:PART].astype(F32) * (1.0 / SCALE_ONE)
    pre = jnp.dot(scaled_ref[...], down[...], preferred_element_type=F32)
    pre = pre.reshape(SPEC, SHARED, PART)
    mid, terms = relaxed(pre, *(bounds_ref[step, kind] for kind in range(4)))
    terms = jnp.sum(terms.reshape(SPEC, SHARED // 8, 8, PART), axis=1)
    bias = terms[:, :, 0:128] + terms[:, :, 128:256]
    weighted = (mid.reshape(ROWS_DEV, PART) * scale).astype(BF16)
    part = jnp.dot(weighted, up[...], preferred_element_type=F32)
    total = acc_in[...] + part
    if not first:
        bias = bias + bias_in[...]
    if last:
        keep_ref, send_ref, bias_ref = outs
        own = core_ref[0] == 0
        turned = total.T.reshape(32, 2, 16, ROWS_DEV)
        keep_ref[...] = jnp.where(own, turned[:, 0], turned[:, 1])
        send_ref[...] = jnp.where(own, turned[:, 1], turned[:, 0]).astype(BF16)
    else:
        if not first:
            acc_ref, bias_ref = outs
        acc_ref[...] = total
    bias_ref[...] = bias


def channel_part(step, core, *rest):
    acc_shape = jax.ShapeDtypeStruct((ROWS_DEV, D), F32)
    bias_shape = jax.ShapeDtypeStruct((SPEC, 8, 128), F32)
    operands = [core, *rest]
    aliases = {}
    if step == 0:
        scaled_shape = jax.ShapeDtypeStruct((ROWS_DEV, D), BF16)
        bounds_shape = jax.ShapeDtypeStruct((STEPS, 4, SHARED, PART), BF16)
        out_shape = (acc_shape, bias_shape, scaled_shape, bounds_shape)
    elif step == STEPS - 1:
        out_shape = (
            jax.ShapeDtypeStruct((32, 16, ROWS_DEV), F32),
            jax.ShapeDtypeStruct((32, 16, ROWS_DEV), BF16),
            bias_shape,
        )
    else:
        out_shape = (acc_shape, bias_shape)
        aliases = {len(operands) - 2: 0, len(operands) - 1: 1}
    smem, vmem = pl.BlockSpec(memory_space=pltpu.SMEM), pl.BlockSpec(memory_space=pltpu.VMEM)
    return pl.pallas_call(
        functools.partial(channel_kernel, step),
        out_shape=out_shape,
        in_specs=[smem] + [vmem] * (len(operands) - 1),
        out_specs=(vmem,) * len(out_shape),
        scratch_shapes=[pltpu.VMEM((D, PART), BF16), pltpu.VMEM((PART, D), BF16)],
        input_output_aliases=aliases,
        compiler_params=pltpu.CompilerParams(vmem_limit_bytes=VMEM),
        cost_estimate=pl.CostEstimate(
            flops=4 * ROWS_DEV * PART * D,
            bytes_accessed=PACKED * D * 4 + 3 * ROWS_DEV * D * 4,
            transcendentals=0,
        ),
        name="channel",
    )(*operands)


def token_kernel(got_ref, dense_ref, slopes_ref, icpt_ref, columns_ref, mid_ref, bias_ref):
    low = lax.broadcasted_iota(I32, (16, 128), 1) < SHARED
    for u in range(NTB):
        for a in range(SPEC // 2):
            cut = slice(a * 128, (a + 1) * 128)
            v = [
                got_ref[s, :, cut].astype(F32) + got_ref[s + 1, :, cut].astype(F32)
                for s in (4 * u, 4 * u + 2)
            ]
            even = jnp.where(low, v[0], pltpu.roll(v[1], SHARED, 1))
            odd = jnp.where(low, pltpu.roll(v[0], SHARED, 1), v[1])
            for r, value in ((2 * a, even), (2 * a + 1, odd)):
                columns_ref[r * 16 : (r + 1) * 16, u * 128 : (u + 1) * 128] = value.astype(BF16)
    pre = jnp.dot(columns_ref[...], dense_ref[...], preferred_element_type=F32)
    pre = pre.reshape(SPEC, 16, TH)
    mid, terms = relaxed(pre, slopes_ref[0], slopes_ref[1], icpt_ref[0], icpt_ref[1])
    mid_ref[...] = mid.reshape(SPEC * 16, TH).astype(BF16)
    terms = terms[:, 0:8, :] + terms[:, 8:16, :]
    bias_ref[...] = sum(terms[:, :, k * 128 : (k + 1) * 128] for k in range(NHB))


def token_mlp(got, dense_out, slopes, icpt):
    return pl.pallas_call(
        token_kernel,
        out_shape=(
            jax.ShapeDtypeStruct((SPEC * 16, TOK), BF16),
            jax.ShapeDtypeStruct((SPEC * 16, TH), BF16),
            jax.ShapeDtypeStruct((SPEC, 8, 128), F32),
        ),
        compiler_params=pltpu.CompilerParams(vmem_limit_bytes=VMEM),
        name="token",
    )(got, dense_out, slopes, icpt)


def back_kernel(columns_ref, mid_ref, dense_ref, out_ref):
    back = jnp.dot(mid_ref[...], dense_ref[...], preferred_element_type=F32)
    out_ref[...] = (columns_ref[...].astype(F32) + back).astype(BF16)


def token_back(columns, mid, dense_in):
    return pl.pallas_call(
        back_kernel,
        out_shape=jax.ShapeDtypeStruct((SPEC * 16, TOK), BF16),
        compiler_params=pltpu.CompilerParams(vmem_limit_bytes=VMEM),
        name="back",
    )(columns, mid, dense_in)


def on_device(
    lam_out,
    q_down,
    down_scale,
    q_up,
    up_scale,
    chan_slopes,
    chan_icpt,
    tok_in_blocks,
    tok_out_blocks,
    block_cells,
    tok_slopes,
    tok_icpt,
):
    row = lax.axis_index("rows").astype(I32).reshape(1)
    core = lax.axis_index("core").astype(I32).reshape(1)
    half = lax.axis_index("xl").astype(I32).reshape(1)
    tok_dev = lam_out.shape[0]
    slices = lax.axis_size("rows")
    ahead = [(i * 2, (i + 1) % slices * 2) for i in range(slices)]
    behind = [(i * 2 + 1, (i - 1) % slices * 2 + 1) for i in range(slices)]

    def forward(words, pairs):
        return lax.ppermute(words, ("rows", "core"), pairs)

    own = pack(half, q_down, q_up, up_scale)
    first = forward(own, ahead + behind)
    blocks = share(
        row,
        jnp.swapaxes(lam_out, 0, 1),
        chan_slopes.reshape(2, tok_dev, CH),
        chan_icpt.reshape(2, tok_dev, CH),
    )
    _, blocks = lax.optimization_barrier((first, blocks))
    team = lax.all_to_all(blocks, TEAM, 0, 0, tiled=True)
    second = forward(first, ahead + behind)
    third = forward(second, ahead + behind)
    far = forward(third, ahead)

    dense_in, dense_out = dense_blocks(block_cells, tok_in_blocks, tok_out_blocks)
    slopes = jnp.transpose(tok_slopes, (0, 2, 3, 1)).reshape(2, 16, TH)
    icpt = jnp.transpose(tok_icpt, (0, 2, 3, 1)).reshape(2, 16, TH)

    acc, chan_bias, *given = channel_part(0, core, first, down_scale.reshape(1, D), team)
    acc, chan_bias = channel_part(1, core, second, *given, acc, chan_bias)
    acc, chan_bias = channel_part(2, core, third, *given, acc, chan_bias)
    keep, send, chan_bias = channel_part(3, core, far, own, *given, acc, chan_bias)
    summed = (keep + lax.ppermute(send, "core", SWAP).astype(F32)).astype(BF16)
    got = lax.all_to_all(summed, ("z", "xh", "xl"), 0, 0, tiled=True)
    columns, mid, tok_bias = token_mlp(got, dense_out, slopes, icpt)
    own_bias = jnp.sum(chan_bias + tok_bias, axis=(1, 2))
    all_bias = lax.all_to_all(
        jnp.broadcast_to(own_bias[None, :], (64, SPEC)), MP, 0, 0, tiled=True
    )
    lam_in = token_back(columns, mid, dense_in)
    lam_in = jnp.transpose(lam_in.reshape(SPEC, 16, TOK), (2, 0, 1))
    return (lam_in, jnp.sum(all_bias, axis=0))


def solution(mesh):
    axes = Mesh(mesh.devices.reshape(8, 8, 2, 2, 2), ("rows",) + MP)
    return jax.shard_map(
        on_device,
        mesh=axes,
        in_specs=(
            P(MP, "rows", None),
            P(None, "rows"),
            P(),
            P("rows", None),
            P("rows"),
            P(None, MP, "rows", None),
            P(None, MP, "rows", None),
            P(),
            P(),
            P(),
            P(None, None, "rows", MP),
            P(None, None, "rows", MP),
        ),
        out_specs=(P(None, "rows", MP), P("rows")),
        check_vma=False,
    )
```

```python
import functools

import jax
import jax.numpy as jnp
from jax import lax
from jax.experimental import pallas as pl
from jax.experimental.pallas import tpu as pltpu
from jax.sharding import Mesh
from jax.sharding import PartitionSpec as P

D = 1024
CH = 4096
TH = 512
TOK = 1024
BLK = 128
NB = 16
SPEC = 8
NHB = 4
NTB = 8
F32 = jnp.float32
BF16 = jnp.bfloat16
I32 = jnp.int32
MP = ("z", "xh", "xl", "core")
TEAM = ("xl", "core")
SWAP = [(0, 1), (1, 0)]
VMEM = 32 * 1024 * 1024

PART = 256
STEPS = 4
SHARED = 64
ROWS_DEV = SPEC * SHARED
LAM_TILES = SPEC * (D // 128)
SCALE_ONE = float(2**38)


def pack_codes(parts):
    a, b, c, d = (p.astype(F32).astype(I32) for p in parts)
    return (a & 255) | ((b & 255) << 8) | ((c & 255) << 16) | (d << 24)


def unpack_codes(words, m):
    shifted = words << (24 - 8 * m) if m < 3 else words
    return (shifted >> 24).astype(F32).astype(BF16)


def pack_down_kernel(half_ref, down_hbm, out_ref, down_ref, sem):
    start = pl.multiple_of(half_ref[0] * PART, PART)
    copy = pltpu.make_async_copy(down_hbm.at[:, pl.ds(start, PART)], down_ref, sem)
    copy.start()
    copy.wait()
    down = pack_codes([down_ref[m * 256 : (m + 1) * 256, :] for m in range(4)])
    for k in range(4):
        out_ref[:, k * PART : (k + 1) * PART] = down[k * 64 : (k + 1) * 64, :]


def pack_up_kernel(half_ref, up_hbm, scale_hbm, out_ref, up_ref, scale_ref, sems):
    start = pl.multiple_of(half_ref[0] * PART, PART)
    copies = [
        pltpu.make_async_copy(up_hbm.at[pl.ds(start, PART), :], up_ref, sems.at[0]),
        pltpu.make_async_copy(scale_hbm.at[:, pl.ds(start, PART)], scale_ref, sems.at[1]),
    ]
    for copy in copies:
        copy.start()
    out_ref[64:72, :] = jnp.zeros((8, D), I32)
    copies[1].wait()
    scale = (scale_ref[...] * SCALE_ONE).astype(I32)
    out_ref[64:72, 0:PART] = jnp.broadcast_to(scale, (8, PART))
    copies[0].wait()
    out_ref[0:64, :] = pack_codes([up_ref[m * 64 : (m + 1) * 64, :] for m in range(4)])


def pack(half, q_down, q_up, up_scale):
    smem, hbm = pl.BlockSpec(memory_space=pltpu.SMEM), pl.BlockSpec(memory_space=pltpu.HBM)
    vmem = pl.BlockSpec(memory_space=pltpu.VMEM)
    params = pltpu.CompilerParams(vmem_limit_bytes=60 * 1024 * 1024)
    down = pl.pallas_call(
        pack_down_kernel,
        out_shape=jax.ShapeDtypeStruct((64, D), I32),
        in_specs=[smem, hbm],
        out_specs=vmem,
        scratch_shapes=[pltpu.VMEM((D, PART), BF16), pltpu.SemaphoreType.DMA(())],
        compiler_params=params,
        name="pack_down",
    )(half, q_down)
    up = pl.pallas_call(
        pack_up_kernel,
        out_shape=jax.ShapeDtypeStruct((72, D), I32),
        in_specs=[smem, hbm, hbm],
        out_specs=vmem,
        scratch_shapes=[
            pltpu.VMEM((PART, D), BF16),
            pltpu.VMEM((1, PART), F32),
            pltpu.SemaphoreType.DMA((2,)),
        ],
        compiler_params=params,
        name="pack_up",
    )(half, q_up, up_scale.reshape(1, -1))
    return down, up


def dense_kernel(cells_ref, in_ref, out_ref, dense_in_ref, dense_out_ref):
    dense_in_ref[...] = jnp.zeros_like(dense_in_ref)
    dense_out_ref[...] = jnp.zeros_like(dense_out_ref)
    for b in range(NB):
        h = pl.multiple_of(cells_ref[b] // NTB * BLK, BLK)
        u = pl.multiple_of(cells_ref[b] % NTB * BLK, BLK)
        dense_in_ref[pl.ds(h, BLK), pl.ds(u, BLK)] = in_ref[b]
        dense_out_ref[pl.ds(u, BLK), pl.ds(h, BLK)] = out_ref[b]


def dense_blocks(cells, in_blocks, out_blocks):
    return pl.pallas_call(
        dense_kernel,
        out_shape=(
            jax.ShapeDtypeStruct((TH, TOK), BF16),
            jax.ShapeDtypeStruct((TOK, TH), BF16),
        ),
        in_specs=[
            pl.BlockSpec(memory_space=pltpu.SMEM),
            pl.BlockSpec(memory_space=pltpu.VMEM),
            pl.BlockSpec(memory_space=pltpu.VMEM),
        ],
        out_specs=(
            pl.BlockSpec(memory_space=pltpu.VMEM),
            pl.BlockSpec(memory_space=pltpu.VMEM),
        ),
        compiler_params=pltpu.CompilerParams(vmem_limit_bytes=VMEM),
        name="dense",
    )(cells, in_blocks, out_blocks)


def relaxed(pre, lower, upper, icpt_low, icpt_high):
    pos = jnp.maximum(pre, 0.0)
    neg = jnp.minimum(pre, 0.0)
    mid = pos * lower.astype(F32) + neg * upper.astype(F32)
    return mid, pos * icpt_low.astype(F32) + neg * icpt_high.astype(F32)


def share_kernel(row_ref, lam_ref, slopes_ref, icpt_ref, out_ref):
    for r in range(SPEC):
        for k in range(D // 128):
            tile = lam_ref[r, :, k * 128 : (k + 1) * 128]
            for to in range(4):
                out_ref[to, r * (D // 128) + k] = tile
    row = row_ref[0]
    for to in range(4):
        half, core = to // 2, to % 2
        for j in range(STEPS):
            owner = row + (j + 1) % STEPS if core else row - (j + 1)
            start = pl.multiple_of((owner & 7) * TH + half * PART, PART)
            for kind in range(4):
                ref = slopes_ref if kind < 2 else icpt_ref
                values = ref[kind % 2, :, pl.ds(start, PART)]
                for h in range(2):
                    tile = LAM_TILES + (j * 4 + kind) * 2 + h
                    out_ref[to, tile] = values[:, h * 128 : (h + 1) * 128]


def share(row, by_row, slopes, icpt):
    tiles = LAM_TILES + 4 * STEPS * 2
    return pl.pallas_call(
        share_kernel,
        out_shape=jax.ShapeDtypeStruct((4, tiles, 16, 128), BF16),
        in_specs=[pl.BlockSpec(memory_space=pltpu.SMEM)]
        + [pl.BlockSpec(memory_space=pltpu.VMEM)] * 3,
        compiler_params=pltpu.CompilerParams(vmem_limit_bytes=60 * 1024 * 1024),
        name="share",
    )(row, by_row, slopes, icpt)


def channel_kernel(step, *refs):
    first, last = step == 0, step == STEPS - 1
    core_ref, down_words_ref, up_words_ref, *refs = refs
    if first:
        down_scale_ref, got_ref, acc_ref, bias_ref, scaled_ref, bounds_ref, down, up = refs
        for q in range(4):
            for r in range(SPEC):
                rows = slice(r * SHARED + q * 16, r * SHARED + (q + 1) * 16)
                for c in range(D // 128):
                    cut = slice(c * 128, (c + 1) * 128)
                    lam = got_ref[q, r * (D // 128) + c].astype(F32)
                    scaled_ref[rows, cut] = (lam * down_scale_ref[:, cut]).astype(BF16)
                    acc_ref[rows, cut] = 0.25 * lam
            for i in range(STEPS * 4):
                for h in range(2):
                    tile = got_ref[q, LAM_TILES + i * 2 + h]
                    bounds_ref[i // 4, i % 4, q * 16 : (q + 1) * 16, h * 128 : (h + 1) * 128] = tile
        acc_in, bias_in = acc_ref, None
    else:
        if last:
            own_down_ref, own_up_ref, *refs = refs
        scaled_ref, bounds_ref, acc_in, bias_in, *outs, down, up = refs
    down_words, up_words = down_words_ref[...], up_words_ref[...]
    if last:
        down_words = jnp.where(core_ref[0] == 0, down_words, own_down_ref[...])
        up_words = jnp.where(core_ref[0] == 0, up_words, own_up_ref[...])
    for m in range(4):
        codes = unpack_codes(down_words, m)
        for q in range(4):
            rows = m * 256 + q * 64
            down[rows : rows + 64, :] = codes[:, q * PART : (q + 1) * PART]
        up[m * 64 : (m + 1) * 64, :] = unpack_codes(up_words[0:64], m)
    scale = up_words[64:65, 0:PART].astype(F32) * (1.0 / SCALE_ONE)
    pre = jnp.dot(scaled_ref[...], down[...], preferred_element_type=F32)
    pre = pre.reshape(SPEC, SHARED, PART)
    mid, terms = relaxed(pre, *(bounds_ref[step, kind] for kind in range(4)))
    terms = jnp.sum(terms.reshape(SPEC, SHARED // 8, 8, PART), axis=1)
    bias = terms[:, :, 0:128] + terms[:, :, 128:256]
    weighted = (mid.reshape(ROWS_DEV, PART) * scale).astype(BF16)
    part = jnp.dot(weighted, up[...], preferred_element_type=F32)
    total = acc_in[...] + part
    if not first:
        bias = bias + bias_in[...]
    if last:
        keep_ref, send_ref, bias_ref = outs
        own = core_ref[0] == 0
        turned = total.T.reshape(32, 2, 16, ROWS_DEV)
        keep_ref[...] = jnp.where(own, turned[:, 0], turned[:, 1])
        send_ref[...] = jnp.where(own, turned[:, 1], turned[:, 0]).astype(BF16)
    else:
        if not first:
            acc_ref, bias_ref = outs
        acc_ref[...] = total
    bias_ref[...] = bias


def channel_part(step, core, *rest):
    acc_shape = jax.ShapeDtypeStruct((ROWS_DEV, D), F32)
    bias_shape = jax.ShapeDtypeStruct((SPEC, 8, 128), F32)
    operands = [core, *rest]
    aliases = {}
    if step == 0:
        scaled_shape = jax.ShapeDtypeStruct((ROWS_DEV, D), BF16)
        bounds_shape = jax.ShapeDtypeStruct((STEPS, 4, SHARED, PART), BF16)
        out_shape = (acc_shape, bias_shape, scaled_shape, bounds_shape)
    elif step == STEPS - 1:
        out_shape = (
            jax.ShapeDtypeStruct((32, 16, ROWS_DEV), F32),
            jax.ShapeDtypeStruct((32, 16, ROWS_DEV), BF16),
            bias_shape,
        )
    else:
        out_shape = (acc_shape, bias_shape)
        aliases = {len(operands) - 2: 0, len(operands) - 1: 1}
    smem, vmem = pl.BlockSpec(memory_space=pltpu.SMEM), pl.BlockSpec(memory_space=pltpu.VMEM)
    return pl.pallas_call(
        functools.partial(channel_kernel, step),
        out_shape=out_shape,
        in_specs=[smem] + [vmem] * (len(operands) - 1),
        out_specs=(vmem,) * len(out_shape),
        scratch_shapes=[pltpu.VMEM((D, PART), BF16), pltpu.VMEM((PART, D), BF16)],
        input_output_aliases=aliases,
        compiler_params=pltpu.CompilerParams(vmem_limit_bytes=VMEM),
        cost_estimate=pl.CostEstimate(
            flops=4 * ROWS_DEV * PART * D,
            bytes_accessed=136 * D * 4 + 3 * ROWS_DEV * D * 4,
            transcendentals=0,
        ),
        name="channel",
    )(*operands)


def token_kernel(got_ref, dense_ref, slopes_ref, icpt_ref, columns_ref, mid_ref, bias_ref):
    low = lax.broadcasted_iota(I32, (16, 128), 1) < SHARED
    for u in range(NTB):
        for a in range(SPEC // 2):
            cut = slice(a * 128, (a + 1) * 128)
            v = [
                got_ref[s, :, cut].astype(F32) + got_ref[s + 1, :, cut].astype(F32)
                for s in (4 * u, 4 * u + 2)
            ]
            even = jnp.where(low, v[0], pltpu.roll(v[1], SHARED, 1))
            odd = jnp.where(low, pltpu.roll(v[0], SHARED, 1), v[1])
            for r, value in ((2 * a, even), (2 * a + 1, odd)):
                columns_ref[r * 16 : (r + 1) * 16, u * 128 : (u + 1) * 128] = value.astype(BF16)
    pre = jnp.dot(columns_ref[...], dense_ref[...], preferred_element_type=F32)
    pre = pre.reshape(SPEC, 16, TH)
    mid, terms = relaxed(pre, slopes_ref[0], slopes_ref[1], icpt_ref[0], icpt_ref[1])
    mid_ref[...] = mid.reshape(SPEC * 16, TH).astype(BF16)
    terms = terms[:, 0:8, :] + terms[:, 8:16, :]
    bias_ref[...] = sum(terms[:, :, k * 128 : (k + 1) * 128] for k in range(NHB))


def token_mlp(got, dense_out, slopes, icpt):
    return pl.pallas_call(
        token_kernel,
        out_shape=(
            jax.ShapeDtypeStruct((SPEC * 16, TOK), BF16),
            jax.ShapeDtypeStruct((SPEC * 16, TH), BF16),
            jax.ShapeDtypeStruct((SPEC, 8, 128), F32),
        ),
        compiler_params=pltpu.CompilerParams(vmem_limit_bytes=VMEM),
        name="token",
    )(got, dense_out, slopes, icpt)


def back_kernel(columns_ref, mid_ref, dense_ref, out_ref):
    back = jnp.dot(mid_ref[...], dense_ref[...], preferred_element_type=F32)
    out_ref[...] = (columns_ref[...].astype(F32) + back).astype(BF16)


def token_back(columns, mid, dense_in):
    return pl.pallas_call(
        back_kernel,
        out_shape=jax.ShapeDtypeStruct((SPEC * 16, TOK), BF16),
        compiler_params=pltpu.CompilerParams(vmem_limit_bytes=VMEM),
        name="back",
    )(columns, mid, dense_in)


def on_device(
    lam_out,
    q_down,
    down_scale,
    q_up,
    up_scale,
    chan_slopes,
    chan_icpt,
    tok_in_blocks,
    tok_out_blocks,
    block_cells,
    tok_slopes,
    tok_icpt,
):
    row = lax.axis_index("rows").astype(I32).reshape(1)
    core = lax.axis_index("core").astype(I32).reshape(1)
    half = lax.axis_index("xl").astype(I32).reshape(1)
    tok_dev = lam_out.shape[0]
    slices = lax.axis_size("rows")
    ahead = [(i * 2, (i + 1) % slices * 2) for i in range(slices)]
    behind = [(i * 2 + 1, (i - 1) % slices * 2 + 1) for i in range(slices)]

    def forward(words, pairs):
        return tuple(lax.ppermute(w, ("rows", "core"), pairs) for w in words)

    own = pack(half, q_down, q_up, up_scale)
    first = forward(own, ahead + behind)
    _, lam, *bounds = lax.optimization_barrier((own, lam_out, chan_slopes, chan_icpt))
    blocks = share(row, jnp.swapaxes(lam, 0, 1), *(b.reshape(2, tok_dev, CH) for b in bounds))
    _, blocks = lax.optimization_barrier((first, blocks))
    team = lax.all_to_all(blocks, TEAM, 0, 0, tiled=True)
    second = forward(first, ahead + behind)
    third = forward(second, ahead + behind)
    far = forward(third, ahead)

    dense_in, dense_out = dense_blocks(block_cells, tok_in_blocks, tok_out_blocks)
    slopes = jnp.transpose(tok_slopes, (0, 2, 3, 1)).reshape(2, 16, TH)
    icpt = jnp.transpose(tok_icpt, (0, 2, 3, 1)).reshape(2, 16, TH)

    acc, chan_bias, *given = channel_part(0, core, *first, down_scale.reshape(1, D), team)
    acc, chan_bias = channel_part(1, core, *second, *given, acc, chan_bias)
    acc, chan_bias = channel_part(2, core, *third, *given, acc, chan_bias)
    keep, send, chan_bias = channel_part(3, core, *far, *own, *given, acc, chan_bias)
    summed = (keep + lax.ppermute(send, "core", SWAP).astype(F32)).astype(BF16)
    got = lax.all_to_all(summed, ("z", "xh", "xl"), 0, 0, tiled=True)
    columns, mid, tok_bias = token_mlp(got, dense_out, slopes, icpt)
    own_bias = jnp.sum(chan_bias + tok_bias, axis=(1, 2))
    all_bias = lax.all_to_all(
        jnp.broadcast_to(own_bias[None, :], (64, SPEC)), MP, 0, 0, tiled=True
    )
    lam_in = token_back(columns, mid, dense_in)
    lam_in = jnp.transpose(lam_in.reshape(SPEC, 16, TOK), (2, 0, 1))
    return (lam_in, jnp.sum(all_bias, axis=0))


def solution(mesh):
    axes = Mesh(mesh.devices.reshape(8, 8, 2, 2, 2), ("rows",) + MP)
    return jax.shard_map(
        on_device,
        mesh=axes,
        in_specs=(
            P(MP, "rows", None),
            P(None, "rows"),
            P(),
            P("rows", None),
            P("rows"),
            P(None, MP, "rows", None),
            P(None, MP, "rows", None),
            P(),
            P(),
            P(),
            P(None, None, "rows", MP),
            P(None, None, "rows", MP),
        ),
        out_specs=(P(None, "rows", MP), P("rows")),
        check_vma=False,
    )
```

```python
import functools

import jax
import jax.numpy as jnp
from jax import lax
from jax.experimental import pallas as pl
from jax.experimental.pallas import tpu as pltpu
from jax.sharding import Mesh
from jax.sharding import PartitionSpec as P

D = 1024
CH = 4096
TH = 512
TOK = 1024
BLK = 128
NB = 16
SPEC = 8
NHB = 4
NTB = 8
F32 = jnp.float32
BF16 = jnp.bfloat16
I32 = jnp.int32
MP = ("z", "xh", "xl", "core")
TEAM = ("xl", "core")
SWAP = [(0, 1), (1, 0)]
VMEM = 32 * 1024 * 1024

PART = 256
STEPS = 4
SHARED = 64
ROWS_DEV = SPEC * SHARED
LAM_TILES = SPEC * (D // 128)
SCALE_ONE = float(2**38)


def pack_codes(parts):
    a, b, c, d = (p.astype(F32).astype(I32) for p in parts)
    return (a & 255) | ((b & 255) << 8) | ((c & 255) << 16) | (d << 24)


def unpack_codes(words, m):
    shifted = words << (24 - 8 * m) if m < 3 else words
    return (shifted >> 24).astype(F32).astype(BF16)


def pack_kernel(half_ref, down_hbm, up_hbm, scale_hbm, *refs):
    out_refs, (down_ref, up_ref, scale_ref, sems) = refs[:2], refs[2:]
    start = pl.multiple_of(half_ref[0] * PART, PART)
    copies = [
        pltpu.make_async_copy(down_hbm.at[:, pl.ds(start, PART)], down_ref, sems.at[0]),
        pltpu.make_async_copy(up_hbm.at[pl.ds(start, PART), :], up_ref, sems.at[1]),
        pltpu.make_async_copy(scale_hbm.at[:, pl.ds(start, PART)], scale_ref, sems.at[2]),
    ]
    for copy in copies:
        copy.start()
    for out_ref in out_refs:
        out_ref[64:72, :] = jnp.zeros((8, D), I32)
    copies[0].wait()
    down = pack_codes([down_ref[m * 256 : (m + 1) * 256, :] for m in range(4)])
    for h, out_ref in enumerate(out_refs):
        for k in range(8):
            cut = slice(k * 128, (k + 1) * 128)
            out_ref[0:32, cut] = down[k * 32 : (k + 1) * 32, h * 128 : (h + 1) * 128]
    copies[1].wait()
    copies[2].wait()
    scale = (scale_ref[...] * SCALE_ONE).astype(I32)
    for h, out_ref in enumerate(out_refs):
        rows = [h * 128 + m * 32 for m in range(4)]
        out_ref[32:64, :] = pack_codes([up_ref[i : i + 32, :] for i in rows])
        out_ref[64:72, 0:128] = jnp.broadcast_to(scale[:, h * 128 : (h + 1) * 128], (8, 128))


def pack(half, q_down, q_up, up_scale):
    smem, hbm = pl.BlockSpec(memory_space=pltpu.SMEM), pl.BlockSpec(memory_space=pltpu.HBM)
    vmem = pl.BlockSpec(memory_space=pltpu.VMEM)
    return pl.pallas_call(
        pack_kernel,
        out_shape=(jax.ShapeDtypeStruct((72, D), I32),) * 2,
        in_specs=[smem, hbm, hbm, hbm],
        out_specs=(vmem, vmem),
        scratch_shapes=[
            pltpu.VMEM((D, PART), BF16),
            pltpu.VMEM((PART, D), BF16),
            pltpu.VMEM((1, PART), F32),
            pltpu.SemaphoreType.DMA((3,)),
        ],
        compiler_params=pltpu.CompilerParams(vmem_limit_bytes=60 * 1024 * 1024),
        name="pack",
    )(half, q_down, q_up, up_scale.reshape(1, -1))


def dense_kernel(cells_ref, in_ref, out_ref, dense_in_ref, dense_out_ref):
    dense_in_ref[...] = jnp.zeros_like(dense_in_ref)
    dense_out_ref[...] = jnp.zeros_like(dense_out_ref)
    for b in range(NB):
        h = pl.multiple_of(cells_ref[b] // NTB * BLK, BLK)
        u = pl.multiple_of(cells_ref[b] % NTB * BLK, BLK)
        dense_in_ref[pl.ds(h, BLK), pl.ds(u, BLK)] = in_ref[b]
        dense_out_ref[pl.ds(u, BLK), pl.ds(h, BLK)] = out_ref[b]


def dense_blocks(cells, in_blocks, out_blocks):
    return pl.pallas_call(
        dense_kernel,
        out_shape=(
            jax.ShapeDtypeStruct((TH, TOK), BF16),
            jax.ShapeDtypeStruct((TOK, TH), BF16),
        ),
        in_specs=[
            pl.BlockSpec(memory_space=pltpu.SMEM),
            pl.BlockSpec(memory_space=pltpu.VMEM),
            pl.BlockSpec(memory_space=pltpu.VMEM),
        ],
        out_specs=(
            pl.BlockSpec(memory_space=pltpu.VMEM),
            pl.BlockSpec(memory_space=pltpu.VMEM),
        ),
        compiler_params=pltpu.CompilerParams(vmem_limit_bytes=VMEM),
        name="dense",
    )(cells, in_blocks, out_blocks)


def relaxed(pre, lower, upper, icpt_low, icpt_high):
    pos = jnp.maximum(pre, 0.0)
    neg = jnp.minimum(pre, 0.0)
    mid = pos * lower.astype(F32) + neg * upper.astype(F32)
    return mid, pos * icpt_low.astype(F32) + neg * icpt_high.astype(F32)


def share_kernel(row_ref, lam_ref, slopes_ref, icpt_ref, out_ref):
    for r in range(SPEC):
        for k in range(D // 128):
            tile = lam_ref[r, :, k * 128 : (k + 1) * 128]
            for to in range(4):
                out_ref[to, r * (D // 128) + k] = tile
    row = row_ref[0]
    for to in range(4):
        half, core = to // 2, to % 2
        for j in range(STEPS):
            if j < STEPS - 1:
                owner = row + (j + 1) if core else row - (j + 1)
                cuts = [(owner, 0), (owner, 1)]
            else:
                cuts = [(row + STEPS, core), (row, core)]
            for h, (owner, chunk) in enumerate(cuts):
                start = pl.multiple_of((owner & 7) * TH + half * PART + chunk * 128, 128)
                for kind in range(4):
                    ref = slopes_ref if kind < 2 else icpt_ref
                    values = ref[kind % 2, :, pl.ds(start, 128)]
                    out_ref[to, LAM_TILES + (j * 4 + kind) * 2 + h] = values


def share(row, by_row, slopes, icpt):
    tiles = LAM_TILES + 4 * STEPS * 2
    return pl.pallas_call(
        share_kernel,
        out_shape=jax.ShapeDtypeStruct((4, tiles, 16, 128), BF16),
        in_specs=[pl.BlockSpec(memory_space=pltpu.SMEM)]
        + [pl.BlockSpec(memory_space=pltpu.VMEM)] * 3,
        compiler_params=pltpu.CompilerParams(vmem_limit_bytes=60 * 1024 * 1024),
        name="share",
    )(row, by_row, slopes, icpt)


def channel_kernel(step, *refs):
    first, last = step == 0, step == STEPS - 1
    core_ref, *words, refs = refs[0], refs[1], refs[2], refs[3:]
    if first:
        down_scale_ref, got_ref, acc_ref, bias_ref, scaled_ref, bounds_ref, down, up = refs
        for q in range(4):
            for r in range(SPEC):
                rows = slice(r * SHARED + q * 16, r * SHARED + (q + 1) * 16)
                for c in range(D // 128):
                    cut = slice(c * 128, (c + 1) * 128)
                    lam = got_ref[q, r * (D // 128) + c].astype(F32)
                    scaled_ref[rows, cut] = (lam * down_scale_ref[:, cut]).astype(BF16)
                    acc_ref[rows, cut] = 0.25 * lam
            for i in range(STEPS * 4):
                for h in range(2):
                    tile = got_ref[q, LAM_TILES + i * 2 + h]
                    bounds_ref[i // 4, i % 4, q * 16 : (q + 1) * 16, h * 128 : (h + 1) * 128] = tile
        acc_in, bias_in = acc_ref, None
    else:
        if last:
            *own_words, refs = refs[0], refs[1], refs[2:]
        scaled_ref, bounds_ref, acc_in, bias_in, *outs, down, up = refs
    words = [w[...] for w in words]
    if last:
        own_core = core_ref[0] == 0
        words = [
            jnp.where(own_core, words[0], words[1]),
            jnp.where(own_core, own_words[0][...], own_words[1][...]),
        ]
    for h, chunk in enumerate(words):
        for m in range(4):
            codes = unpack_codes(chunk[0:32], m)
            for q in range(8):
                rows = m * 256 + q * 32
                down[rows : rows + 32, h * 128 : (h + 1) * 128] = codes[:, q * 128 : (q + 1) * 128]
            rows = h * 128 + m * 32
            up[rows : rows + 32, :] = unpack_codes(chunk[32:64], m)
    scale = jnp.concatenate([chunk[64:65, 0:128] for chunk in words], axis=1)
    scale = scale.astype(F32) * (1.0 / SCALE_ONE)
    pre = jnp.dot(scaled_ref[...], down[...], preferred_element_type=F32)
    pre = pre.reshape(SPEC, SHARED, PART)
    mid, terms = relaxed(pre, *(bounds_ref[step, kind] for kind in range(4)))
    terms = jnp.sum(terms.reshape(SPEC, SHARED // 8, 8, PART), axis=1)
    bias = terms[:, :, 0:128] + terms[:, :, 128:256]
    weighted = (mid.reshape(ROWS_DEV, PART) * scale).astype(BF16)
    part = jnp.dot(weighted, up[...], preferred_element_type=F32)
    total = acc_in[...] + part
    if not first:
        bias = bias + bias_in[...]
    if last:
        keep_ref, send_ref, bias_ref = outs
        own = core_ref[0] == 0
        turned = total.T.reshape(32, 2, 16, ROWS_DEV)
        keep_ref[...] = jnp.where(own, turned[:, 0], turned[:, 1])
        send_ref[...] = jnp.where(own, turned[:, 1], turned[:, 0]).astype(BF16)
    else:
        if not first:
            acc_ref, bias_ref = outs
        acc_ref[...] = total
    bias_ref[...] = bias


def channel_part(step, core, *rest):
    acc_shape = jax.ShapeDtypeStruct((ROWS_DEV, D), F32)
    bias_shape = jax.ShapeDtypeStruct((SPEC, 8, 128), F32)
    operands = [core, *rest]
    aliases = {}
    if step == 0:
        scaled_shape = jax.ShapeDtypeStruct((ROWS_DEV, D), BF16)
        bounds_shape = jax.ShapeDtypeStruct((STEPS, 4, SHARED, PART), BF16)
        out_shape = (acc_shape, bias_shape, scaled_shape, bounds_shape)
    elif step == STEPS - 1:
        out_shape = (
            jax.ShapeDtypeStruct((32, 16, ROWS_DEV), F32),
            jax.ShapeDtypeStruct((32, 16, ROWS_DEV), BF16),
            bias_shape,
        )
    else:
        out_shape = (acc_shape, bias_shape)
        aliases = {len(operands) - 2: 0, len(operands) - 1: 1}
    smem, vmem = pl.BlockSpec(memory_space=pltpu.SMEM), pl.BlockSpec(memory_space=pltpu.VMEM)
    return pl.pallas_call(
        functools.partial(channel_kernel, step),
        out_shape=out_shape,
        in_specs=[smem] + [vmem] * (len(operands) - 1),
        out_specs=(vmem,) * len(out_shape),
        scratch_shapes=[pltpu.VMEM((D, PART), BF16), pltpu.VMEM((PART, D), BF16)],
        input_output_aliases=aliases,
        compiler_params=pltpu.CompilerParams(vmem_limit_bytes=VMEM),
        cost_estimate=pl.CostEstimate(
            flops=4 * ROWS_DEV * PART * D,
            bytes_accessed=144 * D * 4 + 3 * ROWS_DEV * D * 4,
            transcendentals=0,
        ),
        name="channel",
    )(*operands)


def token_kernel(got_ref, dense_ref, slopes_ref, icpt_ref, columns_ref, mid_ref, bias_ref):
    low = lax.broadcasted_iota(I32, (16, 128), 1) < SHARED
    for u in range(NTB):
        for a in range(SPEC // 2):
            cut = slice(a * 128, (a + 1) * 128)
            v = [
                got_ref[s, :, cut].astype(F32) + got_ref[s + 1, :, cut].astype(F32)
                for s in (4 * u, 4 * u + 2)
            ]
            even = jnp.where(low, v[0], pltpu.roll(v[1], SHARED, 1))
            odd = jnp.where(low, pltpu.roll(v[0], SHARED, 1), v[1])
            for r, value in ((2 * a, even), (2 * a + 1, odd)):
                columns_ref[r * 16 : (r + 1) * 16, u * 128 : (u + 1) * 128] = value.astype(BF16)
    pre = jnp.dot(columns_ref[...], dense_ref[...], preferred_element_type=F32)
    pre = pre.reshape(SPEC, 16, TH)
    mid, terms = relaxed(pre, slopes_ref[0], slopes_ref[1], icpt_ref[0], icpt_ref[1])
    mid_ref[...] = mid.reshape(SPEC * 16, TH).astype(BF16)
    terms = terms[:, 0:8, :] + terms[:, 8:16, :]
    bias_ref[...] = sum(terms[:, :, k * 128 : (k + 1) * 128] for k in range(NHB))


def token_mlp(got, dense_out, slopes, icpt):
    return pl.pallas_call(
        token_kernel,
        out_shape=(
            jax.ShapeDtypeStruct((SPEC * 16, TOK), BF16),
            jax.ShapeDtypeStruct((SPEC * 16, TH), BF16),
            jax.ShapeDtypeStruct((SPEC, 8, 128), F32),
        ),
        compiler_params=pltpu.CompilerParams(vmem_limit_bytes=VMEM),
        name="token",
    )(got, dense_out, slopes, icpt)


def back_kernel(columns_ref, mid_ref, dense_ref, out_ref):
    back = jnp.dot(mid_ref[...], dense_ref[...], preferred_element_type=F32)
    out_ref[...] = (columns_ref[...].astype(F32) + back).astype(BF16)


def token_back(columns, mid, dense_in):
    return pl.pallas_call(
        back_kernel,
        out_shape=jax.ShapeDtypeStruct((SPEC * 16, TOK), BF16),
        compiler_params=pltpu.CompilerParams(vmem_limit_bytes=VMEM),
        name="back",
    )(columns, mid, dense_in)


def on_device(
    lam_out,
    q_down,
    down_scale,
    q_up,
    up_scale,
    chan_slopes,
    chan_icpt,
    tok_in_blocks,
    tok_out_blocks,
    block_cells,
    tok_slopes,
    tok_icpt,
):
    row = lax.axis_index("rows").astype(I32).reshape(1)
    core = lax.axis_index("core").astype(I32).reshape(1)
    half = lax.axis_index("xl").astype(I32).reshape(1)
    tok_dev = lam_out.shape[0]
    slices = lax.axis_size("rows")
    ahead = [(i * 2, (i + 1) % slices * 2) for i in range(slices)]
    behind = [(i * 2 + 1, (i - 1) % slices * 2 + 1) for i in range(slices)]

    def forward(words, pairs):
        return tuple(lax.ppermute(w, ("rows", "core"), pairs) for w in words)

    own = pack(half, q_down, q_up, up_scale)
    first = forward(own, ahead + behind)
    _, lam, *bounds = lax.optimization_barrier((own, lam_out, chan_slopes, chan_icpt))
    blocks = share(row, jnp.swapaxes(lam, 0, 1), *(b.reshape(2, tok_dev, CH) for b in bounds))
    _, blocks = lax.optimization_barrier((first, blocks))
    team = lax.all_to_all(blocks, TEAM, 0, 0, tiled=True)
    second = forward(first, ahead + behind)
    third = forward(second, ahead + behind)
    far = forward(third[:1], ahead) + forward(third[1:], behind)

    dense_in, dense_out = dense_blocks(block_cells, tok_in_blocks, tok_out_blocks)
    slopes = jnp.transpose(tok_slopes, (0, 2, 3, 1)).reshape(2, 16, TH)
    icpt = jnp.transpose(tok_icpt, (0, 2, 3, 1)).reshape(2, 16, TH)

    acc, chan_bias, *given = channel_part(0, core, *first, down_scale.reshape(1, D), team)
    acc, chan_bias = channel_part(1, core, *second, *given, acc, chan_bias)
    acc, chan_bias = channel_part(2, core, *third, *given, acc, chan_bias)
    keep, send, chan_bias = channel_part(3, core, *far, *own, *given, acc, chan_bias)
    summed = (keep + lax.ppermute(send, "core", SWAP).astype(F32)).astype(BF16)
    got = lax.all_to_all(summed, ("z", "xh", "xl"), 0, 0, tiled=True)
    columns, mid, tok_bias = token_mlp(got, dense_out, slopes, icpt)
    own_bias = jnp.sum(chan_bias + tok_bias, axis=(1, 2))
    all_bias = lax.all_to_all(
        jnp.broadcast_to(own_bias[None, :], (64, SPEC)), MP, 0, 0, tiled=True
    )
    lam_in = token_back(columns, mid, dense_in)
    lam_in = jnp.transpose(lam_in.reshape(SPEC, 16, TOK), (2, 0, 1))
    return (lam_in, jnp.sum(all_bias, axis=0))


def solution(mesh):
    axes = Mesh(mesh.devices.reshape(8, 8, 2, 2, 2), ("rows",) + MP)
    return jax.shard_map(
        on_device,
        mesh=axes,
        in_specs=(
            P(MP, "rows", None),
            P(None, "rows"),
            P(),
            P("rows", None),
            P("rows"),
            P(None, MP, "rows", None),
            P(None, MP, "rows", None),
            P(),
            P(),
            P(),
            P(None, None, "rows", MP),
            P(None, None, "rows", MP),
        ),
        out_specs=(P(None, "rows", MP), P("rows")),
        check_vma=False,
    )
```

```python
import functools

import jax
import jax.numpy as jnp
from jax import lax
from jax.experimental import pallas as pl
from jax.experimental.pallas import tpu as pltpu
from jax.sharding import Mesh
from jax.sharding import PartitionSpec as P

D = 1024
CH = 4096
TH = 512
TOK = 1024
BLK = 128
NB = 16
SPEC = 8
NHB = 4
NTB = 8
F32 = jnp.float32
BF16 = jnp.bfloat16
I32 = jnp.int32
MP = ("z", "x", "core")
SWAP = [(0, 1), (1, 0)]
VMEM = 32 * 1024 * 1024

PART = 512
CHUNK = 256
STEPS = 4
SHARED = 32
ROWS_DEV = SPEC * SHARED
PACKED = 136
LAM_TILES = SPEC * (D // 128)
SCALE_ONE = float(2**38)


def pack_codes(parts):
    a, b, c, d = (p.astype(F32).astype(I32) for p in parts)
    return (a & 255) | ((b & 255) << 8) | ((c & 255) << 16) | (d << 24)


def unpack_codes(words, m):
    shifted = words << (24 - 8 * m) if m < 3 else words
    return (shifted >> 24).astype(F32).astype(BF16)


def pack_kernel(start, down_hbm, up_hbm, scale_hbm, out_ref, down_ref, up_ref, scale_ref, sems):
    cut = pl.ds(start, CHUNK)
    copies = [
        pltpu.make_async_copy(down_hbm.at[:, cut], down_ref, sems.at[0]),
        pltpu.make_async_copy(up_hbm.at[cut, :], up_ref, sems.at[1]),
        pltpu.make_async_copy(scale_hbm.at[:, cut], scale_ref, sems.at[2]),
    ]
    for copy in copies:
        copy.start()
    out_ref[128:136, :] = jnp.zeros((8, D), I32)
    copies[0].wait()
    down = pack_codes([down_ref[m * 256 : (m + 1) * 256, :] for m in range(4)])
    for k in range(4):
        out_ref[0:64, k * CHUNK : (k + 1) * CHUNK] = down[k * 64 : (k + 1) * 64, :]
    copies[1].wait()
    out_ref[64:128, :] = pack_codes([up_ref[m * 64 : (m + 1) * 64, :] for m in range(4)])
    copies[2].wait()
    scale = (scale_ref[...] * SCALE_ONE).astype(I32)
    out_ref[128:136, 0:CHUNK] = jnp.broadcast_to(scale, (8, CHUNK))


def pack(chunk, q_down, q_up, up_scale):
    hbm, vmem = pl.BlockSpec(memory_space=pltpu.HBM), pl.BlockSpec(memory_space=pltpu.VMEM)
    return pl.pallas_call(
        functools.partial(pack_kernel, chunk * CHUNK),
        out_shape=jax.ShapeDtypeStruct((PACKED, D), I32),
        in_specs=[hbm, hbm, hbm],
        out_specs=vmem,
        scratch_shapes=[
            pltpu.VMEM((D, CHUNK), BF16),
            pltpu.VMEM((CHUNK, D), BF16),
            pltpu.VMEM((1, CHUNK), F32),
            pltpu.SemaphoreType.DMA((3,)),
        ],
        compiler_params=pltpu.CompilerParams(vmem_limit_bytes=60 * 1024 * 1024),
        name="pack",
    )(q_down, q_up, up_scale.reshape(1, -1))


def dense_kernel(cells_ref, in_ref, out_ref, dense_in_ref, dense_out_ref):
    dense_in_ref[...] = jnp.zeros_like(dense_in_ref)
    dense_out_ref[...] = jnp.zeros_like(dense_out_ref)
    for b in range(NB):
        h = pl.multiple_of(cells_ref[b] // NTB * BLK, BLK)
        u = pl.multiple_of(cells_ref[b] % NTB * BLK, BLK)
        dense_in_ref[pl.ds(h, BLK), pl.ds(u, BLK)] = in_ref[b]
        dense_out_ref[pl.ds(u, BLK), pl.ds(h, BLK)] = out_ref[b]


def dense_blocks(cells, in_blocks, out_blocks):
    return pl.pallas_call(
        dense_kernel,
        out_shape=(
            jax.ShapeDtypeStruct((TH, TOK), BF16),
            jax.ShapeDtypeStruct((TOK, TH), BF16),
        ),
        in_specs=[
            pl.BlockSpec(memory_space=pltpu.SMEM),
            pl.BlockSpec(memory_space=pltpu.VMEM),
            pl.BlockSpec(memory_space=pltpu.VMEM),
        ],
        out_specs=(
            pl.BlockSpec(memory_space=pltpu.VMEM),
            pl.BlockSpec(memory_space=pltpu.VMEM),
        ),
        compiler_params=pltpu.CompilerParams(vmem_limit_bytes=VMEM),
        name="dense",
    )(cells, in_blocks, out_blocks)


def relaxed(pre, lower, upper, icpt_low, icpt_high):
    pos = jnp.maximum(pre, 0.0)
    neg = jnp.minimum(pre, 0.0)
    mid = pos * lower.astype(F32) + neg * upper.astype(F32)
    return mid, pos * icpt_low.astype(F32) + neg * icpt_high.astype(F32)


def share_kernel(place_ref, lam_ref, slopes_ref, icpt_ref, *out_refs):
    for r in range(SPEC):
        for k in range(D // 128):
            tile = lam_ref[r, :, k * 128 : (k + 1) * 128]
            for out_ref in out_refs:
                out_ref[r * (D // 128) + k] = tile
    row = place_ref[1]
    for k, out_ref in enumerate(out_refs):
        core = place_ref[0] ^ k
        for j in range(STEPS):
            if j < STEPS - 1:
                owner = row + (2 * core - 1) * (j + 1)
                cuts = [(owner, 0), (owner, 1)]
            else:
                cuts = [(row + STEPS, core), (row, core)]
            for h, (owner, chunk) in enumerate(cuts):
                start = pl.multiple_of((owner & 7) * PART + chunk * CHUNK, CHUNK)
                for kind in range(4):
                    ref = slopes_ref if kind < 2 else icpt_ref
                    values = ref[kind % 2, :, pl.ds(start, CHUNK)]
                    tile = LAM_TILES + (j * 4 + kind) * 4 + h * 2
                    out_ref[tile] = values[:, 0:128]
                    out_ref[tile + 1] = values[:, 128:256]


def share(place, by_row, slopes, icpt):
    tiles = LAM_TILES + 4 * STEPS * 4
    return pl.pallas_call(
        share_kernel,
        out_shape=(jax.ShapeDtypeStruct((tiles, 16, 128), BF16),) * 2,
        in_specs=[pl.BlockSpec(memory_space=pltpu.SMEM)]
        + [pl.BlockSpec(memory_space=pltpu.VMEM)] * 3,
        compiler_params=pltpu.CompilerParams(vmem_limit_bytes=60 * 1024 * 1024),
        name="share",
    )(place, by_row, slopes, icpt)


def channel_kernel(step, *refs):
    first, last = step == 0, step == STEPS - 1
    core_ref, *words, refs = refs[0], refs[1], refs[2], refs[3:]
    if first:
        down_scale_ref, *team, acc_ref, bias_ref, scaled_ref, bounds_ref, down, up = refs
        for k, got_ref in enumerate(team):
            start = (core_ref[0] ^ k) * 16
            for r in range(SPEC):
                rows = pl.ds(pl.multiple_of(r * SHARED + start, 16), 16)
                for c in range(D // 128):
                    cut = slice(c * 128, (c + 1) * 128)
                    lam = got_ref[r * (D // 128) + c].astype(F32)
                    scaled_ref[rows, cut] = (lam * down_scale_ref[:, cut]).astype(BF16)
                    acc_ref[rows, cut] = 0.5 * lam
            rows = pl.ds(pl.multiple_of(start, 16), 16)
            for i in range(STEPS * 4):
                for h in range(4):
                    tile = got_ref[LAM_TILES + i * 4 + h]
                    bounds_ref[i // 4, i % 4, rows, h * 128 : (h + 1) * 128] = tile
        acc_in, bias_in = acc_ref, None
    else:
        if last:
            *own_words, refs = refs[0], refs[1], refs[2:]
        scaled_ref, bounds_ref, acc_in, bias_in, *outs, down, up = refs
    words = [w[...] for w in words]
    if last:
        own_core = core_ref[0] == 0
        words = [
            jnp.where(own_core, words[0], words[1]),
            jnp.where(own_core, own_words[0][...], own_words[1][...]),
        ]
    for h, chunk in enumerate(words):
        for m in range(4):
            codes = unpack_codes(chunk[0:64], m)
            for q in range(4):
                rows = m * 256 + q * 64
                cut = slice(q * CHUNK, (q + 1) * CHUNK)
                down[rows : rows + 64, h * CHUNK : (h + 1) * CHUNK] = codes[:, cut]
            rows = h * CHUNK + m * 64
            up[rows : rows + 64, :] = unpack_codes(chunk[64:128], m)
    scale = jnp.concatenate([chunk[128:129, 0:CHUNK] for chunk in words], axis=1)
    scale = scale.astype(F32) * (1.0 / SCALE_ONE)
    pre = jnp.dot(scaled_ref[...], down[...], preferred_element_type=F32)
    pre = pre.reshape(SPEC, SHARED, PART)
    mid, terms = relaxed(pre, *(bounds_ref[step, kind] for kind in range(4)))
    terms = jnp.sum(terms.reshape(SPEC, SHARED // 8, 8, PART), axis=1)
    bias = sum(terms[:, :, k * 128 : (k + 1) * 128] for k in range(PART // 128))
    weighted = (mid.reshape(ROWS_DEV, PART) * scale).astype(BF16)
    part = jnp.dot(weighted, up[...], preferred_element_type=F32)
    total = acc_in[...] + part
    if not first:
        bias = bias + bias_in[...]
    if last:
        keep_ref, send_ref, bias_ref = outs
        own = core_ref[0] == 0
        turned = total.T.reshape(32, 2, 16, ROWS_DEV)
        keep_ref[...] = jnp.where(own, turned[:, 0], turned[:, 1])
        send_ref[...] = jnp.where(own, turned[:, 1], turned[:, 0]).astype(BF16)
    else:
        if not first:
            acc_ref, bias_ref = outs
        acc_ref[...] = total
    bias_ref[...] = bias


def channel_part(step, core, *rest):
    acc_shape = jax.ShapeDtypeStruct((ROWS_DEV, D), F32)
    bias_shape = jax.ShapeDtypeStruct((SPEC, 8, 128), F32)
    operands = [core, *rest]
    aliases = {}
    if step == 0:
        scaled_shape = jax.ShapeDtypeStruct((ROWS_DEV, D), BF16)
        bounds_shape = jax.ShapeDtypeStruct((STEPS, 4, SHARED, PART), BF16)
        out_shape = (acc_shape, bias_shape, scaled_shape, bounds_shape)
    elif step == STEPS - 1:
        out_shape = (
            jax.ShapeDtypeStruct((32, 16, ROWS_DEV), F32),
            jax.ShapeDtypeStruct((32, 16, ROWS_DEV), BF16),
            bias_shape,
        )
    else:
        out_shape = (acc_shape, bias_shape)
        aliases = {len(operands) - 2: 0, len(operands) - 1: 1}
    smem, vmem = pl.BlockSpec(memory_space=pltpu.SMEM), pl.BlockSpec(memory_space=pltpu.VMEM)
    return pl.pallas_call(
        functools.partial(channel_kernel, step),
        out_shape=out_shape,
        in_specs=[smem] + [vmem] * (len(operands) - 1),
        out_specs=(vmem,) * len(out_shape),
        scratch_shapes=[pltpu.VMEM((D, PART), BF16), pltpu.VMEM((PART, D), BF16)],
        input_output_aliases=aliases,
        compiler_params=pltpu.CompilerParams(vmem_limit_bytes=VMEM),
        cost_estimate=pl.CostEstimate(
            flops=4 * ROWS_DEV * PART * D,
            bytes_accessed=2 * PACKED * D * 4 + 3 * ROWS_DEV * D * 4,
            transcendentals=0,
        ),
        name="channel",
    )(*operands)


def token_kernel(got_ref, dense_ref, slopes_ref, icpt_ref, columns_ref, mid_ref, bias_ref):
    lane = lax.broadcasted_iota(I32, (16, 128), 1) // 32
    for u in range(NTB):
        for a in range(2):
            v = [got_ref[4 * u + p, :, a * 128 : (a + 1) * 128].astype(F32) for p in range(4)]
            for bit in (1, 2):
                low = (lane & bit) == 0
                new = list(v)
                for p in range(4):
                    if p & bit == 0:
                        q = p + bit
                        new[p] = jnp.where(low, v[p], pltpu.roll(v[q], 32 * bit, 1))
                        new[q] = jnp.where(low, pltpu.roll(v[p], 128 - 32 * bit, 1), v[q])
                v = new
            for q in range(4):
                r = 4 * a + q
                columns_ref[r * 16 : (r + 1) * 16, u * 128 : (u + 1) * 128] = v[q].astype(BF16)
    pre = jnp.dot(columns_ref[...], dense_ref[...], preferred_element_type=F32)
    pre = pre.reshape(SPEC, 16, TH)
    mid, terms = relaxed(pre, slopes_ref[0], slopes_ref[1], icpt_ref[0], icpt_ref[1])
    mid_ref[...] = mid.reshape(SPEC * 16, TH).astype(BF16)
    terms = terms[:, 0:8, :] + terms[:, 8:16, :]
    bias_ref[...] = sum(terms[:, :, k * 128 : (k + 1) * 128] for k in range(NHB))


def token_mlp(got, dense_out, slopes, icpt):
    return pl.pallas_call(
        token_kernel,
        out_shape=(
            jax.ShapeDtypeStruct((SPEC * 16, TOK), BF16),
            jax.ShapeDtypeStruct((SPEC * 16, TH), BF16),
            jax.ShapeDtypeStruct((SPEC, 8, 128), F32),
        ),
        compiler_params=pltpu.CompilerParams(vmem_limit_bytes=VMEM),
        name="token",
    )(got, dense_out, slopes, icpt)


def back_kernel(columns_ref, mid_ref, dense_ref, out_ref):
    back = jnp.dot(mid_ref[...], dense_ref[...], preferred_element_type=F32)
    out_ref[...] = (columns_ref[...].astype(F32) + back).astype(BF16)


def token_back(columns, mid, dense_in):
    return pl.pallas_call(
        back_kernel,
        out_shape=jax.ShapeDtypeStruct((SPEC * 16, TOK), BF16),
        compiler_params=pltpu.CompilerParams(vmem_limit_bytes=VMEM),
        name="back",
    )(columns, mid, dense_in)


def on_device(
    lam_out,
    q_down,
    down_scale,
    q_up,
    up_scale,
    chan_slopes,
    chan_icpt,
    tok_in_blocks,
    tok_out_blocks,
    block_cells,
    tok_slopes,
    tok_icpt,
):
    core, row = lax.axis_index("core").astype(I32), lax.axis_index("rows").astype(I32)
    place, core = jnp.stack([core, row]), core.reshape(1)
    tok_dev = lam_out.shape[0]
    slices = lax.axis_size("rows")
    ahead = [(i * 2, (i + 1) % slices * 2) for i in range(slices)]
    behind = [(i * 2 + 1, (i - 1) % slices * 2 + 1) for i in range(slices)]

    def forward(words, pairs):
        return tuple(lax.ppermute(w, ("rows", "core"), pairs) for w in words)

    own = tuple(pack(chunk, q_down, q_up, up_scale) for chunk in range(2))
    first = forward(own, ahead + behind)
    _, lam, *bounds = lax.optimization_barrier((own, lam_out, chan_slopes, chan_icpt))
    keep_part, send_part = share(
        place, jnp.swapaxes(lam, 0, 1), *(b.reshape(2, tok_dev, CH) for b in bounds)
    )
    team = (keep_part, lax.ppermute(send_part, "core", SWAP))
    second = forward(first, ahead + behind)
    third = forward(second, ahead + behind)
    far = forward(third[:1], ahead) + forward(third[1:], behind)

    dense_in, dense_out = dense_blocks(block_cells, tok_in_blocks, tok_out_blocks)
    slopes = jnp.transpose(tok_slopes, (0, 2, 3, 1)).reshape(2, 16, TH)
    icpt = jnp.transpose(tok_icpt, (0, 2, 3, 1)).reshape(2, 16, TH)

    acc, chan_bias, *given = channel_part(0, core, *first, down_scale.reshape(1, D), *team)
    acc, chan_bias = channel_part(1, core, *second, *given, acc, chan_bias)
    acc, chan_bias = channel_part(2, core, *third, *given, acc, chan_bias)
    keep, send, chan_bias = channel_part(3, core, *far, *own, *given, acc, chan_bias)
    summed = (keep + lax.ppermute(send, "core", SWAP).astype(F32)).astype(BF16)
    got = lax.all_to_all(summed, ("z", "x"), 0, 0, tiled=True)
    columns, mid, tok_bias = token_mlp(got, dense_out, slopes, icpt)
    own_bias = jnp.sum(chan_bias + tok_bias, axis=(1, 2))
    all_bias = lax.all_to_all(
        jnp.broadcast_to(own_bias[None, :], (64, SPEC)), MP, 0, 0, tiled=True
    )
    lam_in = token_back(columns, mid, dense_in)
    lam_in = jnp.transpose(lam_in.reshape(SPEC, 16, TOK), (2, 0, 1))
    return (lam_in, jnp.sum(all_bias, axis=0))


def solution(mesh):
    axes = Mesh(mesh.devices.reshape(8, 8, 4, 2), ("rows",) + MP)
    return jax.shard_map(
        on_device,
        mesh=axes,
        in_specs=(
            P(MP, "rows", None),
            P(None, "rows"),
            P(),
            P("rows", None),
            P("rows"),
            P(None, MP, "rows", None),
            P(None, MP, "rows", None),
            P(),
            P(),
            P(),
            P(None, None, "rows", MP),
            P(None, None, "rows", MP),
        ),
        out_specs=(P(None, "rows", MP), P("rows")),
        check_vma=False,
    )
```

```python
import functools

import jax
import jax.numpy as jnp
from jax import lax
from jax.experimental import pallas as pl
from jax.experimental.pallas import tpu as pltpu
from jax.sharding import Mesh
from jax.sharding import PartitionSpec as P

D = 1024
CH = 4096
TH = 512
TOK = 1024
BLK = 128
NB = 16
SPEC = 8
NHB = 4
NTB = 8
F32 = jnp.float32
BF16 = jnp.bfloat16
I32 = jnp.int32
MP = ("z", "x", "core")
SWAP = [(0, 1), (1, 0)]
VMEM = 32 * 1024 * 1024

PART = 512
CHUNK = 256
STEPS = 4
SHARED = 32
ROWS_DEV = SPEC * SHARED
PACKED = 1032
LAM_TILES = SPEC * (D // 128)
SCALE_ONE = float(2**38)


def pack_codes(parts):
    a, b, c, d = (p.astype(F32).astype(I32) for p in parts)
    return (a & 255) | ((b & 255) << 8) | ((c & 255) << 16) | (d << 24)


def unpack_codes(words, m):
    shifted = words << (24 - 8 * m) if m < 3 else words
    return (shifted >> 24).astype(F32).astype(BF16)


def pack_kernel(start, down_hbm, up_hbm, scale_hbm, out_ref, down_ref, up_ref, scale_ref, sems):
    cut = pl.ds(start, CHUNK)
    copies = [
        pltpu.make_async_copy(down_hbm.at[:, cut], down_ref, sems.at[0]),
        pltpu.make_async_copy(up_hbm.at[cut, :], up_ref, sems.at[1]),
        pltpu.make_async_copy(scale_hbm.at[:, cut], scale_ref, sems.at[2]),
    ]
    for copy in copies:
        copy.start()
    out_ref[1024:1032, :] = jnp.zeros((8, 128), I32)
    copies[0].wait()
    down = pack_codes([down_ref[m * 256 : (m + 1) * 256, :] for m in range(4)])
    for k in range(8):
        rows, cut = slice(k // 2 * 64, (k // 2 + 1) * 64), slice(k % 2 * 128, (k % 2 + 1) * 128)
        out_ref[k * 64 : (k + 1) * 64, :] = down[rows, cut]
    copies[1].wait()
    up = pack_codes([up_ref[m * 64 : (m + 1) * 64, :] for m in range(4)])
    for k in range(8):
        out_ref[512 + k * 64 : 512 + (k + 1) * 64, :] = up[:, k * 128 : (k + 1) * 128]
    copies[2].wait()
    scale = (scale_ref[...] * SCALE_ONE).astype(I32)
    for h in range(2):
        out_ref[1024 + h : 1025 + h, :] = scale[:, h * 128 : (h + 1) * 128]


def pack(chunk, q_down, q_up, up_scale):
    hbm, vmem = pl.BlockSpec(memory_space=pltpu.HBM), pl.BlockSpec(memory_space=pltpu.VMEM)
    return pl.pallas_call(
        functools.partial(pack_kernel, chunk * CHUNK),
        out_shape=jax.ShapeDtypeStruct((PACKED, 128), I32),
        in_specs=[hbm, hbm, hbm],
        out_specs=vmem,
        scratch_shapes=[
            pltpu.VMEM((D, CHUNK), BF16),
            pltpu.VMEM((CHUNK, D), BF16),
            pltpu.VMEM((1, CHUNK), F32),
            pltpu.SemaphoreType.DMA((3,)),
        ],
        compiler_params=pltpu.CompilerParams(vmem_limit_bytes=60 * 1024 * 1024),
        name="pack",
    )(q_down, q_up, up_scale.reshape(1, -1))


def dense_kernel(cells_ref, in_ref, out_ref, dense_in_ref, dense_out_ref):
    dense_in_ref[...] = jnp.zeros_like(dense_in_ref)
    dense_out_ref[...] = jnp.zeros_like(dense_out_ref)
    for b in range(NB):
        h = pl.multiple_of(cells_ref[b] // NTB * BLK, BLK)
        u = pl.multiple_of(cells_ref[b] % NTB * BLK, BLK)
        dense_in_ref[pl.ds(h, BLK), pl.ds(u, BLK)] = in_ref[b]
        dense_out_ref[pl.ds(u, BLK), pl.ds(h, BLK)] = out_ref[b]


def dense_blocks(cells, in_blocks, out_blocks):
    return pl.pallas_call(
        dense_kernel,
        out_shape=(
            jax.ShapeDtypeStruct((TH, TOK), BF16),
            jax.ShapeDtypeStruct((TOK, TH), BF16),
        ),
        in_specs=[
            pl.BlockSpec(memory_space=pltpu.SMEM),
            pl.BlockSpec(memory_space=pltpu.VMEM),
            pl.BlockSpec(memory_space=pltpu.VMEM),
        ],
        out_specs=(
            pl.BlockSpec(memory_space=pltpu.VMEM),
            pl.BlockSpec(memory_space=pltpu.VMEM),
        ),
        compiler_params=pltpu.CompilerParams(vmem_limit_bytes=VMEM),
        name="dense",
    )(cells, in_blocks, out_blocks)


def relaxed(pre, lower, upper, icpt_low, icpt_high):
    pos = jnp.maximum(pre, 0.0)
    neg = jnp.minimum(pre, 0.0)
    mid = pos * lower.astype(F32) + neg * upper.astype(F32)
    return mid, pos * icpt_low.astype(F32) + neg * icpt_high.astype(F32)


def share_kernel(core_ref, row_ref, lam_ref, slopes_ref, icpt_ref, *out_refs):
    for r in range(SPEC):
        for k in range(D // 128):
            tile = lam_ref[r, :, k * 128 : (k + 1) * 128]
            for out_ref in out_refs:
                out_ref[r * (D // 128) + k] = tile
    row = row_ref[0]
    for k, out_ref in enumerate(out_refs):
        core = core_ref[0] ^ k
        for j in range(STEPS):
            if j < STEPS - 1:
                owner = row + (2 * core - 1) * (j + 1)
                cuts = [(owner, 0), (owner, 1)]
            else:
                cuts = [(row + STEPS, core), (row, core)]
            for h, (owner, chunk) in enumerate(cuts):
                start = pl.multiple_of((owner & 7) * PART + chunk * CHUNK, CHUNK)
                for kind in range(4):
                    ref = slopes_ref if kind < 2 else icpt_ref
                    values = ref[kind % 2, :, pl.ds(start, CHUNK)]
                    tile = LAM_TILES + (j * 4 + kind) * 4 + h * 2
                    out_ref[tile] = values[:, 0:128]
                    out_ref[tile + 1] = values[:, 128:256]


def share(core, row, by_row, slopes, icpt):
    tiles = LAM_TILES + 4 * STEPS * 4
    return pl.pallas_call(
        share_kernel,
        out_shape=(jax.ShapeDtypeStruct((tiles, 16, 128), BF16),) * 2,
        in_specs=[pl.BlockSpec(memory_space=pltpu.SMEM)] * 2
        + [pl.BlockSpec(memory_space=pltpu.VMEM)] * 3,
        compiler_params=pltpu.CompilerParams(vmem_limit_bytes=60 * 1024 * 1024),
        name="share",
    )(core, row, by_row, slopes, icpt)


def channel_kernel(step, *refs):
    first, last = step == 0, step == STEPS - 1
    core_ref, *words, refs = refs[0], refs[1], refs[2], refs[3:]
    if first:
        down_scale_ref, *team, acc_ref, bias_ref, scaled_ref, bounds_ref, down, up = refs
        for k, got_ref in enumerate(team):
            start = (core_ref[0] ^ k) * 16
            for r in range(SPEC):
                rows = pl.ds(pl.multiple_of(r * SHARED + start, 16), 16)
                for c in range(D // 128):
                    cut = slice(c * 128, (c + 1) * 128)
                    lam = got_ref[r * (D // 128) + c].astype(F32)
                    scaled_ref[rows, cut] = (lam * down_scale_ref[:, cut]).astype(BF16)
                    acc_ref[rows, cut] = 0.5 * lam
            rows = pl.ds(pl.multiple_of(start, 16), 16)
            for i in range(STEPS * 4):
                for h in range(4):
                    tile = got_ref[LAM_TILES + i * 4 + h]
                    bounds_ref[i // 4, i % 4, rows, h * 128 : (h + 1) * 128] = tile
        acc_in, bias_in = acc_ref, None
    else:
        if last:
            *own_words, refs = refs[0], refs[1], refs[2:]
        scaled_ref, bounds_ref, acc_in, bias_in, *outs, down, up = refs
    words = [w[...] for w in words]
    if last:
        own_core = core_ref[0] == 0
        words = [
            jnp.where(own_core, words[0], words[1]),
            jnp.where(own_core, own_words[0][...], own_words[1][...]),
        ]
    for h, chunk in enumerate(words):
        for m in range(4):
            for k in range(8):
                rows = m * 256 + k // 2 * 64
                cut = h * CHUNK + k % 2 * 128
                codes = unpack_codes(chunk[k * 64 : (k + 1) * 64], m)
                down[rows : rows + 64, cut : cut + 128] = codes
                rows = h * CHUNK + m * 64
                codes = unpack_codes(chunk[512 + k * 64 : 512 + (k + 1) * 64], m)
                up[rows : rows + 64, k * 128 : (k + 1) * 128] = codes
    scale = [chunk[1024 + h : 1025 + h] for chunk in words for h in range(2)]
    scale = jnp.concatenate(scale, axis=1).astype(F32) * (1.0 / SCALE_ONE)
    pre = jnp.dot(scaled_ref[...], down[...], preferred_element_type=F32)
    pre = pre.reshape(SPEC, SHARED, PART)
    mid, terms = relaxed(pre, *(bounds_ref[step, kind] for kind in range(4)))
    terms = jnp.sum(terms.reshape(SPEC, SHARED // 8, 8, PART), axis=1)
    bias = sum(terms[:, :, k * 128 : (k + 1) * 128] for k in range(PART // 128))
    weighted = (mid.reshape(ROWS_DEV, PART) * scale).astype(BF16)
    part = jnp.dot(weighted, up[...], preferred_element_type=F32)
    total = acc_in[...] + part
    if not first:
        bias = bias + bias_in[...]
    if last:
        keep_ref, send_ref, bias_ref = outs
        own = core_ref[0] == 0
        turned = total.T.reshape(32, 2, 16, ROWS_DEV)
        keep_ref[...] = jnp.where(own, turned[:, 0], turned[:, 1])
        send_ref[...] = jnp.where(own, turned[:, 1], turned[:, 0]).astype(BF16)
    else:
        if not first:
            acc_ref, bias_ref = outs
        acc_ref[...] = total
    bias_ref[...] = bias


def channel_part(step, core, *rest):
    acc_shape = jax.ShapeDtypeStruct((ROWS_DEV, D), F32)
    bias_shape = jax.ShapeDtypeStruct((SPEC, 8, 128), F32)
    operands = [core, *rest]
    aliases = {}
    if step == 0:
        scaled_shape = jax.ShapeDtypeStruct((ROWS_DEV, D), BF16)
        bounds_shape = jax.ShapeDtypeStruct((STEPS, 4, SHARED, PART), BF16)
        out_shape = (acc_shape, bias_shape, scaled_shape, bounds_shape)
    elif step == STEPS - 1:
        out_shape = (
            jax.ShapeDtypeStruct((32, 16, ROWS_DEV), F32),
            jax.ShapeDtypeStruct((32, 16, ROWS_DEV), BF16),
            bias_shape,
        )
    else:
        out_shape = (acc_shape, bias_shape)
        aliases = {len(operands) - 2: 0, len(operands) - 1: 1}
    smem, vmem = pl.BlockSpec(memory_space=pltpu.SMEM), pl.BlockSpec(memory_space=pltpu.VMEM)
    return pl.pallas_call(
        functools.partial(channel_kernel, step),
        out_shape=out_shape,
        in_specs=[smem] + [vmem] * (len(operands) - 1),
        out_specs=(vmem,) * len(out_shape),
        scratch_shapes=[pltpu.VMEM((D, PART), BF16), pltpu.VMEM((PART, D), BF16)],
        input_output_aliases=aliases,
        compiler_params=pltpu.CompilerParams(vmem_limit_bytes=VMEM),
        cost_estimate=pl.CostEstimate(
            flops=4 * ROWS_DEV * PART * D,
            bytes_accessed=2 * PACKED * 128 * 4 + 3 * ROWS_DEV * D * 4,
            transcendentals=0,
        ),
        name="channel",
    )(*operands)


def token_kernel(
    got_ref, dense_ref, slopes_ref, icpt_ref, chan_bias_ref, columns_ref, mid_ref, bias_ref
):
    lane = lax.broadcasted_iota(I32, (16, 128), 1) // 32
    for u in range(NTB):
        for a in range(2):
            v = [got_ref[4 * u + p, :, a * 128 : (a + 1) * 128].astype(F32) for p in range(4)]
            for bit in (1, 2):
                low = (lane & bit) == 0
                new = list(v)
                for p in range(4):
                    if p & bit == 0:
                        q = p + bit
                        new[p] = jnp.where(low, v[p], pltpu.roll(v[q], 32 * bit, 1))
                        new[q] = jnp.where(low, pltpu.roll(v[p], 128 - 32 * bit, 1), v[q])
                v = new
            for q in range(4):
                r = 4 * a + q
                columns_ref[r * 16 : (r + 1) * 16, u * 128 : (u + 1) * 128] = v[q].astype(BF16)
    pre = jnp.dot(columns_ref[...], dense_ref[...], preferred_element_type=F32)
    pre = pre.reshape(SPEC, 16, TH)
    mid, terms = relaxed(pre, slopes_ref[0], slopes_ref[1], icpt_ref[0], icpt_ref[1])
    mid_ref[...] = mid.reshape(SPEC * 16, TH).astype(BF16)
    terms = terms[:, 0:8, :] + terms[:, 8:16, :]
    terms = sum(terms[:, :, k * 128 : (k + 1) * 128] for k in range(NHB)) + chan_bias_ref[...]
    by_row = jnp.sum(jnp.sum(terms, axis=1), axis=1, keepdims=True)
    row = lax.broadcasted_iota(I32, (SPEC, 128), 0)
    lane = lax.broadcasted_iota(I32, (SPEC, 128), 1)
    line = jnp.sum(jnp.where(row == lane, by_row, 0.0), axis=0, keepdims=True)
    bias_ref[...] = jnp.broadcast_to(line[None], bias_ref.shape)


def token_mlp(got, dense_out, slopes, icpt, chan_bias):
    return pl.pallas_call(
        token_kernel,
        out_shape=(
            jax.ShapeDtypeStruct((SPEC * 16, TOK), BF16),
            jax.ShapeDtypeStruct((SPEC * 16, TH), BF16),
            jax.ShapeDtypeStruct((64, 1, 128), F32),
        ),
        compiler_params=pltpu.CompilerParams(vmem_limit_bytes=VMEM),
        name="token",
    )(got, dense_out, slopes, icpt, chan_bias)


def back_kernel(columns_ref, mid_ref, dense_ref, out_ref):
    back = jnp.dot(mid_ref[...], dense_ref[...], preferred_element_type=F32)
    out_ref[...] = (columns_ref[...].astype(F32) + back).astype(BF16)


def token_back(columns, mid, dense_in):
    return pl.pallas_call(
        back_kernel,
        out_shape=jax.ShapeDtypeStruct((SPEC * 16, TOK), BF16),
        compiler_params=pltpu.CompilerParams(vmem_limit_bytes=VMEM),
        name="back",
    )(columns, mid, dense_in)


def on_device(
    lam_out,
    q_down,
    down_scale,
    q_up,
    up_scale,
    chan_slopes,
    chan_icpt,
    tok_in_blocks,
    tok_out_blocks,
    block_cells,
    tok_slopes,
    tok_icpt,
):
    core = lax.axis_index("core").astype(I32).reshape(1)
    row = lax.axis_index("rows").astype(I32).reshape(1)
    tok_dev = lam_out.shape[0]
    slices = lax.axis_size("rows")
    ahead = [(i * 2, (i + 1) % slices * 2) for i in range(slices)]
    behind = [(i * 2 + 1, (i - 1) % slices * 2 + 1) for i in range(slices)]

    def forward(words, pairs):
        return tuple(lax.ppermute(w, ("rows", "core"), pairs) for w in words)

    own = tuple(pack(chunk, q_down, q_up, up_scale) for chunk in range(2))
    first = forward(own, ahead + behind)
    _, lam, *bounds = lax.optimization_barrier((own, lam_out, chan_slopes, chan_icpt))
    keep_part, send_part = share(
        core, row, jnp.swapaxes(lam, 0, 1), *(b.reshape(2, tok_dev, CH) for b in bounds)
    )
    words, send_part = lax.optimization_barrier((first[0], send_part))
    second = forward((words, first[1]), ahead + behind)
    other_part = lax.ppermute(send_part, "core", SWAP)
    words, other_part = lax.optimization_barrier((second[0], other_part))
    third = forward((words, second[1]), ahead + behind)
    carried = channel_part(0, core, *first, down_scale.reshape(1, D), keep_part, other_part)
    acc, chan_bias, *given = carried
    acc, chan_bias = channel_part(1, core, *second, *given, acc, chan_bias)
    words, acc = lax.optimization_barrier((third[0], acc))
    far = forward((words,), ahead) + forward(third[1:], behind)

    dense_in, dense_out = dense_blocks(block_cells, tok_in_blocks, tok_out_blocks)
    slopes = jnp.transpose(tok_slopes, (0, 2, 3, 1)).reshape(2, 16, TH)
    icpt = jnp.transpose(tok_icpt, (0, 2, 3, 1)).reshape(2, 16, TH)

    acc, chan_bias = channel_part(2, core, *third, *given, acc, chan_bias)
    keep, send, chan_bias = channel_part(3, core, *far, *own, *given, acc, chan_bias)
    summed = (keep + lax.ppermute(send, "core", SWAP).astype(F32)).astype(BF16)
    got = lax.all_to_all(summed, ("z", "x"), 0, 0, tiled=True)
    columns, mid, own_bias = token_mlp(got, dense_out, slopes, icpt, chan_bias)
    all_bias = lax.all_to_all(own_bias, MP, 0, 0, tiled=True)
    lam_in = token_back(columns, mid, dense_in)
    lam_in = jnp.transpose(lam_in.reshape(SPEC, 16, TOK), (2, 0, 1))
    return (lam_in, jnp.sum(all_bias, axis=(0, 1))[:SPEC])


def solution(mesh):
    axes = Mesh(mesh.devices.reshape(8, 8, 4, 2), ("rows",) + MP)
    return jax.shard_map(
        on_device,
        mesh=axes,
        in_specs=(
            P(MP, "rows", None),
            P(None, "rows"),
            P(),
            P("rows", None),
            P("rows"),
            P(None, MP, "rows", None),
            P(None, MP, "rows", None),
            P(),
            P(),
            P(),
            P(None, None, "rows", MP),
            P(None, None, "rows", MP),
        ),
        out_specs=(P(None, "rows", MP), P("rows")),
        check_vma=False,
    )
```

```python
import functools

import jax
import jax.numpy as jnp
from jax import lax
from jax.experimental import pallas as pl
from jax.experimental.pallas import tpu as pltpu
from jax.sharding import Mesh
from jax.sharding import PartitionSpec as P

D = 1024
CH = 4096
TH = 512
TOK = 1024
BLK = 128
NB = 16
SPEC = 8
NHB = 4
NTB = 8
F32 = jnp.float32
BF16 = jnp.bfloat16
I32 = jnp.int32
MP = ("z", "x", "core")
SWAP = [(0, 1), (1, 0)]
VMEM = 32 * 1024 * 1024

PART = 512
CHUNK = 256
STEPS = 4
SHARED = 32
ROWS_DEV = SPEC * SHARED
PACKED = 1032
LAM_TILES = SPEC * (D // 128)
SCALE_ONE = float(2**38)


def pack_codes(parts):
    a, b, c, d = (p.astype(F32).astype(I32) for p in parts)
    return (a & 255) | ((b & 255) << 8) | ((c & 255) << 16) | (d << 24)


def unpack_codes(words, m):
    shifted = words << (24 - 8 * m) if m < 3 else words
    return (shifted >> 24).astype(F32).astype(BF16)


def pack_kernel(chain, core_ref, down_hbm, up_hbm, scale_hbm, out_ref, down_ref, up_ref, scale_ref, sems):
    cut = pl.ds(pl.multiple_of((core_ref[0] ^ chain) * CHUNK, CHUNK), CHUNK)
    copies = [
        pltpu.make_async_copy(down_hbm.at[:, cut], down_ref, sems.at[0]),
        pltpu.make_async_copy(up_hbm.at[cut, :], up_ref, sems.at[1]),
        pltpu.make_async_copy(scale_hbm.at[:, cut], scale_ref, sems.at[2]),
    ]
    for copy in copies:
        copy.start()
    out_ref[1024:1032, :] = jnp.zeros((8, 128), I32)
    copies[0].wait()
    down = pack_codes([down_ref[m * 256 : (m + 1) * 256, :] for m in range(4)])
    for k in range(8):
        rows, cut = slice(k // 2 * 64, (k // 2 + 1) * 64), slice(k % 2 * 128, (k % 2 + 1) * 128)
        out_ref[k * 64 : (k + 1) * 64, :] = down[rows, cut]
    copies[1].wait()
    up = pack_codes([up_ref[m * 64 : (m + 1) * 64, :] for m in range(4)])
    for k in range(8):
        out_ref[512 + k * 64 : 512 + (k + 1) * 64, :] = up[:, k * 128 : (k + 1) * 128]
    copies[2].wait()
    scale = (scale_ref[...] * SCALE_ONE).astype(I32)
    for h in range(2):
        out_ref[1024 + h : 1025 + h, :] = scale[:, h * 128 : (h + 1) * 128]


def pack(chain, core, q_down, q_up, up_scale):
    smem, hbm, vmem = (
        pl.BlockSpec(memory_space=space) for space in (pltpu.SMEM, pltpu.HBM, pltpu.VMEM)
    )
    return pl.pallas_call(
        functools.partial(pack_kernel, chain),
        out_shape=jax.ShapeDtypeStruct((PACKED, 128), I32),
        in_specs=[smem, hbm, hbm, hbm],
        out_specs=vmem,
        scratch_shapes=[
            pltpu.VMEM((D, CHUNK), BF16),
            pltpu.VMEM((CHUNK, D), BF16),
            pltpu.VMEM((1, CHUNK), F32),
            pltpu.SemaphoreType.DMA((3,)),
        ],
        compiler_params=pltpu.CompilerParams(vmem_limit_bytes=60 * 1024 * 1024),
        name="pack",
    )(core, q_down, q_up, up_scale.reshape(1, -1))


def dense_kernel(cells_ref, in_ref, out_ref, dense_in_ref, dense_out_ref):
    dense_in_ref[...] = jnp.zeros_like(dense_in_ref)
    dense_out_ref[...] = jnp.zeros_like(dense_out_ref)
    for b in range(NB):
        h = pl.multiple_of(cells_ref[b] // NTB * BLK, BLK)
        u = pl.multiple_of(cells_ref[b] % NTB * BLK, BLK)
        dense_in_ref[pl.ds(h, BLK), pl.ds(u, BLK)] = in_ref[b]
        dense_out_ref[pl.ds(u, BLK), pl.ds(h, BLK)] = out_ref[b]


def dense_blocks(cells, in_blocks, out_blocks):
    return pl.pallas_call(
        dense_kernel,
        out_shape=(
            jax.ShapeDtypeStruct((TH, TOK), BF16),
            jax.ShapeDtypeStruct((TOK, TH), BF16),
        ),
        in_specs=[
            pl.BlockSpec(memory_space=pltpu.SMEM),
            pl.BlockSpec(memory_space=pltpu.VMEM),
            pl.BlockSpec(memory_space=pltpu.VMEM),
        ],
        out_specs=(
            pl.BlockSpec(memory_space=pltpu.VMEM),
            pl.BlockSpec(memory_space=pltpu.VMEM),
        ),
        compiler_params=pltpu.CompilerParams(vmem_limit_bytes=VMEM),
        name="dense",
    )(cells, in_blocks, out_blocks)


def relaxed(pre, lower, upper, icpt_low, icpt_high):
    pos = jnp.maximum(pre, 0.0)
    neg = jnp.minimum(pre, 0.0)
    mid = pos * lower.astype(F32) + neg * upper.astype(F32)
    return mid, pos * icpt_low.astype(F32) + neg * icpt_high.astype(F32)


def share_kernel(core_ref, row_ref, lam_ref, slopes_ref, icpt_ref, *out_refs):
    for r in range(SPEC):
        for k in range(D // 128):
            tile = lam_ref[r, :, k * 128 : (k + 1) * 128]
            for out_ref in out_refs:
                out_ref[r * (D // 128) + k] = tile
    row = row_ref[0]
    for k, out_ref in enumerate(out_refs):
        core = core_ref[0] ^ k
        for j in range(STEPS):
            if j < STEPS - 1:
                owner = row + (2 * core - 1) * (j + 1)
                cuts = [(owner, core), (owner, 1 - core)]
            else:
                cuts = [(row + STEPS, core), (row, core)]
            for h, (owner, chunk) in enumerate(cuts):
                start = pl.multiple_of((owner & 7) * PART + chunk * CHUNK, CHUNK)
                for kind in range(4):
                    ref = slopes_ref if kind < 2 else icpt_ref
                    values = ref[kind % 2, :, pl.ds(start, CHUNK)]
                    tile = LAM_TILES + (j * 4 + kind) * 4 + h * 2
                    out_ref[tile] = values[:, 0:128]
                    out_ref[tile + 1] = values[:, 128:256]


def share(core, row, by_row, slopes, icpt):
    tiles = LAM_TILES + 4 * STEPS * 4
    return pl.pallas_call(
        share_kernel,
        out_shape=(jax.ShapeDtypeStruct((tiles, 16, 128), BF16),) * 2,
        in_specs=[pl.BlockSpec(memory_space=pltpu.SMEM)] * 2
        + [pl.BlockSpec(memory_space=pltpu.VMEM)] * 3,
        compiler_params=pltpu.CompilerParams(vmem_limit_bytes=60 * 1024 * 1024),
        name="share",
    )(core, row, by_row, slopes, icpt)


def channel_kernel(step, *refs):
    first, last = step == 0, step == STEPS - 1
    core_ref, *words, refs = refs[0], refs[1], refs[2], refs[3:]
    if first:
        down_scale_ref, *team, acc_ref, bias_ref, scaled_ref, bounds_ref, down, up = refs
        for k, got_ref in enumerate(team):
            start = (core_ref[0] ^ k) * 16
            for r in range(SPEC):
                rows = pl.ds(pl.multiple_of(r * SHARED + start, 16), 16)
                for c in range(D // 128):
                    cut = slice(c * 128, (c + 1) * 128)
                    lam = got_ref[r * (D // 128) + c].astype(F32)
                    scaled_ref[rows, cut] = (lam * down_scale_ref[:, cut]).astype(BF16)
                    acc_ref[rows, cut] = 0.5 * lam
            rows = pl.ds(pl.multiple_of(start, 16), 16)
            for i in range(STEPS * 4):
                for h in range(4):
                    tile = got_ref[LAM_TILES + i * 4 + h]
                    bounds_ref[i // 4, i % 4, rows, h * 128 : (h + 1) * 128] = tile
        acc_in, bias_in = acc_ref, None
    else:
        scaled_ref, bounds_ref, acc_in, bias_in, *outs, down, up = refs
    words = [w[...] for w in words]
    for h, chunk in enumerate(words):
        for m in range(4):
            for k in range(8):
                rows = m * 256 + k // 2 * 64
                cut = h * CHUNK + k % 2 * 128
                codes = unpack_codes(chunk[k * 64 : (k + 1) * 64], m)
                down[rows : rows + 64, cut : cut + 128] = codes
                rows = h * CHUNK + m * 64
                codes = unpack_codes(chunk[512 + k * 64 : 512 + (k + 1) * 64], m)
                up[rows : rows + 64, k * 128 : (k + 1) * 128] = codes
    scale = [chunk[1024 + h : 1025 + h] for chunk in words for h in range(2)]
    scale = jnp.concatenate(scale, axis=1).astype(F32) * (1.0 / SCALE_ONE)
    pre = jnp.dot(scaled_ref[...], down[...], preferred_element_type=F32)
    pre = pre.reshape(SPEC, SHARED, PART)
    mid, terms = relaxed(pre, *(bounds_ref[step, kind] for kind in range(4)))
    terms = jnp.sum(terms.reshape(SPEC, SHARED // 8, 8, PART), axis=1)
    bias = sum(terms[:, :, k * 128 : (k + 1) * 128] for k in range(PART // 128))
    weighted = (mid.reshape(ROWS_DEV, PART) * scale).astype(BF16)
    part = jnp.dot(weighted, up[...], preferred_element_type=F32)
    total = acc_in[...] + part
    if not first:
        bias = bias + bias_in[...]
    if last:
        keep_ref, send_ref, bias_ref = outs
        own = core_ref[0] == 0
        turned = total.T.reshape(32, 2, 16, ROWS_DEV)
        keep_ref[...] = jnp.where(own, turned[:, 0], turned[:, 1])
        send_ref[...] = jnp.where(own, turned[:, 1], turned[:, 0]).astype(BF16)
    else:
        if not first:
            acc_ref, bias_ref = outs
        acc_ref[...] = total
    bias_ref[...] = bias


def channel_part(step, core, *rest):
    acc_shape = jax.ShapeDtypeStruct((ROWS_DEV, D), F32)
    bias_shape = jax.ShapeDtypeStruct((SPEC, 8, 128), F32)
    operands = [core, *rest]
    aliases = {}
    if step == 0:
        scaled_shape = jax.ShapeDtypeStruct((ROWS_DEV, D), BF16)
        bounds_shape = jax.ShapeDtypeStruct((STEPS, 4, SHARED, PART), BF16)
        out_shape = (acc_shape, bias_shape, scaled_shape, bounds_shape)
    elif step == STEPS - 1:
        out_shape = (
            jax.ShapeDtypeStruct((32, 16, ROWS_DEV), F32),
            jax.ShapeDtypeStruct((32, 16, ROWS_DEV), BF16),
            bias_shape,
        )
    else:
        out_shape = (acc_shape, bias_shape)
        aliases = {len(operands) - 2: 0, len(operands) - 1: 1}
    smem, vmem = pl.BlockSpec(memory_space=pltpu.SMEM), pl.BlockSpec(memory_space=pltpu.VMEM)
    return pl.pallas_call(
        functools.partial(channel_kernel, step),
        out_shape=out_shape,
        in_specs=[smem] + [vmem] * (len(operands) - 1),
        out_specs=(vmem,) * len(out_shape),
        scratch_shapes=[pltpu.VMEM((D, PART), BF16), pltpu.VMEM((PART, D), BF16)],
        input_output_aliases=aliases,
        compiler_params=pltpu.CompilerParams(vmem_limit_bytes=VMEM),
        cost_estimate=pl.CostEstimate(
            flops=4 * ROWS_DEV * PART * D,
            bytes_accessed=2 * PACKED * 128 * 4 + 3 * ROWS_DEV * D * 4,
            transcendentals=0,
        ),
        name="channel",
    )(*operands)


def token_kernel(
    got_ref, dense_ref, slopes_ref, icpt_ref, chan_bias_ref, columns_ref, mid_ref, bias_ref
):
    lane = lax.broadcasted_iota(I32, (16, 128), 1) // 32
    for u in range(NTB):
        for a in range(2):
            v = [got_ref[4 * u + p, :, a * 128 : (a + 1) * 128].astype(F32) for p in range(4)]
            for bit in (1, 2):
                low = (lane & bit) == 0
                new = list(v)
                for p in range(4):
                    if p & bit == 0:
                        q = p + bit
                        new[p] = jnp.where(low, v[p], pltpu.roll(v[q], 32 * bit, 1))
                        new[q] = jnp.where(low, pltpu.roll(v[p], 128 - 32 * bit, 1), v[q])
                v = new
            for q in range(4):
                r = 4 * a + q
                columns_ref[r * 16 : (r + 1) * 16, u * 128 : (u + 1) * 128] = v[q].astype(BF16)
    pre = jnp.dot(columns_ref[...], dense_ref[...], preferred_element_type=F32)
    pre = pre.reshape(SPEC, 16, TH)
    mid, terms = relaxed(pre, slopes_ref[0], slopes_ref[1], icpt_ref[0], icpt_ref[1])
    mid_ref[...] = mid.reshape(SPEC * 16, TH).astype(BF16)
    terms = terms[:, 0:8, :] + terms[:, 8:16, :]
    terms = sum(terms[:, :, k * 128 : (k + 1) * 128] for k in range(NHB)) + chan_bias_ref[...]
    by_row = jnp.sum(jnp.sum(terms, axis=1), axis=1, keepdims=True)
    row = lax.broadcasted_iota(I32, (SPEC, 128), 0)
    lane = lax.broadcasted_iota(I32, (SPEC, 128), 1)
    line = jnp.sum(jnp.where(row == lane, by_row, 0.0), axis=0, keepdims=True)
    bias_ref[...] = jnp.broadcast_to(line[None], bias_ref.shape)


def token_mlp(got, dense_out, slopes, icpt, chan_bias):
    return pl.pallas_call(
        token_kernel,
        out_shape=(
            jax.ShapeDtypeStruct((SPEC * 16, TOK), BF16),
            jax.ShapeDtypeStruct((SPEC * 16, TH), BF16),
            jax.ShapeDtypeStruct((64, 1, 128), F32),
        ),
        compiler_params=pltpu.CompilerParams(vmem_limit_bytes=VMEM),
        name="token",
    )(got, dense_out, slopes, icpt, chan_bias)


def back_kernel(columns_ref, mid_ref, dense_ref, out_ref):
    back = jnp.dot(mid_ref[...], dense_ref[...], preferred_element_type=F32)
    out_ref[...] = (columns_ref[...].astype(F32) + back).astype(BF16)


def token_back(columns, mid, dense_in):
    return pl.pallas_call(
        back_kernel,
        out_shape=jax.ShapeDtypeStruct((SPEC * 16, TOK), BF16),
        compiler_params=pltpu.CompilerParams(vmem_limit_bytes=VMEM),
        name="back",
    )(columns, mid, dense_in)


def on_device(
    lam_out,
    q_down,
    down_scale,
    q_up,
    up_scale,
    chan_slopes,
    chan_icpt,
    tok_in_blocks,
    tok_out_blocks,
    block_cells,
    tok_slopes,
    tok_icpt,
):
    core = lax.axis_index("core").astype(I32).reshape(1)
    row = lax.axis_index("rows").astype(I32).reshape(1)
    tok_dev = lam_out.shape[0]
    slices = lax.axis_size("rows")
    ahead = [(i * 2, (i + 1) % slices * 2) for i in range(slices)]
    behind = [(i * 2 + 1, (i - 1) % slices * 2 + 1) for i in range(slices)]

    def forward(words, pairs):
        return tuple(lax.ppermute(w, ("rows", "core"), pairs) for w in words)

    own = tuple(pack(chain, core, q_down, q_up, up_scale) for chain in range(2))
    first = forward(own, ahead + behind)
    _, lam, *bounds = lax.optimization_barrier((own, lam_out, chan_slopes, chan_icpt))
    keep_part, send_part = share(
        core, row, jnp.swapaxes(lam, 0, 1), *(b.reshape(2, tok_dev, CH) for b in bounds)
    )
    words, send_part = lax.optimization_barrier((first[0], send_part))
    second = forward((words, first[1]), ahead + behind)
    other_part = lax.ppermute(send_part, "core", SWAP)
    words, other_part = lax.optimization_barrier((second[0], other_part))
    third = forward((words, second[1]), ahead + behind)
    carried = channel_part(0, core, *first, down_scale.reshape(1, D), keep_part, other_part)
    acc, chan_bias, *given = carried
    acc, chan_bias = channel_part(1, core, *second, *given, acc, chan_bias)
    words, acc = lax.optimization_barrier((third[0], acc))
    far = forward((words,), ahead + behind)

    dense_in, dense_out = dense_blocks(block_cells, tok_in_blocks, tok_out_blocks)
    slopes = jnp.transpose(tok_slopes, (0, 2, 3, 1)).reshape(2, 16, TH)
    icpt = jnp.transpose(tok_icpt, (0, 2, 3, 1)).reshape(2, 16, TH)

    acc, chan_bias = channel_part(2, core, *third, *given, acc, chan_bias)
    keep, send, chan_bias = channel_part(3, core, *far, own[0], *given, acc, chan_bias)
    summed = (keep + lax.ppermute(send, "core", SWAP).astype(F32)).astype(BF16)
    got = lax.all_to_all(summed, ("z", "x"), 0, 0, tiled=True)
    columns, mid, own_bias = token_mlp(got, dense_out, slopes, icpt, chan_bias)
    all_bias = lax.all_to_all(own_bias, MP, 0, 0, tiled=True)
    lam_in = token_back(columns, mid, dense_in)
    lam_in = jnp.transpose(lam_in.reshape(SPEC, 16, TOK), (2, 0, 1))
    return (lam_in, jnp.sum(all_bias, axis=(0, 1))[:SPEC])


def solution(mesh):
    axes = Mesh(mesh.devices.reshape(8, 8, 4, 2), ("rows",) + MP)
    return jax.shard_map(
        on_device,
        mesh=axes,
        in_specs=(
            P(MP, "rows", None),
            P(None, "rows"),
            P(),
            P("rows", None),
            P("rows"),
            P(None, MP, "rows", None),
            P(None, MP, "rows", None),
            P(),
            P(),
            P(),
            P(None, None, "rows", MP),
            P(None, None, "rows", MP),
        ),
        out_specs=(P(None, "rows", MP), P("rows")),
        check_vma=False,
    )
```

```python
import functools

import jax
import jax.numpy as jnp
from jax import lax
from jax.experimental import pallas as pl
from jax.experimental.pallas import tpu as pltpu
from jax.sharding import Mesh
from jax.sharding import PartitionSpec as P

D = 1024
CH = 4096
TH = 512
TOK = 1024
BLK = 128
NB = 16
SPEC = 8
NHB = 4
NTB = 8
F32 = jnp.float32
BF16 = jnp.bfloat16
I32 = jnp.int32
MP = ("z", "x", "core")
SWAP = [(0, 1), (1, 0)]
VMEM = 32 * 1024 * 1024

PART = 512
CHUNK = 256
STEPS = 4
SHARED = 32
ROWS_DEV = SPEC * SHARED
PACKED = 1032
LAM_TILES = SPEC * (D // 128)
SCALE_ONE = float(2**38)


def pack_codes(parts):
    a, b, c, d = (p.astype(F32).astype(I32) for p in parts)
    return (a & 255) | ((b & 255) << 8) | ((c & 255) << 16) | (d << 24)


def unpack_codes(words, m):
    shifted = words << (24 - 8 * m) if m < 3 else words
    return (shifted >> 24).astype(F32).astype(BF16)


def pack_kernel(chain, core_ref, down_hbm, up_hbm, scale_hbm, out_ref, down_ref, up_ref, scale_ref, sems):
    cut = pl.ds(pl.multiple_of((core_ref[0] ^ chain) * CHUNK, CHUNK), CHUNK)
    copies = [
        pltpu.make_async_copy(down_hbm.at[:, cut], down_ref, sems.at[0]),
        pltpu.make_async_copy(up_hbm.at[cut, :], up_ref, sems.at[1]),
        pltpu.make_async_copy(scale_hbm.at[:, cut], scale_ref, sems.at[2]),
    ]
    for copy in copies:
        copy.start()
    out_ref[1024:1032, :] = jnp.zeros((8, 128), I32)
    copies[0].wait()
    down = pack_codes([down_ref[m * 256 : (m + 1) * 256, :] for m in range(4)])
    for k in range(8):
        rows, cut = slice(k // 2 * 64, (k // 2 + 1) * 64), slice(k % 2 * 128, (k % 2 + 1) * 128)
        out_ref[k * 64 : (k + 1) * 64, :] = down[rows, cut]
    copies[1].wait()
    up = pack_codes([up_ref[m * 64 : (m + 1) * 64, :] for m in range(4)])
    for k in range(8):
        out_ref[512 + k * 64 : 512 + (k + 1) * 64, :] = up[:, k * 128 : (k + 1) * 128]
    copies[2].wait()
    scale = (scale_ref[...] * SCALE_ONE).astype(I32)
    for h in range(2):
        out_ref[1024 + h : 1025 + h, :] = scale[:, h * 128 : (h + 1) * 128]


def pack(chain, core, q_down, q_up, up_scale):
    smem, hbm, vmem = (
        pl.BlockSpec(memory_space=space) for space in (pltpu.SMEM, pltpu.HBM, pltpu.VMEM)
    )
    return pl.pallas_call(
        functools.partial(pack_kernel, chain),
        out_shape=jax.ShapeDtypeStruct((PACKED, 128), I32),
        in_specs=[smem, hbm, hbm, hbm],
        out_specs=vmem,
        scratch_shapes=[
            pltpu.VMEM((D, CHUNK), BF16),
            pltpu.VMEM((CHUNK, D), BF16),
            pltpu.VMEM((1, CHUNK), F32),
            pltpu.SemaphoreType.DMA((3,)),
        ],
        compiler_params=pltpu.CompilerParams(vmem_limit_bytes=60 * 1024 * 1024),
        name="pack",
    )(core, q_down, q_up, up_scale.reshape(1, -1))


def dense_kernel(cells_ref, in_ref, out_ref, dense_in_ref, dense_out_ref):
    dense_in_ref[...] = jnp.zeros_like(dense_in_ref)
    dense_out_ref[...] = jnp.zeros_like(dense_out_ref)
    for b in range(NB):
        h = pl.multiple_of(cells_ref[b] // NTB * BLK, BLK)
        u = pl.multiple_of(cells_ref[b] % NTB * BLK, BLK)
        dense_in_ref[pl.ds(h, BLK), pl.ds(u, BLK)] = in_ref[b]
        dense_out_ref[pl.ds(u, BLK), pl.ds(h, BLK)] = out_ref[b]


def dense_blocks(cells, in_blocks, out_blocks):
    return pl.pallas_call(
        dense_kernel,
        out_shape=(
            jax.ShapeDtypeStruct((TH, TOK), BF16),
            jax.ShapeDtypeStruct((TOK, TH), BF16),
        ),
        in_specs=[
            pl.BlockSpec(memory_space=pltpu.SMEM),
            pl.BlockSpec(memory_space=pltpu.VMEM),
            pl.BlockSpec(memory_space=pltpu.VMEM),
        ],
        out_specs=(
            pl.BlockSpec(memory_space=pltpu.VMEM),
            pl.BlockSpec(memory_space=pltpu.VMEM),
        ),
        compiler_params=pltpu.CompilerParams(vmem_limit_bytes=VMEM),
        name="dense",
    )(cells, in_blocks, out_blocks)


def relaxed(pre, lower, upper, icpt_low, icpt_high):
    pos = jnp.maximum(pre, 0.0)
    neg = jnp.minimum(pre, 0.0)
    mid = pos * lower.astype(F32) + neg * upper.astype(F32)
    return mid, pos * icpt_low.astype(F32) + neg * icpt_high.astype(F32)


def share_kernel(core_ref, row_ref, lam_ref, slopes_ref, icpt_ref, *out_refs):
    for r in range(SPEC):
        for k in range(D // 128):
            tile = lam_ref[r, :, k * 128 : (k + 1) * 128]
            for out_ref in out_refs:
                out_ref[r * (D // 128) + k] = tile
    row = row_ref[0]
    for k, out_ref in enumerate(out_refs):
        core = core_ref[0] ^ k
        for j in range(STEPS):
            if j < STEPS - 1:
                owner = row + (2 * core - 1) * (j + 1)
                cuts = [(owner, core), (owner, 1 - core)]
            else:
                cuts = [(row + STEPS, core), (row, core)]
            for h, (owner, chunk) in enumerate(cuts):
                start = pl.multiple_of((owner & 7) * PART + chunk * CHUNK, CHUNK)
                for kind in range(4):
                    ref = slopes_ref if kind < 2 else icpt_ref
                    values = ref[kind % 2, :, pl.ds(start, CHUNK)]
                    tile = LAM_TILES + (j * 4 + kind) * 4 + h * 2
                    out_ref[tile] = values[:, 0:128]
                    out_ref[tile + 1] = values[:, 128:256]


def share(core, row, by_row, slopes, icpt):
    tiles = LAM_TILES + 4 * STEPS * 4
    return pl.pallas_call(
        share_kernel,
        out_shape=(jax.ShapeDtypeStruct((tiles, 16, 128), BF16),) * 2,
        in_specs=[pl.BlockSpec(memory_space=pltpu.SMEM)] * 2
        + [pl.BlockSpec(memory_space=pltpu.VMEM)] * 3,
        compiler_params=pltpu.CompilerParams(vmem_limit_bytes=60 * 1024 * 1024),
        name="share",
    )(core, row, by_row, slopes, icpt)


def channel_kernel(step, *refs):
    first, last = step == 0, step == STEPS - 1
    count = (3, 2, 2, 1)[step]
    core_ref, words, refs = refs[0], refs[1 : 1 + count], refs[1 + count :]
    if first:
        down_scale_ref, *team, acc_ref, bias_ref, scaled_ref, bounds_ref, down, up = refs
        for k, got_ref in enumerate(team):
            start = (core_ref[0] ^ k) * 16
            for r in range(SPEC):
                rows = pl.ds(pl.multiple_of(r * SHARED + start, 16), 16)
                for c in range(D // 128):
                    cut = slice(c * 128, (c + 1) * 128)
                    lam = got_ref[r * (D // 128) + c].astype(F32)
                    scaled_ref[rows, cut] = (lam * down_scale_ref[:, cut]).astype(BF16)
                    acc_ref[rows, cut] = 0.5 * lam
            rows = pl.ds(pl.multiple_of(start, 16), 16)
            for i in range(STEPS * 4):
                for h in range(4):
                    tile = got_ref[LAM_TILES + i * 4 + h]
                    bounds_ref[i // 4, i % 4, rows, h * 128 : (h + 1) * 128] = tile
        acc_in, bias_in = acc_ref, None
    else:
        scaled_ref, bounds_ref, acc_in, bias_in, *outs, down, up = refs
    words = [w[...] for w in words]
    for h, chunk in enumerate(words):
        for m in range(4):
            for k in range(8):
                rows = m * 256 + k // 2 * 64
                cut = h * CHUNK + k % 2 * 128
                codes = unpack_codes(chunk[k * 64 : (k + 1) * 64], m)
                down[rows : rows + 64, cut : cut + 128] = codes
                rows = h * CHUNK + m * 64
                codes = unpack_codes(chunk[512 + k * 64 : 512 + (k + 1) * 64], m)
                up[rows : rows + 64, k * 128 : (k + 1) * 128] = codes
    scale = [chunk[1024 + h : 1025 + h] for chunk in words for h in range(2)]
    scale = jnp.concatenate(scale, axis=1).astype(F32) * (1.0 / SCALE_ONE)
    pre = jnp.dot(scaled_ref[...], down[...], preferred_element_type=F32)
    width = count * CHUNK
    pre = pre.reshape(SPEC, SHARED, width)
    if first:
        bounds = [
            jnp.concatenate([bounds_ref[0, kind], bounds_ref[STEPS - 1, kind, :, CHUNK:PART]], axis=1)
            for kind in range(4)
        ]
    else:
        bounds = [bounds_ref[step, kind, :, 0:width] for kind in range(4)]
    mid, terms = relaxed(pre, *bounds)
    terms = jnp.sum(terms.reshape(SPEC, SHARED // 8, 8, width), axis=1)
    bias = sum(terms[:, :, k * 128 : (k + 1) * 128] for k in range(width // 128))
    weighted = (mid.reshape(ROWS_DEV, width) * scale).astype(BF16)
    part = jnp.dot(weighted, up[...], preferred_element_type=F32)
    total = acc_in[...] + part
    if not first:
        bias = bias + bias_in[...]
    if last:
        keep_ref, send_ref, bias_ref = outs
        own = core_ref[0] == 0
        turned = total.T.reshape(32, 2, 16, ROWS_DEV)
        keep_ref[...] = jnp.where(own, turned[:, 0], turned[:, 1])
        send_ref[...] = jnp.where(own, turned[:, 1], turned[:, 0]).astype(BF16)
    else:
        if not first:
            acc_ref, bias_ref = outs
        acc_ref[...] = total
    bias_ref[...] = bias


def channel_part(step, core, *rest):
    acc_shape = jax.ShapeDtypeStruct((ROWS_DEV, D), F32)
    bias_shape = jax.ShapeDtypeStruct((SPEC, 8, 128), F32)
    operands = [core, *rest]
    width = (3, 2, 2, 1)[step] * CHUNK
    aliases = {}
    if step == 0:
        scaled_shape = jax.ShapeDtypeStruct((ROWS_DEV, D), BF16)
        bounds_shape = jax.ShapeDtypeStruct((STEPS, 4, SHARED, PART), BF16)
        out_shape = (acc_shape, bias_shape, scaled_shape, bounds_shape)
    elif step == STEPS - 1:
        out_shape = (
            jax.ShapeDtypeStruct((32, 16, ROWS_DEV), F32),
            jax.ShapeDtypeStruct((32, 16, ROWS_DEV), BF16),
            bias_shape,
        )
    else:
        out_shape = (acc_shape, bias_shape)
        aliases = {len(operands) - 2: 0, len(operands) - 1: 1}
    smem, vmem = pl.BlockSpec(memory_space=pltpu.SMEM), pl.BlockSpec(memory_space=pltpu.VMEM)
    return pl.pallas_call(
        functools.partial(channel_kernel, step),
        out_shape=out_shape,
        in_specs=[smem] + [vmem] * (len(operands) - 1),
        out_specs=(vmem,) * len(out_shape),
        scratch_shapes=[pltpu.VMEM((D, width), BF16), pltpu.VMEM((width, D), BF16)],
        input_output_aliases=aliases,
        compiler_params=pltpu.CompilerParams(vmem_limit_bytes=VMEM),
        cost_estimate=pl.CostEstimate(
            flops=4 * ROWS_DEV * width * D,
            bytes_accessed=2 * PACKED * 128 * 4 + 3 * ROWS_DEV * D * 4,
            transcendentals=0,
        ),
        name="channel",
    )(*operands)


def token_kernel(
    got_ref, dense_ref, slopes_ref, icpt_ref, chan_bias_ref, columns_ref, mid_ref, bias_ref
):
    lane = lax.broadcasted_iota(I32, (16, 128), 1) // 32
    for u in range(NTB):
        for a in range(2):
            v = [got_ref[4 * u + p, :, a * 128 : (a + 1) * 128].astype(F32) for p in range(4)]
            for bit in (1, 2):
                low = (lane & bit) == 0
                new = list(v)
                for p in range(4):
                    if p & bit == 0:
                        q = p + bit
                        new[p] = jnp.where(low, v[p], pltpu.roll(v[q], 32 * bit, 1))
                        new[q] = jnp.where(low, pltpu.roll(v[p], 128 - 32 * bit, 1), v[q])
                v = new
            for q in range(4):
                r = 4 * a + q
                columns_ref[r * 16 : (r + 1) * 16, u * 128 : (u + 1) * 128] = v[q].astype(BF16)
    pre = jnp.dot(columns_ref[...], dense_ref[...], preferred_element_type=F32)
    pre = pre.reshape(SPEC, 16, TH)
    mid, terms = relaxed(pre, slopes_ref[0], slopes_ref[1], icpt_ref[0], icpt_ref[1])
    mid_ref[...] = mid.reshape(SPEC * 16, TH).astype(BF16)
    terms = terms[:, 0:8, :] + terms[:, 8:16, :]
    terms = sum(terms[:, :, k * 128 : (k + 1) * 128] for k in range(NHB)) + chan_bias_ref[...]
    by_row = jnp.sum(jnp.sum(terms, axis=1), axis=1, keepdims=True)
    row = lax.broadcasted_iota(I32, (SPEC, 128), 0)
    lane = lax.broadcasted_iota(I32, (SPEC, 128), 1)
    line = jnp.sum(jnp.where(row == lane, by_row, 0.0), axis=0, keepdims=True)
    bias_ref[...] = jnp.broadcast_to(line[None], bias_ref.shape)


def token_mlp(got, dense_out, slopes, icpt, chan_bias):
    return pl.pallas_call(
        token_kernel,
        out_shape=(
            jax.ShapeDtypeStruct((SPEC * 16, TOK), BF16),
            jax.ShapeDtypeStruct((SPEC * 16, TH), BF16),
            jax.ShapeDtypeStruct((64, 1, 128), F32),
        ),
        compiler_params=pltpu.CompilerParams(vmem_limit_bytes=VMEM),
        name="token",
    )(got, dense_out, slopes, icpt, chan_bias)


def back_kernel(columns_ref, mid_ref, dense_ref, out_ref):
    back = jnp.dot(mid_ref[...], dense_ref[...], preferred_element_type=F32)
    out_ref[...] = (columns_ref[...].astype(F32) + back).astype(BF16)


def token_back(columns, mid, dense_in):
    return pl.pallas_call(
        back_kernel,
        out_shape=jax.ShapeDtypeStruct((SPEC * 16, TOK), BF16),
        compiler_params=pltpu.CompilerParams(vmem_limit_bytes=VMEM),
        name="back",
    )(columns, mid, dense_in)


def on_device(
    lam_out,
    q_down,
    down_scale,
    q_up,
    up_scale,
    chan_slopes,
    chan_icpt,
    tok_in_blocks,
    tok_out_blocks,
    block_cells,
    tok_slopes,
    tok_icpt,
):
    core = lax.axis_index("core").astype(I32).reshape(1)
    row = lax.axis_index("rows").astype(I32).reshape(1)
    tok_dev = lam_out.shape[0]
    slices = lax.axis_size("rows")
    ahead = [(i * 2, (i + 1) % slices * 2) for i in range(slices)]
    behind = [(i * 2 + 1, (i - 1) % slices * 2 + 1) for i in range(slices)]

    def forward(words, pairs):
        return tuple(lax.ppermute(w, ("rows", "core"), pairs) for w in words)

    own = tuple(pack(chain, core, q_down, q_up, up_scale) for chain in range(2))
    first = forward(own, ahead + behind)
    _, lam, *bounds = lax.optimization_barrier((own, lam_out, chan_slopes, chan_icpt))
    keep_part, send_part = share(
        core, row, jnp.swapaxes(lam, 0, 1), *(b.reshape(2, tok_dev, CH) for b in bounds)
    )
    words, send_part = lax.optimization_barrier((first[0], send_part))
    second = forward((words, first[1]), ahead + behind)
    other_part = lax.ppermute(send_part, "core", SWAP)
    words, other_part = lax.optimization_barrier((second[0], other_part))
    third = forward((words, second[1]), ahead + behind)
    carried = channel_part(0, core, *first, own[0], down_scale.reshape(1, D), keep_part, other_part)
    acc, chan_bias, *given = carried
    acc, chan_bias = channel_part(1, core, *second, *given, acc, chan_bias)
    far = forward(third[:1], ahead + behind)

    dense_in, dense_out = dense_blocks(block_cells, tok_in_blocks, tok_out_blocks)
    slopes = jnp.transpose(tok_slopes, (0, 2, 3, 1)).reshape(2, 16, TH)
    icpt = jnp.transpose(tok_icpt, (0, 2, 3, 1)).reshape(2, 16, TH)

    acc, chan_bias = channel_part(2, core, *third, *given, acc, chan_bias)
    keep, send, chan_bias = channel_part(3, core, *far, *given, acc, chan_bias)
    summed = (keep + lax.ppermute(send, "core", SWAP).astype(F32)).astype(BF16)
    got = lax.all_to_all(summed, ("z", "x"), 0, 0, tiled=True)
    columns, mid, own_bias = token_mlp(got, dense_out, slopes, icpt, chan_bias)
    all_bias = lax.all_to_all(own_bias, MP, 0, 0, tiled=True)
    lam_in = token_back(columns, mid, dense_in)
    lam_in = jnp.transpose(lam_in.reshape(SPEC, 16, TOK), (2, 0, 1))
    return (lam_in, jnp.sum(all_bias, axis=(0, 1))[:SPEC])


def solution(mesh):
    axes = Mesh(mesh.devices.reshape(8, 8, 4, 2), ("rows",) + MP)
    return jax.shard_map(
        on_device,
        mesh=axes,
        in_specs=(
            P(MP, "rows", None),
            P(None, "rows"),
            P(),
            P("rows", None),
            P("rows"),
            P(None, MP, "rows", None),
            P(None, MP, "rows", None),
            P(),
            P(),
            P(),
            P(None, None, "rows", MP),
            P(None, None, "rows", MP),
        ),
        out_specs=(P(None, "rows", MP), P("rows")),
        check_vma=False,
    )
```

```python
import functools

import jax
import jax.numpy as jnp
from jax import lax
from jax.experimental import pallas as pl
from jax.experimental.pallas import tpu as pltpu
from jax.sharding import Mesh
from jax.sharding import PartitionSpec as P

D = 1024
CH = 4096
TH = 512
TOK = 1024
BLK = 128
NB = 16
SPEC = 8
NHB = 4
NTB = 8
F32 = jnp.float32
BF16 = jnp.bfloat16
I32 = jnp.int32
MP = ("z", "x", "core")
SWAP = [(0, 1), (1, 0)]
VMEM = 32 * 1024 * 1024

PART = 512
CHUNK = 256
STEPS = 4
SHARED = 32
ROWS_DEV = SPEC * SHARED
PACKED = 1032
LAM_TILES = SPEC * (D // 128)
SCALE_ONE = float(2**38)


def pack_codes(parts):
    a, b, c, d = (p.astype(F32).astype(I32) for p in parts)
    return (a & 255) | ((b & 255) << 8) | ((c & 255) << 16) | (d << 24)


def unpack_codes(words, m):
    shifted = words << (24 - 8 * m) if m < 3 else words
    return (shifted >> 24).astype(F32).astype(BF16)


def pack_kernel(chain, core_ref, down_hbm, up_hbm, scale_hbm, out_ref, down_ref, up_ref, scale_ref, sems):
    cut = pl.ds(pl.multiple_of((core_ref[0] ^ chain) * CHUNK, CHUNK), CHUNK)
    copies = [
        pltpu.make_async_copy(down_hbm.at[:, cut], down_ref, sems.at[0]),
        pltpu.make_async_copy(up_hbm.at[cut, :], up_ref, sems.at[1]),
        pltpu.make_async_copy(scale_hbm.at[:, cut], scale_ref, sems.at[2]),
    ]
    for copy in copies:
        copy.start()
    out_ref[1024:1032, :] = jnp.zeros((8, 128), I32)
    copies[0].wait()
    down = pack_codes([down_ref[m * 256 : (m + 1) * 256, :] for m in range(4)])
    for k in range(8):
        rows, cut = slice(k // 2 * 64, (k // 2 + 1) * 64), slice(k % 2 * 128, (k % 2 + 1) * 128)
        out_ref[k * 64 : (k + 1) * 64, :] = down[rows, cut]
    copies[1].wait()
    up = pack_codes([up_ref[m * 64 : (m + 1) * 64, :] for m in range(4)])
    for k in range(8):
        out_ref[512 + k * 64 : 512 + (k + 1) * 64, :] = up[:, k * 128 : (k + 1) * 128]
    copies[2].wait()
    scale = (scale_ref[...] * SCALE_ONE).astype(I32)
    for h in range(2):
        out_ref[1024 + h : 1025 + h, :] = scale[:, h * 128 : (h + 1) * 128]


def pack(chain, core, q_down, q_up, up_scale):
    smem, hbm, vmem = (
        pl.BlockSpec(memory_space=space) for space in (pltpu.SMEM, pltpu.HBM, pltpu.VMEM)
    )
    return pl.pallas_call(
        functools.partial(pack_kernel, chain),
        out_shape=jax.ShapeDtypeStruct((PACKED, 128), I32),
        in_specs=[smem, hbm, hbm, hbm],
        out_specs=vmem,
        scratch_shapes=[
            pltpu.VMEM((D, CHUNK), BF16),
            pltpu.VMEM((CHUNK, D), BF16),
            pltpu.VMEM((1, CHUNK), F32),
            pltpu.SemaphoreType.DMA((3,)),
        ],
        compiler_params=pltpu.CompilerParams(vmem_limit_bytes=60 * 1024 * 1024),
        name="pack",
    )(core, q_down, q_up, up_scale.reshape(1, -1))


def dense_kernel(cells_ref, in_ref, out_ref, dense_in_ref, dense_out_ref):
    dense_in_ref[...] = jnp.zeros_like(dense_in_ref)
    dense_out_ref[...] = jnp.zeros_like(dense_out_ref)
    for b in range(NB):
        h = pl.multiple_of(cells_ref[b] // NTB * BLK, BLK)
        u = pl.multiple_of(cells_ref[b] % NTB * BLK, BLK)
        dense_in_ref[pl.ds(h, BLK), pl.ds(u, BLK)] = in_ref[b]
        dense_out_ref[pl.ds(u, BLK), pl.ds(h, BLK)] = out_ref[b]


def dense_blocks(cells, in_blocks, out_blocks):
    return pl.pallas_call(
        dense_kernel,
        out_shape=(
            jax.ShapeDtypeStruct((TH, TOK), BF16),
            jax.ShapeDtypeStruct((TOK, TH), BF16),
        ),
        in_specs=[
            pl.BlockSpec(memory_space=pltpu.SMEM),
            pl.BlockSpec(memory_space=pltpu.VMEM),
            pl.BlockSpec(memory_space=pltpu.VMEM),
        ],
        out_specs=(
            pl.BlockSpec(memory_space=pltpu.VMEM),
            pl.BlockSpec(memory_space=pltpu.VMEM),
        ),
        compiler_params=pltpu.CompilerParams(vmem_limit_bytes=VMEM),
        name="dense",
    )(cells, in_blocks, out_blocks)


def relaxed(pre, lower, upper, icpt_low, icpt_high):
    pos = jnp.maximum(pre, 0.0)
    neg = jnp.minimum(pre, 0.0)
    mid = pos * lower.astype(F32) + neg * upper.astype(F32)
    return mid, pos * icpt_low.astype(F32) + neg * icpt_high.astype(F32)


def share_kernel(core_ref, row_ref, lam_ref, slopes_ref, icpt_ref, *out_refs):
    for r in range(SPEC):
        for k in range(D // 128):
            tile = lam_ref[r, :, k * 128 : (k + 1) * 128]
            for out_ref in out_refs:
                out_ref[r * (D // 128) + k] = tile
    row = row_ref[0]
    for k, out_ref in enumerate(out_refs):
        core = core_ref[0] ^ k
        for j in range(STEPS):
            if j < STEPS - 1:
                owner = row + (2 * core - 1) * (j + 1)
                cuts = [(owner, core), (owner, 1 - core)]
            else:
                cuts = [(row + STEPS, core), (row, core)]
            for h, (owner, chunk) in enumerate(cuts):
                start = pl.multiple_of((owner & 7) * PART + chunk * CHUNK, CHUNK)
                for kind in range(4):
                    ref = slopes_ref if kind < 2 else icpt_ref
                    values = ref[kind % 2, :, pl.ds(start, CHUNK)]
                    tile = LAM_TILES + (j * 4 + kind) * 4 + h * 2
                    out_ref[tile] = values[:, 0:128]
                    out_ref[tile + 1] = values[:, 128:256]


def share(core, row, by_row, slopes, icpt):
    tiles = LAM_TILES + 4 * STEPS * 4
    return pl.pallas_call(
        share_kernel,
        out_shape=(jax.ShapeDtypeStruct((tiles, 16, 128), BF16),) * 2,
        in_specs=[pl.BlockSpec(memory_space=pltpu.SMEM)] * 2
        + [pl.BlockSpec(memory_space=pltpu.VMEM)] * 3,
        compiler_params=pltpu.CompilerParams(vmem_limit_bytes=60 * 1024 * 1024),
        name="share",
    )(core, row, by_row, slopes, icpt)


def channel_kernel(step, *refs):
    first, last = step == 0, step == STEPS - 1
    count = (3, 2, 2, 1)[step]
    core_ref, words, refs = refs[0], refs[1 : 1 + count], refs[1 + count :]
    if first:
        down_scale_ref, *team, acc_ref, bias_ref, scaled_ref, bounds_ref, down, up = refs
        for k, got_ref in enumerate(team):
            start = (core_ref[0] ^ k) * 16
            for r in range(SPEC):
                rows = pl.ds(pl.multiple_of(r * SHARED + start, 16), 16)
                for c in range(D // 128):
                    cut = slice(c * 128, (c + 1) * 128)
                    lam = got_ref[r * (D // 128) + c].astype(F32)
                    scaled_ref[rows, cut] = (lam * down_scale_ref[:, cut]).astype(BF16)
                    acc_ref[rows, cut] = 0.5 * lam
            rows = pl.ds(pl.multiple_of(start, 16), 16)
            for i in range(STEPS * 4):
                for h in range(4):
                    tile = got_ref[LAM_TILES + i * 4 + h]
                    bounds_ref[i // 4, i % 4, rows, h * 128 : (h + 1) * 128] = tile
        acc_in, bias_in = acc_ref, None
    else:
        scaled_ref, bounds_ref, acc_in, bias_in, *outs, down, up = refs
    words = [w[...] for w in words]
    for h, chunk in enumerate(words):
        for m in range(4):
            for k in range(8):
                rows = m * 256 + k // 2 * 64
                cut = h * CHUNK + k % 2 * 128
                codes = unpack_codes(chunk[k * 64 : (k + 1) * 64], m)
                down[rows : rows + 64, cut : cut + 128] = codes
                rows = h * CHUNK + m * 64
                codes = unpack_codes(chunk[512 + k * 64 : 512 + (k + 1) * 64], m)
                up[rows : rows + 64, k * 128 : (k + 1) * 128] = codes
    scale = [chunk[1024 + h : 1025 + h] for chunk in words for h in range(2)]
    scale = jnp.concatenate(scale, axis=1).astype(F32) * (1.0 / SCALE_ONE)
    pre = jnp.dot(scaled_ref[...], down[...], preferred_element_type=F32)
    width = count * CHUNK
    pre = pre.reshape(SPEC, SHARED, width)
    if first:
        bounds = [
            jnp.concatenate([bounds_ref[0, kind], bounds_ref[STEPS - 1, kind, :, CHUNK:PART]], axis=1)
            for kind in range(4)
        ]
    else:
        bounds = [bounds_ref[step, kind, :, 0:width] for kind in range(4)]
    mid, terms = relaxed(pre, *bounds)
    terms = jnp.sum(terms.reshape(SPEC, SHARED // 8, 8, width), axis=1)
    bias = sum(terms[:, :, k * 128 : (k + 1) * 128] for k in range(width // 128))
    weighted = (mid.reshape(ROWS_DEV, width) * scale).astype(BF16)
    part = jnp.dot(weighted, up[...], preferred_element_type=F32)
    total = acc_in[...] + part
    if not first:
        bias = bias + bias_in[...]
    if last:
        part_ref, bias_ref = outs
        part_ref[...] = total.T.reshape(64, 16, ROWS_DEV).astype(BF16)
    else:
        if not first:
            acc_ref, bias_ref = outs
        acc_ref[...] = total
    bias_ref[...] = bias


def channel_part(step, core, *rest):
    acc_shape = jax.ShapeDtypeStruct((ROWS_DEV, D), F32)
    bias_shape = jax.ShapeDtypeStruct((SPEC, 8, 128), F32)
    operands = [core, *rest]
    width = (3, 2, 2, 1)[step] * CHUNK
    aliases = {}
    if step == 0:
        scaled_shape = jax.ShapeDtypeStruct((ROWS_DEV, D), BF16)
        bounds_shape = jax.ShapeDtypeStruct((STEPS, 4, SHARED, PART), BF16)
        out_shape = (acc_shape, bias_shape, scaled_shape, bounds_shape)
    elif step == STEPS - 1:
        out_shape = (jax.ShapeDtypeStruct((64, 16, ROWS_DEV), BF16), bias_shape)
    else:
        out_shape = (acc_shape, bias_shape)
        aliases = {len(operands) - 2: 0, len(operands) - 1: 1}
    smem, vmem = pl.BlockSpec(memory_space=pltpu.SMEM), pl.BlockSpec(memory_space=pltpu.VMEM)
    return pl.pallas_call(
        functools.partial(channel_kernel, step),
        out_shape=out_shape,
        in_specs=[smem] + [vmem] * (len(operands) - 1),
        out_specs=(vmem,) * len(out_shape),
        scratch_shapes=[pltpu.VMEM((D, width), BF16), pltpu.VMEM((width, D), BF16)],
        input_output_aliases=aliases,
        compiler_params=pltpu.CompilerParams(vmem_limit_bytes=VMEM),
        cost_estimate=pl.CostEstimate(
            flops=4 * ROWS_DEV * width * D,
            bytes_accessed=2 * PACKED * 128 * 4 + 3 * ROWS_DEV * D * 4,
            transcendentals=0,
        ),
        name="channel",
    )(*operands)


def token_kernel(
    got_ref, dense_ref, slopes_ref, icpt_ref, chan_bias_ref, columns_ref, mid_ref, bias_ref
):
    lane = lax.broadcasted_iota(I32, (16, 128), 1) // 32
    for u in range(NTB):
        for a in range(2):
            cut = slice(a * 128, (a + 1) * 128)
            v = [
                got_ref[s, :, cut].astype(F32) + got_ref[s + 1, :, cut].astype(F32)
                for s in range(8 * u, 8 * u + 8, 2)
            ]
            for bit in (1, 2):
                low = (lane & bit) == 0
                new = list(v)
                for p in range(4):
                    if p & bit == 0:
                        q = p + bit
                        new[p] = jnp.where(low, v[p], pltpu.roll(v[q], 32 * bit, 1))
                        new[q] = jnp.where(low, pltpu.roll(v[p], 128 - 32 * bit, 1), v[q])
                v = new
            for q in range(4):
                r = 4 * a + q
                columns_ref[r * 16 : (r + 1) * 16, u * 128 : (u + 1) * 128] = v[q].astype(BF16)
    pre = jnp.dot(columns_ref[...], dense_ref[...], preferred_element_type=F32)
    pre = pre.reshape(SPEC, 16, TH)
    mid, terms = relaxed(pre, slopes_ref[0], slopes_ref[1], icpt_ref[0], icpt_ref[1])
    mid_ref[...] = mid.reshape(SPEC * 16, TH).astype(BF16)
    terms = terms[:, 0:8, :] + terms[:, 8:16, :]
    terms = sum(terms[:, :, k * 128 : (k + 1) * 128] for k in range(NHB)) + chan_bias_ref[...]
    by_row = jnp.sum(jnp.sum(terms, axis=1), axis=1, keepdims=True)
    row = lax.broadcasted_iota(I32, (SPEC, 128), 0)
    lane = lax.broadcasted_iota(I32, (SPEC, 128), 1)
    line = jnp.sum(jnp.where(row == lane, by_row, 0.0), axis=0, keepdims=True)
    bias_ref[...] = jnp.broadcast_to(line[None], bias_ref.shape)


def token_mlp(got, dense_out, slopes, icpt, chan_bias):
    return pl.pallas_call(
        token_kernel,
        out_shape=(
            jax.ShapeDtypeStruct((SPEC * 16, TOK), BF16),
            jax.ShapeDtypeStruct((SPEC * 16, TH), BF16),
            jax.ShapeDtypeStruct((64, 1, 128), F32),
        ),
        compiler_params=pltpu.CompilerParams(vmem_limit_bytes=VMEM),
        name="token",
    )(got, dense_out, slopes, icpt, chan_bias)


def back_kernel(columns_ref, mid_ref, dense_ref, out_ref):
    back = jnp.dot(mid_ref[...], dense_ref[...], preferred_element_type=F32)
    out_ref[...] = (columns_ref[...].astype(F32) + back).astype(BF16)


def token_back(columns, mid, dense_in):
    return pl.pallas_call(
        back_kernel,
        out_shape=jax.ShapeDtypeStruct((SPEC * 16, TOK), BF16),
        compiler_params=pltpu.CompilerParams(vmem_limit_bytes=VMEM),
        name="back",
    )(columns, mid, dense_in)


def on_device(
    lam_out,
    q_down,
    down_scale,
    q_up,
    up_scale,
    chan_slopes,
    chan_icpt,
    tok_in_blocks,
    tok_out_blocks,
    block_cells,
    tok_slopes,
    tok_icpt,
):
    core = lax.axis_index("core").astype(I32).reshape(1)
    row = lax.axis_index("rows").astype(I32).reshape(1)
    tok_dev = lam_out.shape[0]
    slices = lax.axis_size("rows")
    ahead = [(i * 2, (i + 1) % slices * 2) for i in range(slices)]
    behind = [(i * 2 + 1, (i - 1) % slices * 2 + 1) for i in range(slices)]

    def forward(words, pairs):
        return tuple(lax.ppermute(w, ("rows", "core"), pairs) for w in words)

    own = tuple(pack(chain, core, q_down, q_up, up_scale) for chain in range(2))
    first = forward(own, ahead + behind)
    _, lam, *bounds = lax.optimization_barrier((own, lam_out, chan_slopes, chan_icpt))
    keep_part, send_part = share(
        core, row, jnp.swapaxes(lam, 0, 1), *(b.reshape(2, tok_dev, CH) for b in bounds)
    )
    words, send_part = lax.optimization_barrier((first[0], send_part))
    second = forward((words, first[1]), ahead + behind)
    other_part = lax.ppermute(send_part, "core", SWAP)
    words, other_part = lax.optimization_barrier((second[0], other_part))
    third = forward((words, second[1]), ahead + behind)
    carried = channel_part(0, core, *first, own[0], down_scale.reshape(1, D), keep_part, other_part)
    acc, chan_bias, *given = carried
    acc, chan_bias = channel_part(1, core, *second, *given, acc, chan_bias)
    far = forward(third[:1], ahead + behind)

    dense_in, dense_out = dense_blocks(block_cells, tok_in_blocks, tok_out_blocks)
    slopes = jnp.transpose(tok_slopes, (0, 2, 3, 1)).reshape(2, 16, TH)
    icpt = jnp.transpose(tok_icpt, (0, 2, 3, 1)).reshape(2, 16, TH)

    acc, chan_bias = channel_part(2, core, *third, *given, acc, chan_bias)
    parts, chan_bias = channel_part(3, core, *far, *given, acc, chan_bias)
    got = lax.all_to_all(parts, MP, 0, 0, tiled=True)
    columns, mid, own_bias = token_mlp(got, dense_out, slopes, icpt, chan_bias)
    all_bias = lax.all_to_all(own_bias, MP, 0, 0, tiled=True)
    lam_in = token_back(columns, mid, dense_in)
    lam_in = jnp.transpose(lam_in.reshape(SPEC, 16, TOK), (2, 0, 1))
    return (lam_in, jnp.sum(all_bias, axis=(0, 1))[:SPEC])


def solution(mesh):
    axes = Mesh(mesh.devices.reshape(8, 8, 4, 2), ("rows",) + MP)
    return jax.shard_map(
        on_device,
        mesh=axes,
        in_specs=(
            P(MP, "rows", None),
            P(None, "rows"),
            P(),
            P("rows", None),
            P("rows"),
            P(None, MP, "rows", None),
            P(None, MP, "rows", None),
            P(),
            P(),
            P(),
            P(None, None, "rows", MP),
            P(None, None, "rows", MP),
        ),
        out_specs=(P(None, "rows", MP), P("rows")),
        check_vma=False,
    )
```

```python
import functools

import jax
import jax.numpy as jnp
from jax import lax
from jax.experimental import pallas as pl
from jax.experimental.pallas import tpu as pltpu
from jax.sharding import Mesh
from jax.sharding import PartitionSpec as P

D = 1024
CH = 4096
TH = 512
TOK = 1024
BLK = 128
NB = 16
SPEC = 8
NHB = 4
NTB = 8
F32 = jnp.float32
BF16 = jnp.bfloat16
I32 = jnp.int32
MP = ("z", "x", "core")
SWAP = [(0, 1), (1, 0)]
VMEM = 32 * 1024 * 1024

PART = 512
CHUNK = 256
STEPS = 4
SHARED = 32
ROWS_DEV = SPEC * SHARED
PACKED = 1032
LAM_TILES = SPEC * (D // 128)
SCALE_ONE = float(2**38)


def pack_codes(parts):
    a, b, c, d = (p.astype(F32).astype(I32) for p in parts)
    return (a & 255) | ((b & 255) << 8) | ((c & 255) << 16) | (d << 24)


def unpack_codes(words, m):
    shifted = words << (24 - 8 * m) if m < 3 else words
    return (shifted >> 24).astype(F32).astype(BF16)


def pack_kernel(chain, core_ref, down_hbm, up_hbm, scale_hbm, out_ref, down_ref, up_ref, scale_ref, sems):
    cut = pl.ds(pl.multiple_of((core_ref[0] ^ chain) * CHUNK, CHUNK), CHUNK)
    copies = [
        pltpu.make_async_copy(down_hbm.at[:, cut], down_ref, sems.at[0]),
        pltpu.make_async_copy(up_hbm.at[cut, :], up_ref, sems.at[1]),
        pltpu.make_async_copy(scale_hbm.at[:, cut], scale_ref, sems.at[2]),
    ]
    for copy in copies:
        copy.start()
    out_ref[1024:1032, :] = jnp.zeros((8, 128), I32)
    copies[0].wait()
    down = pack_codes([down_ref[m * 256 : (m + 1) * 256, :] for m in range(4)])
    for k in range(8):
        rows, cut = slice(k // 2 * 64, (k // 2 + 1) * 64), slice(k % 2 * 128, (k % 2 + 1) * 128)
        out_ref[k * 64 : (k + 1) * 64, :] = down[rows, cut]
    copies[1].wait()
    up = pack_codes([up_ref[m * 64 : (m + 1) * 64, :] for m in range(4)])
    for k in range(8):
        out_ref[512 + k * 64 : 512 + (k + 1) * 64, :] = up[:, k * 128 : (k + 1) * 128]
    copies[2].wait()
    scale = (scale_ref[...] * SCALE_ONE).astype(I32)
    for h in range(2):
        out_ref[1024 + h : 1025 + h, :] = scale[:, h * 128 : (h + 1) * 128]


def pack(chain, core, q_down, q_up, up_scale):
    smem, hbm, vmem = (
        pl.BlockSpec(memory_space=space) for space in (pltpu.SMEM, pltpu.HBM, pltpu.VMEM)
    )
    return pl.pallas_call(
        functools.partial(pack_kernel, chain),
        out_shape=jax.ShapeDtypeStruct((PACKED, 128), I32),
        in_specs=[smem, hbm, hbm, hbm],
        out_specs=vmem,
        scratch_shapes=[
            pltpu.VMEM((D, CHUNK), BF16),
            pltpu.VMEM((CHUNK, D), BF16),
            pltpu.VMEM((1, CHUNK), F32),
            pltpu.SemaphoreType.DMA((3,)),
        ],
        compiler_params=pltpu.CompilerParams(vmem_limit_bytes=60 * 1024 * 1024),
        name="pack",
    )(core, q_down, q_up, up_scale.reshape(1, -1))


def dense_kernel(cells_ref, in_ref, out_ref, dense_in_ref, dense_out_ref):
    dense_in_ref[...] = jnp.zeros_like(dense_in_ref)
    dense_out_ref[...] = jnp.zeros_like(dense_out_ref)
    for b in range(NB):
        h = pl.multiple_of(cells_ref[b] // NTB * BLK, BLK)
        u = pl.multiple_of(cells_ref[b] % NTB * BLK, BLK)
        dense_in_ref[pl.ds(h, BLK), pl.ds(u, BLK)] = in_ref[b]
        dense_out_ref[pl.ds(u, BLK), pl.ds(h, BLK)] = out_ref[b]


def dense_blocks(cells, in_blocks, out_blocks):
    return pl.pallas_call(
        dense_kernel,
        out_shape=(
            jax.ShapeDtypeStruct((TH, TOK), BF16),
            jax.ShapeDtypeStruct((TOK, TH), BF16),
        ),
        in_specs=[
            pl.BlockSpec(memory_space=pltpu.SMEM),
            pl.BlockSpec(memory_space=pltpu.VMEM),
            pl.BlockSpec(memory_space=pltpu.VMEM),
        ],
        out_specs=(
            pl.BlockSpec(memory_space=pltpu.VMEM),
            pl.BlockSpec(memory_space=pltpu.VMEM),
        ),
        compiler_params=pltpu.CompilerParams(vmem_limit_bytes=VMEM),
        name="dense",
    )(cells, in_blocks, out_blocks)


def relaxed(pre, lower, upper, icpt_low, icpt_high):
    pos = jnp.maximum(pre, 0.0)
    neg = jnp.minimum(pre, 0.0)
    mid = pos * lower.astype(F32) + neg * upper.astype(F32)
    return mid, pos * icpt_low.astype(F32) + neg * icpt_high.astype(F32)


def share_kernel(core_ref, row_ref, lam_ref, slopes_ref, icpt_ref, *out_refs):
    for r in range(SPEC):
        for k in range(D // 128):
            tile = lam_ref[r, :, k * 128 : (k + 1) * 128]
            for out_ref in out_refs:
                out_ref[r * (D // 128) + k] = tile
    row = row_ref[0]
    for k, out_ref in enumerate(out_refs):
        core = core_ref[0] ^ k
        for j in range(STEPS):
            if j < STEPS - 1:
                owner = row + (2 * core - 1) * (j + 1)
                cuts = [(owner, core), (owner, 1 - core)]
            else:
                cuts = [(row + STEPS, core), (row, core)]
            for h, (owner, chunk) in enumerate(cuts):
                start = pl.multiple_of((owner & 7) * PART + chunk * CHUNK, CHUNK)
                for kind in range(4):
                    ref = slopes_ref if kind < 2 else icpt_ref
                    values = ref[kind % 2, :, pl.ds(start, CHUNK)]
                    tile = LAM_TILES + (j * 4 + kind) * 4 + h * 2
                    out_ref[tile] = values[:, 0:128]
                    out_ref[tile + 1] = values[:, 128:256]


def share(core, row, by_row, slopes, icpt):
    tiles = LAM_TILES + 4 * STEPS * 4
    return pl.pallas_call(
        share_kernel,
        out_shape=(jax.ShapeDtypeStruct((tiles, 16, 128), BF16),) * 2,
        in_specs=[pl.BlockSpec(memory_space=pltpu.SMEM)] * 2
        + [pl.BlockSpec(memory_space=pltpu.VMEM)] * 3,
        compiler_params=pltpu.CompilerParams(vmem_limit_bytes=60 * 1024 * 1024),
        name="share",
    )(core, row, by_row, slopes, icpt)


def channel_kernel(step, *refs):
    first, last = step == 0, step == STEPS - 1
    count = (3, 2, 2, 1)[step]
    core_ref, words, refs = refs[0], refs[1 : 1 + count], refs[1 + count :]
    if first:
        down_scale_ref, *team, acc_ref, bias_ref, scaled_ref, bounds_ref, down, up = refs
        for k, got_ref in enumerate(team):
            start = (core_ref[0] ^ k) * 16
            for r in range(SPEC):
                rows = pl.ds(pl.multiple_of(r * SHARED + start, 16), 16)
                for c in range(D // 128):
                    cut = slice(c * 128, (c + 1) * 128)
                    lam = got_ref[r * (D // 128) + c].astype(F32)
                    scaled_ref[rows, cut] = (lam * down_scale_ref[:, cut]).astype(BF16)
                    acc_ref[rows, cut] = 0.5 * lam
            rows = pl.ds(pl.multiple_of(start, 16), 16)
            for i in range(STEPS * 4):
                for h in range(4):
                    tile = got_ref[LAM_TILES + i * 4 + h]
                    bounds_ref[i // 4, i % 4, rows, h * 128 : (h + 1) * 128] = tile
        acc_in, bias_in = acc_ref, None
    else:
        scaled_ref, bounds_ref, acc_in, bias_in, *outs, down, up = refs
    words = [w[...] for w in words]
    for h, chunk in enumerate(words):
        for m in range(4):
            for k in range(8):
                rows = m * 256 + k // 2 * 64
                cut = h * CHUNK + k % 2 * 128
                codes = unpack_codes(chunk[k * 64 : (k + 1) * 64], m)
                down[rows : rows + 64, cut : cut + 128] = codes
                rows = h * CHUNK + m * 64
                codes = unpack_codes(chunk[512 + k * 64 : 512 + (k + 1) * 64], m)
                up[rows : rows + 64, k * 128 : (k + 1) * 128] = codes
    scale = [chunk[1024 + h : 1025 + h] for chunk in words for h in range(2)]
    scale = jnp.concatenate(scale, axis=1).astype(F32) * (1.0 / SCALE_ONE)
    pre = jnp.dot(scaled_ref[...], down[...], preferred_element_type=F32)
    width = count * CHUNK
    pre = pre.reshape(SPEC, SHARED, width)
    if first:
        bounds = [
            jnp.concatenate([bounds_ref[0, kind], bounds_ref[STEPS - 1, kind, :, CHUNK:PART]], axis=1)
            for kind in range(4)
        ]
    else:
        bounds = [bounds_ref[step, kind, :, 0:width] for kind in range(4)]
    mid, terms = relaxed(pre, *bounds)
    terms = jnp.sum(terms.reshape(SPEC, SHARED // 8, 8, width), axis=1)
    bias = sum(terms[:, :, k * 128 : (k + 1) * 128] for k in range(width // 128))
    weighted = (mid.reshape(ROWS_DEV, width) * scale).astype(BF16)
    part = jnp.dot(weighted, up[...], preferred_element_type=F32)
    total = acc_in[...] + part
    if not first:
        bias = bias + bias_in[...]
    if last:
        keep_ref, send_ref, bias_ref = outs
        own = core_ref[0] == 0
        turned = total.T.reshape(8, 4, 2, 16, ROWS_DEV)
        for x in range(4):
            chips = slice(x * 8, (x + 1) * 8)
            keep_ref[chips] = jnp.where(own, turned[:, x, 0], turned[:, x, 1])
            send_ref[chips] = jnp.where(own, turned[:, x, 1], turned[:, x, 0]).astype(BF16)
    else:
        if not first:
            acc_ref, bias_ref = outs
        acc_ref[...] = total
    bias_ref[...] = bias


def channel_part(step, core, *rest):
    acc_shape = jax.ShapeDtypeStruct((ROWS_DEV, D), F32)
    bias_shape = jax.ShapeDtypeStruct((SPEC, 8, 128), F32)
    operands = [core, *rest]
    width = (3, 2, 2, 1)[step] * CHUNK
    aliases = {}
    if step == 0:
        scaled_shape = jax.ShapeDtypeStruct((ROWS_DEV, D), BF16)
        bounds_shape = jax.ShapeDtypeStruct((STEPS, 4, SHARED, PART), BF16)
        out_shape = (acc_shape, bias_shape, scaled_shape, bounds_shape)
    elif step == STEPS - 1:
        out_shape = (
            jax.ShapeDtypeStruct((32, 16, ROWS_DEV), F32),
            jax.ShapeDtypeStruct((32, 16, ROWS_DEV), BF16),
            bias_shape,
        )
    else:
        out_shape = (acc_shape, bias_shape)
        aliases = {len(operands) - 2: 0, len(operands) - 1: 1}
    smem, vmem = pl.BlockSpec(memory_space=pltpu.SMEM), pl.BlockSpec(memory_space=pltpu.VMEM)
    return pl.pallas_call(
        functools.partial(channel_kernel, step),
        out_shape=out_shape,
        in_specs=[smem] + [vmem] * (len(operands) - 1),
        out_specs=(vmem,) * len(out_shape),
        scratch_shapes=[pltpu.VMEM((D, width), BF16), pltpu.VMEM((width, D), BF16)],
        input_output_aliases=aliases,
        compiler_params=pltpu.CompilerParams(vmem_limit_bytes=VMEM),
        cost_estimate=pl.CostEstimate(
            flops=4 * ROWS_DEV * width * D,
            bytes_accessed=2 * PACKED * 128 * 4 + 3 * ROWS_DEV * D * 4,
            transcendentals=0,
        ),
        name="channel",
    )(*operands)


def token_kernel(
    got_ref, dense_ref, slopes_ref, icpt_ref, chan_bias_ref, columns_ref, mid_ref, bias_ref
):
    lane = lax.broadcasted_iota(I32, (16, 128), 1) // 32
    for u in range(NTB):
        for a in range(2):
            v = [got_ref[8 * p + u, :, a * 128 : (a + 1) * 128].astype(F32) for p in range(4)]
            for bit in (1, 2):
                low = (lane & bit) == 0
                new = list(v)
                for p in range(4):
                    if p & bit == 0:
                        q = p + bit
                        new[p] = jnp.where(low, v[p], pltpu.roll(v[q], 32 * bit, 1))
                        new[q] = jnp.where(low, pltpu.roll(v[p], 128 - 32 * bit, 1), v[q])
                v = new
            for q in range(4):
                r = 4 * a + q
                columns_ref[r * 16 : (r + 1) * 16, u * 128 : (u + 1) * 128] = v[q].astype(BF16)
    pre = jnp.dot(columns_ref[...], dense_ref[...], preferred_element_type=F32)
    pre = pre.reshape(SPEC, 16, TH)
    mid, terms = relaxed(pre, slopes_ref[0], slopes_ref[1], icpt_ref[0], icpt_ref[1])
    mid_ref[...] = mid.reshape(SPEC * 16, TH).astype(BF16)
    terms = terms[:, 0:8, :] + terms[:, 8:16, :]
    terms = sum(terms[:, :, k * 128 : (k + 1) * 128] for k in range(NHB)) + chan_bias_ref[...]
    by_row = jnp.sum(jnp.sum(terms, axis=1), axis=1, keepdims=True)
    row = lax.broadcasted_iota(I32, (SPEC, 128), 0)
    lane = lax.broadcasted_iota(I32, (SPEC, 128), 1)
    line = jnp.sum(jnp.where(row == lane, by_row, 0.0), axis=0, keepdims=True)
    bias_ref[...] = jnp.broadcast_to(line[None], bias_ref.shape)


def token_mlp(got, dense_out, slopes, icpt, chan_bias):
    return pl.pallas_call(
        token_kernel,
        out_shape=(
            jax.ShapeDtypeStruct((SPEC * 16, TOK), BF16),
            jax.ShapeDtypeStruct((SPEC * 16, TH), BF16),
            jax.ShapeDtypeStruct((64, 1, 128), F32),
        ),
        compiler_params=pltpu.CompilerParams(vmem_limit_bytes=VMEM),
        name="token",
    )(got, dense_out, slopes, icpt, chan_bias)


def back_kernel(columns_ref, mid_ref, dense_ref, out_ref):
    back = jnp.dot(mid_ref[...], dense_ref[...], preferred_element_type=F32)
    out_ref[...] = (columns_ref[...].astype(F32) + back).astype(BF16)


def token_back(columns, mid, dense_in):
    return pl.pallas_call(
        back_kernel,
        out_shape=jax.ShapeDtypeStruct((SPEC * 16, TOK), BF16),
        compiler_params=pltpu.CompilerParams(vmem_limit_bytes=VMEM),
        name="back",
    )(columns, mid, dense_in)


def on_device(
    lam_out,
    q_down,
    down_scale,
    q_up,
    up_scale,
    chan_slopes,
    chan_icpt,
    tok_in_blocks,
    tok_out_blocks,
    block_cells,
    tok_slopes,
    tok_icpt,
):
    core = lax.axis_index("core").astype(I32).reshape(1)
    row = lax.axis_index("rows").astype(I32).reshape(1)
    tok_dev = lam_out.shape[0]
    slices = lax.axis_size("rows")
    ahead = [(i * 2, (i + 1) % slices * 2) for i in range(slices)]
    behind = [(i * 2 + 1, (i - 1) % slices * 2 + 1) for i in range(slices)]

    def forward(words, pairs):
        return tuple(lax.ppermute(w, ("rows", "core"), pairs) for w in words)

    own = tuple(pack(chain, core, q_down, q_up, up_scale) for chain in range(2))
    first = forward(own, ahead + behind)
    _, lam, *bounds = lax.optimization_barrier((own, lam_out, chan_slopes, chan_icpt))
    keep_part, send_part = share(
        core, row, jnp.swapaxes(lam, 0, 1), *(b.reshape(2, tok_dev, CH) for b in bounds)
    )
    words, send_part = lax.optimization_barrier((first[0], send_part))
    second = forward((words, first[1]), ahead + behind)
    other_part = lax.ppermute(send_part, "core", SWAP)
    words, other_part = lax.optimization_barrier((second[0], other_part))
    third = forward((words, second[1]), ahead + behind)
    carried = channel_part(0, core, *first, own[0], down_scale.reshape(1, D), keep_part, other_part)
    acc, chan_bias, *given = carried
    acc, chan_bias = channel_part(1, core, *second, *given, acc, chan_bias)
    far = forward(third[:1], ahead + behind)

    dense_in, dense_out = dense_blocks(block_cells, tok_in_blocks, tok_out_blocks)
    slopes = jnp.transpose(tok_slopes, (0, 2, 3, 1)).reshape(2, 16, TH)
    icpt = jnp.transpose(tok_icpt, (0, 2, 3, 1)).reshape(2, 16, TH)

    acc, chan_bias = channel_part(2, core, *third, *given, acc, chan_bias)
    keep, send, chan_bias = channel_part(3, core, *far, *given, acc, chan_bias)
    summed = (keep + lax.ppermute(send, "core", SWAP).astype(F32)).astype(BF16)
    got = lax.all_to_all(summed, ("x", "z"), 0, 0, tiled=True)
    columns, mid, own_bias = token_mlp(got, dense_out, slopes, icpt, chan_bias)
    all_bias = lax.all_to_all(own_bias, MP, 0, 0, tiled=True)
    lam_in = token_back(columns, mid, dense_in)
    lam_in = jnp.transpose(lam_in.reshape(SPEC, 16, TOK), (2, 0, 1))
    return (lam_in, jnp.sum(all_bias, axis=(0, 1))[:SPEC])


def solution(mesh):
    axes = Mesh(mesh.devices.reshape(8, 8, 4, 2), ("rows",) + MP)
    return jax.shard_map(
        on_device,
        mesh=axes,
        in_specs=(
            P(MP, "rows", None),
            P(None, "rows"),
            P(),
            P("rows", None),
            P("rows"),
            P(None, MP, "rows", None),
            P(None, MP, "rows", None),
            P(),
            P(),
            P(),
            P(None, None, "rows", MP),
            P(None, None, "rows", MP),
        ),
        out_specs=(P(None, "rows", MP), P("rows")),
        check_vma=False,
    )
```

```python
import functools

import jax
import jax.numpy as jnp
from jax import lax
from jax.experimental import pallas as pl
from jax.experimental.pallas import tpu as pltpu
from jax.sharding import Mesh
from jax.sharding import PartitionSpec as P

D = 1024
CH = 4096
TH = 512
TOK = 1024
BLK = 128
NB = 16
SPEC = 8
NHB = 4
NTB = 8
F32 = jnp.float32
BF16 = jnp.bfloat16
I32 = jnp.int32
MP = ("z", "x", "core")
SWAP = [(0, 1), (1, 0)]
VMEM = 32 * 1024 * 1024

PART = 512
CHUNK = 256
STEPS = 4
SHARED = 32
ROWS_DEV = SPEC * SHARED
PACKED = 1032
LAM_TILES = SPEC * (D // 128)
SCALE_ONE = float(2**38)


def pack_codes(parts):
    a, b, c, d = (p.astype(F32) for p in parts)
    low, high = ((y * 256.0 + (x + 128.0)).astype(I32) for x, y in ((a, b), (c, d)))
    return (low & 65535) | (high << 16)


def unpack_codes(words, m):
    if m % 2 == 0:
        codes = ((words if m == 0 else words >> 16) & 255) - 128
    else:
        codes = (words << 16 if m == 1 else words) >> 24
    return codes.astype(F32).astype(BF16)


def pack_kernel(chain, core_ref, down_hbm, up_hbm, scale_hbm, out_ref, down_ref, up_ref, scale_ref, sems):
    cut = pl.ds(pl.multiple_of((core_ref[0] ^ chain) * CHUNK, CHUNK), CHUNK)
    copies = [
        pltpu.make_async_copy(down_hbm.at[:, cut], down_ref, sems.at[0]),
        pltpu.make_async_copy(up_hbm.at[cut, :], up_ref, sems.at[1]),
        pltpu.make_async_copy(scale_hbm.at[:, cut], scale_ref, sems.at[2]),
    ]
    for copy in copies:
        copy.start()
    out_ref[1024:1032, :] = jnp.zeros((8, 128), I32)
    copies[0].wait()
    down = pack_codes([down_ref[m * 256 : (m + 1) * 256, :] for m in range(4)])
    for k in range(8):
        rows, cut = slice(k // 2 * 64, (k // 2 + 1) * 64), slice(k % 2 * 128, (k % 2 + 1) * 128)
        out_ref[k * 64 : (k + 1) * 64, :] = down[rows, cut]
    copies[1].wait()
    up = pack_codes([up_ref[m * 64 : (m + 1) * 64, :] for m in range(4)])
    for k in range(8):
        out_ref[512 + k * 64 : 512 + (k + 1) * 64, :] = up[:, k * 128 : (k + 1) * 128]
    copies[2].wait()
    scale = (scale_ref[...] * SCALE_ONE).astype(I32)
    for h in range(2):
        out_ref[1024 + h : 1025 + h, :] = scale[:, h * 128 : (h + 1) * 128]


def pack(chain, core, q_down, q_up, up_scale):
    smem, hbm, vmem = (
        pl.BlockSpec(memory_space=space) for space in (pltpu.SMEM, pltpu.HBM, pltpu.VMEM)
    )
    return pl.pallas_call(
        functools.partial(pack_kernel, chain),
        out_shape=jax.ShapeDtypeStruct((PACKED, 128), I32),
        in_specs=[smem, hbm, hbm, hbm],
        out_specs=vmem,
        scratch_shapes=[
            pltpu.VMEM((D, CHUNK), BF16),
            pltpu.VMEM((CHUNK, D), BF16),
            pltpu.VMEM((1, CHUNK), F32),
            pltpu.SemaphoreType.DMA((3,)),
        ],
        compiler_params=pltpu.CompilerParams(vmem_limit_bytes=60 * 1024 * 1024),
        name="pack",
    )(core, q_down, q_up, up_scale.reshape(1, -1))


def dense_kernel(cells_ref, in_ref, out_ref, dense_in_ref, dense_out_ref):
    dense_in_ref[...] = jnp.zeros_like(dense_in_ref)
    dense_out_ref[...] = jnp.zeros_like(dense_out_ref)
    for b in range(NB):
        h = pl.multiple_of(cells_ref[b] // NTB * BLK, BLK)
        u = pl.multiple_of(cells_ref[b] % NTB * BLK, BLK)
        dense_in_ref[pl.ds(h, BLK), pl.ds(u, BLK)] = in_ref[b]
        dense_out_ref[pl.ds(u, BLK), pl.ds(h, BLK)] = out_ref[b]


def dense_blocks(cells, in_blocks, out_blocks):
    return pl.pallas_call(
        dense_kernel,
        out_shape=(
            jax.ShapeDtypeStruct((TH, TOK), BF16),
            jax.ShapeDtypeStruct((TOK, TH), BF16),
        ),
        in_specs=[
            pl.BlockSpec(memory_space=pltpu.SMEM),
            pl.BlockSpec(memory_space=pltpu.VMEM),
            pl.BlockSpec(memory_space=pltpu.VMEM),
        ],
        out_specs=(
            pl.BlockSpec(memory_space=pltpu.VMEM),
            pl.BlockSpec(memory_space=pltpu.VMEM),
        ),
        compiler_params=pltpu.CompilerParams(vmem_limit_bytes=VMEM),
        name="dense",
    )(cells, in_blocks, out_blocks)


def relaxed(pre, lower, upper, icpt_low, icpt_high):
    pos = jnp.maximum(pre, 0.0)
    neg = jnp.minimum(pre, 0.0)
    mid = pos * lower.astype(F32) + neg * upper.astype(F32)
    return mid, pos * icpt_low.astype(F32) + neg * icpt_high.astype(F32)


def share_kernel(core_ref, row_ref, lam_ref, slopes_ref, icpt_ref, *out_refs):
    for r in range(SPEC):
        for k in range(D // 128):
            tile = lam_ref[r, :, k * 128 : (k + 1) * 128]
            for out_ref in out_refs:
                out_ref[r * (D // 128) + k] = tile
    row = row_ref[0]
    for k, out_ref in enumerate(out_refs):
        core = core_ref[0] ^ k
        for j in range(STEPS):
            if j < STEPS - 1:
                owner = row + (2 * core - 1) * (j + 1)
                cuts = [(owner, core), (owner, 1 - core)]
            else:
                cuts = [(row + STEPS, core), (row, core)]
            for h, (owner, chunk) in enumerate(cuts):
                start = pl.multiple_of((owner & 7) * PART + chunk * CHUNK, CHUNK)
                for kind in range(4):
                    ref = slopes_ref if kind < 2 else icpt_ref
                    values = ref[kind % 2, :, pl.ds(start, CHUNK)]
                    tile = LAM_TILES + (j * 4 + kind) * 4 + h * 2
                    out_ref[tile] = values[:, 0:128]
                    out_ref[tile + 1] = values[:, 128:256]


def share(core, row, by_row, slopes, icpt):
    tiles = LAM_TILES + 4 * STEPS * 4
    return pl.pallas_call(
        share_kernel,
        out_shape=(jax.ShapeDtypeStruct((tiles, 16, 128), BF16),) * 2,
        in_specs=[pl.BlockSpec(memory_space=pltpu.SMEM)] * 2
        + [pl.BlockSpec(memory_space=pltpu.VMEM)] * 3,
        compiler_params=pltpu.CompilerParams(vmem_limit_bytes=60 * 1024 * 1024),
        name="share",
    )(core, row, by_row, slopes, icpt)


def channel_kernel(step, *refs):
    first, last = step == 0, step == STEPS - 1
    count = (3, 2, 2, 1)[step]
    core_ref, words, refs = refs[0], refs[1 : 1 + count], refs[1 + count :]
    if first:
        down_scale_ref, *team, acc_ref, bias_ref, scaled_ref, bounds_ref, down, up = refs
        for k, got_ref in enumerate(team):
            start = (core_ref[0] ^ k) * 16
            for r in range(SPEC):
                rows = pl.ds(pl.multiple_of(r * SHARED + start, 16), 16)
                for c in range(D // 128):
                    cut = slice(c * 128, (c + 1) * 128)
                    lam = got_ref[r * (D // 128) + c].astype(F32)
                    scaled_ref[rows, cut] = (lam * down_scale_ref[:, cut]).astype(BF16)
                    acc_ref[rows, cut] = 0.5 * lam
            rows = pl.ds(pl.multiple_of(start, 16), 16)
            for i in range(STEPS * 4):
                for h in range(4):
                    tile = got_ref[LAM_TILES + i * 4 + h]
                    bounds_ref[i // 4, i % 4, rows, h * 128 : (h + 1) * 128] = tile
        acc_in, bias_in = acc_ref, None
    else:
        scaled_ref, bounds_ref, acc_in, bias_in, *outs, down, up = refs
    words = [w[...] for w in words]
    for h, chunk in enumerate(words):
        for m in range(4):
            for k in range(8):
                rows = m * 256 + k // 2 * 64
                cut = h * CHUNK + k % 2 * 128
                codes = unpack_codes(chunk[k * 64 : (k + 1) * 64], m)
                down[rows : rows + 64, cut : cut + 128] = codes
                rows = h * CHUNK + m * 64
                codes = unpack_codes(chunk[512 + k * 64 : 512 + (k + 1) * 64], m)
                up[rows : rows + 64, k * 128 : (k + 1) * 128] = codes
    scale = [chunk[1024 + h : 1025 + h] for chunk in words for h in range(2)]
    scale = jnp.concatenate(scale, axis=1).astype(F32) * (1.0 / SCALE_ONE)
    pre = jnp.dot(scaled_ref[...], down[...], preferred_element_type=F32)
    width = count * CHUNK
    pre = pre.reshape(SPEC, SHARED, width)
    if first:
        bounds = [
            jnp.concatenate([bounds_ref[0, kind], bounds_ref[STEPS - 1, kind, :, CHUNK:PART]], axis=1)
            for kind in range(4)
        ]
    else:
        bounds = [bounds_ref[step, kind, :, 0:width] for kind in range(4)]
    mid, terms = relaxed(pre, *bounds)
    terms = jnp.sum(terms.reshape(SPEC, SHARED // 8, 8, width), axis=1)
    bias = sum(terms[:, :, k * 128 : (k + 1) * 128] for k in range(width // 128))
    weighted = (mid.reshape(ROWS_DEV, width) * scale).astype(BF16)
    part = jnp.dot(weighted, up[...], preferred_element_type=F32)
    total = acc_in[...] + part
    if not first:
        bias = bias + bias_in[...]
    if last:
        keep_ref, send_ref, bias_ref = outs
        own = core_ref[0] == 0
        turned = total.T.reshape(8, 4, 2, 16, ROWS_DEV)
        for x in range(4):
            chips = slice(x * 8, (x + 1) * 8)
            keep_ref[chips] = jnp.where(own, turned[:, x, 0], turned[:, x, 1])
            send_ref[chips] = jnp.where(own, turned[:, x, 1], turned[:, x, 0]).astype(BF16)
    else:
        if not first:
            acc_ref, bias_ref = outs
        acc_ref[...] = total
    bias_ref[...] = bias


def channel_part(step, core, *rest):
    acc_shape = jax.ShapeDtypeStruct((ROWS_DEV, D), F32)
    bias_shape = jax.ShapeDtypeStruct((SPEC, 8, 128), F32)
    operands = [core, *rest]
    width = (3, 2, 2, 1)[step] * CHUNK
    aliases = {}
    if step == 0:
        scaled_shape = jax.ShapeDtypeStruct((ROWS_DEV, D), BF16)
        bounds_shape = jax.ShapeDtypeStruct((STEPS, 4, SHARED, PART), BF16)
        out_shape = (acc_shape, bias_shape, scaled_shape, bounds_shape)
    elif step == STEPS - 1:
        out_shape = (
            jax.ShapeDtypeStruct((32, 16, ROWS_DEV), F32),
            jax.ShapeDtypeStruct((32, 16, ROWS_DEV), BF16),
            bias_shape,
        )
    else:
        out_shape = (acc_shape, bias_shape)
        aliases = {len(operands) - 2: 0, len(operands) - 1: 1}
    smem, vmem = pl.BlockSpec(memory_space=pltpu.SMEM), pl.BlockSpec(memory_space=pltpu.VMEM)
    return pl.pallas_call(
        functools.partial(channel_kernel, step),
        out_shape=out_shape,
        in_specs=[smem] + [vmem] * (len(operands) - 1),
        out_specs=(vmem,) * len(out_shape),
        scratch_shapes=[pltpu.VMEM((D, width), BF16), pltpu.VMEM((width, D), BF16)],
        input_output_aliases=aliases,
        compiler_params=pltpu.CompilerParams(vmem_limit_bytes=VMEM),
        cost_estimate=pl.CostEstimate(
            flops=4 * ROWS_DEV * width * D,
            bytes_accessed=2 * PACKED * 128 * 4 + 3 * ROWS_DEV * D * 4,
            transcendentals=0,
        ),
        name="channel",
    )(*operands)


def token_kernel(
    got_ref, dense_ref, slopes_ref, icpt_ref, chan_bias_ref, columns_ref, mid_ref, bias_ref
):
    lane = lax.broadcasted_iota(I32, (16, 128), 1) // 32
    for u in range(NTB):
        for a in range(2):
            v = [got_ref[8 * p + u, :, a * 128 : (a + 1) * 128].astype(F32) for p in range(4)]
            for bit in (1, 2):
                low = (lane & bit) == 0
                new = list(v)
                for p in range(4):
                    if p & bit == 0:
                        q = p + bit
                        new[p] = jnp.where(low, v[p], pltpu.roll(v[q], 32 * bit, 1))
                        new[q] = jnp.where(low, pltpu.roll(v[p], 128 - 32 * bit, 1), v[q])
                v = new
            for q in range(4):
                r = 4 * a + q
                columns_ref[r * 16 : (r + 1) * 16, u * 128 : (u + 1) * 128] = v[q].astype(BF16)
    pre = jnp.dot(columns_ref[...], dense_ref[...], preferred_element_type=F32)
    pre = pre.reshape(SPEC, 16, TH)
    mid, terms = relaxed(pre, slopes_ref[0], slopes_ref[1], icpt_ref[0], icpt_ref[1])
    mid_ref[...] = mid.reshape(SPEC * 16, TH).astype(BF16)
    terms = terms[:, 0:8, :] + terms[:, 8:16, :]
    terms = sum(terms[:, :, k * 128 : (k + 1) * 128] for k in range(NHB)) + chan_bias_ref[...]
    by_row = jnp.sum(jnp.sum(terms, axis=1), axis=1, keepdims=True)
    row = lax.broadcasted_iota(I32, (SPEC, 128), 0)
    lane = lax.broadcasted_iota(I32, (SPEC, 128), 1)
    line = jnp.sum(jnp.where(row == lane, by_row, 0.0), axis=0, keepdims=True)
    bias_ref[...] = jnp.broadcast_to(line[None], bias_ref.shape)


def token_mlp(got, dense_out, slopes, icpt, chan_bias):
    return pl.pallas_call(
        token_kernel,
        out_shape=(
            jax.ShapeDtypeStruct((SPEC * 16, TOK), BF16),
            jax.ShapeDtypeStruct((SPEC * 16, TH), BF16),
            jax.ShapeDtypeStruct((64, 1, 128), F32),
        ),
        compiler_params=pltpu.CompilerParams(vmem_limit_bytes=VMEM),
        name="token",
    )(got, dense_out, slopes, icpt, chan_bias)


def back_kernel(columns_ref, mid_ref, dense_ref, out_ref):
    back = jnp.dot(mid_ref[...], dense_ref[...], preferred_element_type=F32)
    out_ref[...] = (columns_ref[...].astype(F32) + back).astype(BF16)


def token_back(columns, mid, dense_in):
    return pl.pallas_call(
        back_kernel,
        out_shape=jax.ShapeDtypeStruct((SPEC * 16, TOK), BF16),
        compiler_params=pltpu.CompilerParams(vmem_limit_bytes=VMEM),
        name="back",
    )(columns, mid, dense_in)


def on_device(
    lam_out,
    q_down,
    down_scale,
    q_up,
    up_scale,
    chan_slopes,
    chan_icpt,
    tok_in_blocks,
    tok_out_blocks,
    block_cells,
    tok_slopes,
    tok_icpt,
):
    core = lax.axis_index("core").astype(I32).reshape(1)
    row = lax.axis_index("rows").astype(I32).reshape(1)
    tok_dev = lam_out.shape[0]
    slices = lax.axis_size("rows")
    ahead = [(i * 2, (i + 1) % slices * 2) for i in range(slices)]
    behind = [(i * 2 + 1, (i - 1) % slices * 2 + 1) for i in range(slices)]

    def forward(words, pairs):
        return tuple(lax.ppermute(w, ("rows", "core"), pairs) for w in words)

    own = tuple(pack(chain, core, q_down, q_up, up_scale) for chain in range(2))
    first = forward(own, ahead + behind)
    _, lam, *bounds = lax.optimization_barrier((own, lam_out, chan_slopes, chan_icpt))
    keep_part, send_part = share(
        core, row, jnp.swapaxes(lam, 0, 1), *(b.reshape(2, tok_dev, CH) for b in bounds)
    )
    words, send_part = lax.optimization_barrier((first[0], send_part))
    second = forward((words, first[1]), ahead + behind)
    other_part = lax.ppermute(send_part, "core", SWAP)
    words, other_part = lax.optimization_barrier((second[0], other_part))
    third = forward((words, second[1]), ahead + behind)
    carried = channel_part(0, core, *first, own[0], down_scale.reshape(1, D), keep_part, other_part)
    acc, chan_bias, *given = carried
    acc, chan_bias = channel_part(1, core, *second, *given, acc, chan_bias)
    far = forward(third[:1], ahead + behind)

    dense_in, dense_out = dense_blocks(block_cells, tok_in_blocks, tok_out_blocks)
    slopes = jnp.transpose(tok_slopes, (0, 2, 3, 1)).reshape(2, 16, TH)
    icpt = jnp.transpose(tok_icpt, (0, 2, 3, 1)).reshape(2, 16, TH)

    acc, chan_bias = channel_part(2, core, *third, *given, acc, chan_bias)
    keep, send, chan_bias = channel_part(3, core, *far, *given, acc, chan_bias)
    summed = (keep + lax.ppermute(send, "core", SWAP).astype(F32)).astype(BF16)
    got = lax.all_to_all(summed, ("x", "z"), 0, 0, tiled=True)
    columns, mid, own_bias = token_mlp(got, dense_out, slopes, icpt, chan_bias)
    all_bias = lax.all_to_all(own_bias, ("x", "z", "core"), 0, 0, tiled=True)
    lam_in = token_back(columns, mid, dense_in)
    lam_in = jnp.transpose(lam_in.reshape(SPEC, 16, TOK), (2, 0, 1))
    return (lam_in, jnp.sum(all_bias, axis=(0, 1))[:SPEC])


def solution(mesh):
    axes = Mesh(mesh.devices.reshape(8, 8, 4, 2), ("rows",) + MP)
    return jax.shard_map(
        on_device,
        mesh=axes,
        in_specs=(
            P(MP, "rows", None),
            P(None, "rows"),
            P(),
            P("rows", None),
            P("rows"),
            P(None, MP, "rows", None),
            P(None, MP, "rows", None),
            P(),
            P(),
            P(),
            P(None, None, "rows", MP),
            P(None, None, "rows", MP),
        ),
        out_specs=(P(None, "rows", MP), P("rows")),
        check_vma=False,
    )
```

```python
import functools

import jax
import jax.numpy as jnp
from jax import lax
from jax.experimental import pallas as pl
from jax.experimental.pallas import tpu as pltpu
from jax.sharding import Mesh
from jax.sharding import PartitionSpec as P

D = 1024
CH = 4096
TH = 512
TOK = 1024
BLK = 128
NB = 16
SPEC = 8
NHB = 4
NTB = 8
F32 = jnp.float32
BF16 = jnp.bfloat16
I32 = jnp.int32
MP = ("z", "x", "core")
SWAP = [(0, 1), (1, 0)]
VMEM = 32 * 1024 * 1024

PART = 512
CHUNK = 256
STEPS = 4
SHARED = 32
ROWS_DEV = SPEC * SHARED
PACKED = 1032
LAM_TILES = SPEC * (D // 128)
SCALE_ONE = float(2**38)


def pack_codes(parts):
    a, b, c, d = (p.astype(F32) for p in parts)
    low, high = ((y * 256.0 + (x + 128.0)).astype(I32) for x, y in ((a, b), (c, d)))
    return (low & 65535) | (high << 16)


def unpack_codes(words, m):
    if m % 2 == 0:
        codes = ((words if m == 0 else words >> 16) & 255) - 128
    else:
        codes = (words << 16 if m == 1 else words) >> 24
    return codes.astype(F32).astype(BF16)


def pack_kernel(chain, core_ref, down_hbm, up_hbm, scale_hbm, out_ref, down_ref, up_ref, scale_ref, sems):
    cut = pl.ds(pl.multiple_of((core_ref[0] ^ chain) * CHUNK, CHUNK), CHUNK)
    base = (core_ref[0] ^ chain) * CHUNK
    downs, ups = [], []
    for m in range(4):
        rows = pl.ds(m * 256, 256)
        downs.append(
            pltpu.make_async_copy(down_hbm.at[rows, cut], down_ref.at[rows, :], sems.at[m])
        )
    for m in range(4):
        rows, source = pl.ds(m * 64, 64), pl.ds(pl.multiple_of(base + m * 64, 64), 64)
        ups.append(
            pltpu.make_async_copy(up_hbm.at[source, :], up_ref.at[rows, :], sems.at[4 + m])
        )
    scale_copy = pltpu.make_async_copy(scale_hbm.at[:, cut], scale_ref, sems.at[8])
    for copy in (*downs, *ups, scale_copy):
        copy.start()
    out_ref[1024:1032, :] = jnp.zeros((8, 128), I32)
    for copy in downs:
        copy.wait()
    down = pack_codes([down_ref[m * 256 : (m + 1) * 256, :] for m in range(4)])
    for k in range(8):
        rows, cut = slice(k // 2 * 64, (k // 2 + 1) * 64), slice(k % 2 * 128, (k % 2 + 1) * 128)
        out_ref[k * 64 : (k + 1) * 64, :] = down[rows, cut]
    for copy in ups:
        copy.wait()
    up = pack_codes([up_ref[m * 64 : (m + 1) * 64, :] for m in range(4)])
    for k in range(8):
        out_ref[512 + k * 64 : 512 + (k + 1) * 64, :] = up[:, k * 128 : (k + 1) * 128]
    scale_copy.wait()
    scale = (scale_ref[...] * SCALE_ONE).astype(I32)
    for h in range(2):
        out_ref[1024 + h : 1025 + h, :] = scale[:, h * 128 : (h + 1) * 128]


def pack(chain, core, q_down, q_up, up_scale):
    smem, hbm, vmem = (
        pl.BlockSpec(memory_space=space) for space in (pltpu.SMEM, pltpu.HBM, pltpu.VMEM)
    )
    return pl.pallas_call(
        functools.partial(pack_kernel, chain),
        out_shape=jax.ShapeDtypeStruct((PACKED, 128), I32),
        in_specs=[smem, hbm, hbm, hbm],
        out_specs=vmem,
        scratch_shapes=[
            pltpu.VMEM((D, CHUNK), BF16),
            pltpu.VMEM((CHUNK, D), BF16),
            pltpu.VMEM((1, CHUNK), F32),
            pltpu.SemaphoreType.DMA((9,)),
        ],
        compiler_params=pltpu.CompilerParams(vmem_limit_bytes=60 * 1024 * 1024),
        name="pack",
    )(core, q_down, q_up, up_scale.reshape(1, -1))


def dense_kernel(cells_ref, in_ref, out_ref, dense_in_ref, dense_out_ref):
    dense_in_ref[...] = jnp.zeros_like(dense_in_ref)
    dense_out_ref[...] = jnp.zeros_like(dense_out_ref)
    for b in range(NB):
        h = pl.multiple_of(cells_ref[b] // NTB * BLK, BLK)
        u = pl.multiple_of(cells_ref[b] % NTB * BLK, BLK)
        dense_in_ref[pl.ds(h, BLK), pl.ds(u, BLK)] = in_ref[b]
        dense_out_ref[pl.ds(u, BLK), pl.ds(h, BLK)] = out_ref[b]


def dense_blocks(cells, in_blocks, out_blocks):
    return pl.pallas_call(
        dense_kernel,
        out_shape=(
            jax.ShapeDtypeStruct((TH, TOK), BF16),
            jax.ShapeDtypeStruct((TOK, TH), BF16),
        ),
        in_specs=[
            pl.BlockSpec(memory_space=pltpu.SMEM),
            pl.BlockSpec(memory_space=pltpu.VMEM),
            pl.BlockSpec(memory_space=pltpu.VMEM),
        ],
        out_specs=(
            pl.BlockSpec(memory_space=pltpu.VMEM),
            pl.BlockSpec(memory_space=pltpu.VMEM),
        ),
        compiler_params=pltpu.CompilerParams(vmem_limit_bytes=VMEM),
        name="dense",
    )(cells, in_blocks, out_blocks)


def relaxed(pre, lower, upper, icpt_low, icpt_high):
    pos = jnp.maximum(pre, 0.0)
    neg = jnp.minimum(pre, 0.0)
    mid = pos * lower.astype(F32) + neg * upper.astype(F32)
    return mid, pos * icpt_low.astype(F32) + neg * icpt_high.astype(F32)


def share_kernel(core_ref, row_ref, lam_ref, slopes_ref, icpt_ref, *out_refs):
    for r in range(SPEC):
        for k in range(D // 128):
            tile = lam_ref[r, :, k * 128 : (k + 1) * 128]
            for out_ref in out_refs:
                out_ref[r * (D // 128) + k] = tile
    row = row_ref[0]
    for k, out_ref in enumerate(out_refs):
        core = core_ref[0] ^ k
        for j in range(STEPS):
            if j < STEPS - 1:
                owner = row + (2 * core - 1) * (j + 1)
                cuts = [(owner, core), (owner, 1 - core)]
            else:
                cuts = [(row + STEPS, core), (row, core)]
            for h, (owner, chunk) in enumerate(cuts):
                start = pl.multiple_of((owner & 7) * PART + chunk * CHUNK, CHUNK)
                for kind in range(4):
                    ref = slopes_ref if kind < 2 else icpt_ref
                    values = ref[kind % 2, :, pl.ds(start, CHUNK)]
                    tile = LAM_TILES + (j * 4 + kind) * 4 + h * 2
                    out_ref[tile] = values[:, 0:128]
                    out_ref[tile + 1] = values[:, 128:256]


def share(core, row, by_row, slopes, icpt):
    tiles = LAM_TILES + 4 * STEPS * 4
    return pl.pallas_call(
        share_kernel,
        out_shape=(jax.ShapeDtypeStruct((tiles, 16, 128), BF16),) * 2,
        in_specs=[pl.BlockSpec(memory_space=pltpu.SMEM)] * 2
        + [pl.BlockSpec(memory_space=pltpu.VMEM)] * 3,
        compiler_params=pltpu.CompilerParams(vmem_limit_bytes=60 * 1024 * 1024),
        name="share",
    )(core, row, by_row, slopes, icpt)


def channel_kernel(step, *refs):
    first, last = step == 0, step == STEPS - 1
    count = (3, 2, 2, 1)[step]
    core_ref, words, refs = refs[0], refs[1 : 1 + count], refs[1 + count :]
    if first:
        down_scale_ref, *team, acc_ref, bias_ref, scaled_ref, bounds_ref, down, up = refs
        for k, got_ref in enumerate(team):
            start = (core_ref[0] ^ k) * 16
            for r in range(SPEC):
                rows = pl.ds(pl.multiple_of(r * SHARED + start, 16), 16)
                for c in range(D // 128):
                    cut = slice(c * 128, (c + 1) * 128)
                    lam = got_ref[r * (D // 128) + c].astype(F32)
                    scaled_ref[rows, cut] = (lam * down_scale_ref[:, cut]).astype(BF16)
                    acc_ref[rows, cut] = 0.5 * lam
            rows = pl.ds(pl.multiple_of(start, 16), 16)
            for i in range(STEPS * 4):
                for h in range(4):
                    tile = got_ref[LAM_TILES + i * 4 + h]
                    bounds_ref[i // 4, i % 4, rows, h * 128 : (h + 1) * 128] = tile
        acc_in, bias_in = acc_ref, None
    else:
        scaled_ref, bounds_ref, acc_in, bias_in, *outs, down, up = refs
    words = [w[...] for w in words]
    for h, chunk in enumerate(words):
        for m in range(4):
            for k in range(8):
                rows = m * 256 + k // 2 * 64
                cut = h * CHUNK + k % 2 * 128
                codes = unpack_codes(chunk[k * 64 : (k + 1) * 64], m)
                down[rows : rows + 64, cut : cut + 128] = codes
                rows = h * CHUNK + m * 64
                codes = unpack_codes(chunk[512 + k * 64 : 512 + (k + 1) * 64], m)
                up[rows : rows + 64, k * 128 : (k + 1) * 128] = codes
    scale = [chunk[1024 + h : 1025 + h] for chunk in words for h in range(2)]
    scale = jnp.concatenate(scale, axis=1).astype(F32) * (1.0 / SCALE_ONE)
    pre = jnp.dot(scaled_ref[...], down[...], preferred_element_type=F32)
    width = count * CHUNK
    pre = pre.reshape(SPEC, SHARED, width)
    if first:
        bounds = [
            jnp.concatenate([bounds_ref[0, kind], bounds_ref[STEPS - 1, kind, :, CHUNK:PART]], axis=1)
            for kind in range(4)
        ]
    else:
        bounds = [bounds_ref[step, kind, :, 0:width] for kind in range(4)]
    mid, terms = relaxed(pre, *bounds)
    terms = jnp.sum(terms.reshape(SPEC, SHARED // 8, 8, width), axis=1)
    bias = sum(terms[:, :, k * 128 : (k + 1) * 128] for k in range(width // 128))
    weighted = (mid.reshape(ROWS_DEV, width) * scale).astype(BF16)
    part = jnp.dot(weighted, up[...], preferred_element_type=F32)
    total = acc_in[...] + part
    if not first:
        bias = bias + bias_in[...]
    if last:
        keep_ref, send_ref, bias_ref = outs
        own = core_ref[0] == 0
        turned = total.T.reshape(8, 4, 2, 16, ROWS_DEV)
        for x in range(4):
            chips = slice(x * 8, (x + 1) * 8)
            keep_ref[chips] = jnp.where(own, turned[:, x, 0], turned[:, x, 1])
            send_ref[chips] = jnp.where(own, turned[:, x, 1], turned[:, x, 0]).astype(BF16)
    else:
        if not first:
            acc_ref, bias_ref = outs
        acc_ref[...] = total
    bias_ref[...] = bias


def channel_part(step, core, *rest):
    acc_shape = jax.ShapeDtypeStruct((ROWS_DEV, D), F32)
    bias_shape = jax.ShapeDtypeStruct((SPEC, 8, 128), F32)
    operands = [core, *rest]
    width = (3, 2, 2, 1)[step] * CHUNK
    aliases = {}
    if step == 0:
        scaled_shape = jax.ShapeDtypeStruct((ROWS_DEV, D), BF16)
        bounds_shape = jax.ShapeDtypeStruct((STEPS, 4, SHARED, PART), BF16)
        out_shape = (acc_shape, bias_shape, scaled_shape, bounds_shape)
    elif step == STEPS - 1:
        out_shape = (
            jax.ShapeDtypeStruct((32, 16, ROWS_DEV), F32),
            jax.ShapeDtypeStruct((32, 16, ROWS_DEV), BF16),
            bias_shape,
        )
    else:
        out_shape = (acc_shape, bias_shape)
        aliases = {len(operands) - 2: 0, len(operands) - 1: 1}
    smem, vmem = pl.BlockSpec(memory_space=pltpu.SMEM), pl.BlockSpec(memory_space=pltpu.VMEM)
    return pl.pallas_call(
        functools.partial(channel_kernel, step),
        out_shape=out_shape,
        in_specs=[smem] + [vmem] * (len(operands) - 1),
        out_specs=(vmem,) * len(out_shape),
        scratch_shapes=[pltpu.VMEM((D, width), BF16), pltpu.VMEM((width, D), BF16)],
        input_output_aliases=aliases,
        compiler_params=pltpu.CompilerParams(vmem_limit_bytes=VMEM),
        cost_estimate=pl.CostEstimate(
            flops=4 * ROWS_DEV * width * D,
            bytes_accessed=2 * PACKED * 128 * 4 + 3 * ROWS_DEV * D * 4,
            transcendentals=0,
        ),
        name="channel",
    )(*operands)


def token_kernel(
    got_ref, dense_ref, slopes_ref, icpt_ref, chan_bias_ref, columns_ref, mid_ref, bias_ref
):
    lane = lax.broadcasted_iota(I32, (16, 128), 1) // 32
    for u in range(NTB):
        for a in range(2):
            v = [got_ref[8 * p + u, :, a * 128 : (a + 1) * 128].astype(F32) for p in range(4)]
            for bit in (1, 2):
                low = (lane & bit) == 0
                new = list(v)
                for p in range(4):
                    if p & bit == 0:
                        q = p + bit
                        new[p] = jnp.where(low, v[p], pltpu.roll(v[q], 32 * bit, 1))
                        new[q] = jnp.where(low, pltpu.roll(v[p], 128 - 32 * bit, 1), v[q])
                v = new
            for q in range(4):
                r = 4 * a + q
                columns_ref[r * 16 : (r + 1) * 16, u * 128 : (u + 1) * 128] = v[q].astype(BF16)
    pre = jnp.dot(columns_ref[...], dense_ref[...], preferred_element_type=F32)
    pre = pre.reshape(SPEC, 16, TH)
    mid, terms = relaxed(pre, slopes_ref[0], slopes_ref[1], icpt_ref[0], icpt_ref[1])
    mid_ref[...] = mid.reshape(SPEC * 16, TH).astype(BF16)
    terms = terms[:, 0:8, :] + terms[:, 8:16, :]
    terms = sum(terms[:, :, k * 128 : (k + 1) * 128] for k in range(NHB)) + chan_bias_ref[...]
    by_row = jnp.sum(jnp.sum(terms, axis=1), axis=1, keepdims=True)
    row = lax.broadcasted_iota(I32, (SPEC, 128), 0)
    lane = lax.broadcasted_iota(I32, (SPEC, 128), 1)
    line = jnp.sum(jnp.where(row == lane, by_row, 0.0), axis=0, keepdims=True)
    bias_ref[...] = jnp.broadcast_to(line[None], bias_ref.shape)


def token_mlp(got, dense_out, slopes, icpt, chan_bias):
    return pl.pallas_call(
        token_kernel,
        out_shape=(
            jax.ShapeDtypeStruct((SPEC * 16, TOK), BF16),
            jax.ShapeDtypeStruct((SPEC * 16, TH), BF16),
            jax.ShapeDtypeStruct((64, 1, 128), F32),
        ),
        compiler_params=pltpu.CompilerParams(vmem_limit_bytes=VMEM),
        name="token",
    )(got, dense_out, slopes, icpt, chan_bias)


def back_kernel(columns_ref, mid_ref, dense_ref, out_ref):
    back = jnp.dot(mid_ref[...], dense_ref[...], preferred_element_type=F32)
    out_ref[...] = (columns_ref[...].astype(F32) + back).astype(BF16)


def token_back(columns, mid, dense_in):
    return pl.pallas_call(
        back_kernel,
        out_shape=jax.ShapeDtypeStruct((SPEC * 16, TOK), BF16),
        compiler_params=pltpu.CompilerParams(vmem_limit_bytes=VMEM),
        name="back",
    )(columns, mid, dense_in)


def on_device(
    lam_out,
    q_down,
    down_scale,
    q_up,
    up_scale,
    chan_slopes,
    chan_icpt,
    tok_in_blocks,
    tok_out_blocks,
    block_cells,
    tok_slopes,
    tok_icpt,
):
    core = lax.axis_index("core").astype(I32).reshape(1)
    row = lax.axis_index("rows").astype(I32).reshape(1)
    tok_dev = lam_out.shape[0]
    slices = lax.axis_size("rows")
    ahead = [(i * 2, (i + 1) % slices * 2) for i in range(slices)]
    behind = [(i * 2 + 1, (i - 1) % slices * 2 + 1) for i in range(slices)]

    def forward(words, pairs):
        return tuple(lax.ppermute(w, ("rows", "core"), pairs) for w in words)

    own = tuple(pack(chain, core, q_down, q_up, up_scale) for chain in range(2))
    first = forward(own, ahead + behind)
    _, lam, *bounds = lax.optimization_barrier((own, lam_out, chan_slopes, chan_icpt))
    keep_part, send_part = share(
        core, row, jnp.swapaxes(lam, 0, 1), *(b.reshape(2, tok_dev, CH) for b in bounds)
    )
    words, send_part = lax.optimization_barrier((first[0], send_part))
    second = forward((words, first[1]), ahead + behind)
    other_part = lax.ppermute(send_part, "core", SWAP)
    words, other_part = lax.optimization_barrier((second[0], other_part))
    third = forward((words, second[1]), ahead + behind)
    carried = channel_part(0, core, *first, own[0], down_scale.reshape(1, D), keep_part, other_part)
    acc, chan_bias, *given = carried
    acc, chan_bias = channel_part(1, core, *second, *given, acc, chan_bias)
    far = forward(third[:1], ahead + behind)

    dense_in, dense_out = dense_blocks(block_cells, tok_in_blocks, tok_out_blocks)
    slopes = jnp.transpose(tok_slopes, (0, 2, 3, 1)).reshape(2, 16, TH)
    icpt = jnp.transpose(tok_icpt, (0, 2, 3, 1)).reshape(2, 16, TH)

    acc, chan_bias = channel_part(2, core, *third, *given, acc, chan_bias)
    keep, send, chan_bias = channel_part(3, core, *far, *given, acc, chan_bias)
    summed = (keep + lax.ppermute(send, "core", SWAP).astype(F32)).astype(BF16)
    got = lax.all_to_all(summed, ("x", "z"), 0, 0, tiled=True)
    columns, mid, own_bias = token_mlp(got, dense_out, slopes, icpt, chan_bias)
    all_bias = lax.all_to_all(own_bias, ("x", "z", "core"), 0, 0, tiled=True)
    lam_in = token_back(columns, mid, dense_in)
    lam_in = jnp.transpose(lam_in.reshape(SPEC, 16, TOK), (2, 0, 1))
    return (lam_in, jnp.sum(all_bias, axis=(0, 1))[:SPEC])


def solution(mesh):
    axes = Mesh(mesh.devices.reshape(8, 8, 4, 2), ("rows",) + MP)
    return jax.shard_map(
        on_device,
        mesh=axes,
        in_specs=(
            P(MP, "rows", None),
            P(None, "rows"),
            P(),
            P("rows", None),
            P("rows"),
            P(None, MP, "rows", None),
            P(None, MP, "rows", None),
            P(),
            P(),
            P(),
            P(None, None, "rows", MP),
            P(None, None, "rows", MP),
        ),
        out_specs=(P(None, "rows", MP), P("rows")),
        check_vma=False,
    )
```

```python
import functools

import jax
import jax.numpy as jnp
from jax import lax
from jax.experimental import pallas as pl
from jax.experimental.pallas import tpu as pltpu
from jax.sharding import Mesh
from jax.sharding import PartitionSpec as P

D = 1024
CH = 4096
TH = 512
TOK = 1024
BLK = 128
NB = 16
SPEC = 8
NHB = 4
NTB = 8
F32 = jnp.float32
BF16 = jnp.bfloat16
I32 = jnp.int32
MP = ("z", "x", "core")
SWAP = [(0, 1), (1, 0)]
VMEM = 32 * 1024 * 1024

PART = 512
CHUNK = 256
STEPS = 4
SHARED = 32
ROWS_DEV = SPEC * SHARED
PACKED = 1032
LAM_TILES = SPEC * (D // 128)
SCALE_ONE = float(2**38)


def pack_codes(parts):
    a, b, c, d = (p.astype(F32).astype(I32) for p in parts)
    return (a & 255) | ((b & 255) << 8) | ((c & 255) << 16) | (d << 24)


def unpack_codes(words, m):
    shifted = words << (24 - 8 * m) if m < 3 else words
    return (shifted >> 24).astype(F32).astype(BF16)


def pack_kernel(chain, core_ref, down_hbm, up_hbm, scale_hbm, out_ref, down_ref, up_ref, scale_ref, sems):
    cut = pl.ds(pl.multiple_of((core_ref[0] ^ chain) * CHUNK, CHUNK), CHUNK)
    copies = [
        pltpu.make_async_copy(down_hbm.at[:, cut], down_ref, sems.at[0]),
        pltpu.make_async_copy(up_hbm.at[cut, :], up_ref, sems.at[1]),
        pltpu.make_async_copy(scale_hbm.at[:, cut], scale_ref, sems.at[2]),
    ]
    for copy in copies:
        copy.start()
    out_ref[1024:1032, :] = jnp.zeros((8, 128), I32)
    copies[0].wait()
    down = pack_codes([down_ref[m * 256 : (m + 1) * 256, :] for m in range(4)])
    for k in range(8):
        rows, cut = slice(k // 2 * 64, (k // 2 + 1) * 64), slice(k % 2 * 128, (k % 2 + 1) * 128)
        out_ref[k * 64 : (k + 1) * 64, :] = down[rows, cut]
    copies[1].wait()
    up = pack_codes([up_ref[m * 64 : (m + 1) * 64, :] for m in range(4)])
    for k in range(8):
        out_ref[512 + k * 64 : 512 + (k + 1) * 64, :] = up[:, k * 128 : (k + 1) * 128]
    copies[2].wait()
    scale = (scale_ref[...] * SCALE_ONE).astype(I32)
    for h in range(2):
        out_ref[1024 + h : 1025 + h, :] = scale[:, h * 128 : (h + 1) * 128]


def pack(chain, core, q_down, q_up, up_scale):
    smem, hbm, vmem = (
        pl.BlockSpec(memory_space=space) for space in (pltpu.SMEM, pltpu.HBM, pltpu.VMEM)
    )
    return pl.pallas_call(
        functools.partial(pack_kernel, chain),
        out_shape=jax.ShapeDtypeStruct((PACKED, 128), I32),
        in_specs=[smem, hbm, hbm, hbm],
        out_specs=vmem,
        scratch_shapes=[
            pltpu.VMEM((D, CHUNK), BF16),
            pltpu.VMEM((CHUNK, D), BF16),
            pltpu.VMEM((1, CHUNK), F32),
            pltpu.SemaphoreType.DMA((3,)),
        ],
        compiler_params=pltpu.CompilerParams(vmem_limit_bytes=60 * 1024 * 1024),
        name="pack",
    )(core, q_down, q_up, up_scale.reshape(1, -1))


def dense_kernel(cells_ref, in_ref, out_ref, dense_in_ref, dense_out_ref):
    dense_in_ref[...] = jnp.zeros_like(dense_in_ref)
    dense_out_ref[...] = jnp.zeros_like(dense_out_ref)
    for b in range(NB):
        h = pl.multiple_of(cells_ref[b] // NTB * BLK, BLK)
        u = pl.multiple_of(cells_ref[b] % NTB * BLK, BLK)
        dense_in_ref[pl.ds(h, BLK), pl.ds(u, BLK)] = in_ref[b]
        dense_out_ref[pl.ds(u, BLK), pl.ds(h, BLK)] = out_ref[b]


def dense_blocks(cells, in_blocks, out_blocks):
    return pl.pallas_call(
        dense_kernel,
        out_shape=(
            jax.ShapeDtypeStruct((TH, TOK), BF16),
            jax.ShapeDtypeStruct((TOK, TH), BF16),
        ),
        in_specs=[
            pl.BlockSpec(memory_space=pltpu.SMEM),
            pl.BlockSpec(memory_space=pltpu.VMEM),
            pl.BlockSpec(memory_space=pltpu.VMEM),
        ],
        out_specs=(
            pl.BlockSpec(memory_space=pltpu.VMEM),
            pl.BlockSpec(memory_space=pltpu.VMEM),
        ),
        compiler_params=pltpu.CompilerParams(vmem_limit_bytes=VMEM),
        name="dense",
    )(cells, in_blocks, out_blocks)


def relaxed(pre, lower, upper, icpt_low, icpt_high):
    pos = jnp.maximum(pre, 0.0)
    neg = jnp.minimum(pre, 0.0)
    mid = pos * lower.astype(F32) + neg * upper.astype(F32)
    return mid, pos * icpt_low.astype(F32) + neg * icpt_high.astype(F32)


def share_kernel(core_ref, row_ref, lam_ref, slopes_ref, icpt_ref, *out_refs):
    for r in range(SPEC):
        for k in range(D // 128):
            tile = lam_ref[r, :, k * 128 : (k + 1) * 128]
            for out_ref in out_refs:
                out_ref[r * (D // 128) + k] = tile
    row = row_ref[0]
    for k, out_ref in enumerate(out_refs):
        core = core_ref[0] ^ k
        for j in range(STEPS):
            if j < STEPS - 1:
                owner = row + (2 * core - 1) * (j + 1)
                cuts = [(owner, core), (owner, 1 - core)]
            else:
                cuts = [(row + STEPS, core), (row, core)]
            for h, (owner, chunk) in enumerate(cuts):
                start = pl.multiple_of((owner & 7) * PART + chunk * CHUNK, CHUNK)
                for kind in range(4):
                    ref = slopes_ref if kind < 2 else icpt_ref
                    values = ref[kind % 2, :, pl.ds(start, CHUNK)]
                    tile = LAM_TILES + (j * 4 + kind) * 4 + h * 2
                    out_ref[tile] = values[:, 0:128]
                    out_ref[tile + 1] = values[:, 128:256]


def share(core, row, by_row, slopes, icpt):
    tiles = LAM_TILES + 4 * STEPS * 4
    return pl.pallas_call(
        share_kernel,
        out_shape=(jax.ShapeDtypeStruct((tiles, 16, 128), BF16),) * 2,
        in_specs=[pl.BlockSpec(memory_space=pltpu.SMEM)] * 2
        + [pl.BlockSpec(memory_space=pltpu.VMEM)] * 3,
        compiler_params=pltpu.CompilerParams(vmem_limit_bytes=60 * 1024 * 1024),
        name="share",
    )(core, row, by_row, slopes, icpt)


def channel_kernel(step, *refs):
    first, last = step == 0, step == STEPS - 1
    count = (3, 2, 2, 1)[step]
    core_ref, words, refs = refs[0], refs[1 : 1 + count], refs[1 + count :]
    if first:
        down_scale_ref, *team, acc_ref, bias_ref, scaled_ref, bounds_ref, down, up = refs
        for k, got_ref in enumerate(team):
            start = (core_ref[0] ^ k) * 16
            for r in range(SPEC):
                rows = pl.ds(pl.multiple_of(r * SHARED + start, 16), 16)
                for c in range(D // 128):
                    cut = slice(c * 128, (c + 1) * 128)
                    lam = got_ref[r * (D // 128) + c].astype(F32)
                    scaled_ref[rows, cut] = (lam * down_scale_ref[:, cut]).astype(BF16)
                    acc_ref[rows, cut] = 0.5 * lam
            rows = pl.ds(pl.multiple_of(start, 16), 16)
            for i in range(STEPS * 4):
                for h in range(4):
                    tile = got_ref[LAM_TILES + i * 4 + h]
                    bounds_ref[i // 4, i % 4, rows, h * 128 : (h + 1) * 128] = tile
        acc_in, bias_in = acc_ref, None
    else:
        scaled_ref, bounds_ref, acc_in, bias_in, *outs, down, up = refs
    words = [w[...] for w in words]
    for h, chunk in enumerate(words):
        for m in range(4):
            for k in range(8):
                rows = m * 256 + k // 2 * 64
                cut = h * CHUNK + k % 2 * 128
                codes = unpack_codes(chunk[k * 64 : (k + 1) * 64], m)
                down[rows : rows + 64, cut : cut + 128] = codes
                rows = h * CHUNK + m * 64
                codes = unpack_codes(chunk[512 + k * 64 : 512 + (k + 1) * 64], m)
                up[rows : rows + 64, k * 128 : (k + 1) * 128] = codes
    scale = [chunk[1024 + h : 1025 + h] for chunk in words for h in range(2)]
    scale = jnp.concatenate(scale, axis=1).astype(F32) * (1.0 / SCALE_ONE)
    pre = jnp.dot(scaled_ref[...], down[...], preferred_element_type=F32)
    width = count * CHUNK
    pre = pre.reshape(SPEC, SHARED, width)
    if first:
        bounds = [
            jnp.concatenate([bounds_ref[0, kind], bounds_ref[STEPS - 1, kind, :, CHUNK:PART]], axis=1)
            for kind in range(4)
        ]
    else:
        bounds = [bounds_ref[step, kind, :, 0:width] for kind in range(4)]
    mid, terms = relaxed(pre, *bounds)
    terms = jnp.sum(terms.reshape(SPEC, SHARED // 8, 8, width), axis=1)
    bias = sum(terms[:, :, k * 128 : (k + 1) * 128] for k in range(width // 128))
    weighted = (mid.reshape(ROWS_DEV, width) * scale).astype(BF16)
    part = jnp.dot(weighted, up[...], preferred_element_type=F32)
    total = acc_in[...] + part
    if not first:
        bias = bias + bias_in[...]
    if last:
        keep_ref, send_ref, bias_ref = outs
        own = core_ref[0] == 0
        turned = total.T.reshape(8, 4, 2, 16, ROWS_DEV)
        for x in range(4):
            chips = slice(x * 8, (x + 1) * 8)
            keep_ref[chips] = jnp.where(own, turned[:, x, 0], turned[:, x, 1])
            send_ref[chips] = jnp.where(own, turned[:, x, 1], turned[:, x, 0]).astype(BF16)
    else:
        if not first:
            acc_ref, bias_ref = outs
        acc_ref[...] = total
    bias_ref[...] = bias


def channel_part(step, core, *rest):
    acc_shape = jax.ShapeDtypeStruct((ROWS_DEV, D), F32)
    bias_shape = jax.ShapeDtypeStruct((SPEC, 8, 128), F32)
    operands = [core, *rest]
    width = (3, 2, 2, 1)[step] * CHUNK
    aliases = {}
    if step == 0:
        scaled_shape = jax.ShapeDtypeStruct((ROWS_DEV, D), BF16)
        bounds_shape = jax.ShapeDtypeStruct((STEPS, 4, SHARED, PART), BF16)
        out_shape = (acc_shape, bias_shape, scaled_shape, bounds_shape)
    elif step == STEPS - 1:
        out_shape = (
            jax.ShapeDtypeStruct((32, 16, ROWS_DEV), F32),
            jax.ShapeDtypeStruct((32, 16, ROWS_DEV), BF16),
            bias_shape,
        )
    else:
        out_shape = (acc_shape, bias_shape)
        aliases = {len(operands) - 2: 0, len(operands) - 1: 1}
    smem, vmem = pl.BlockSpec(memory_space=pltpu.SMEM), pl.BlockSpec(memory_space=pltpu.VMEM)
    return pl.pallas_call(
        functools.partial(channel_kernel, step),
        out_shape=out_shape,
        in_specs=[smem] + [vmem] * (len(operands) - 1),
        out_specs=(vmem,) * len(out_shape),
        scratch_shapes=[pltpu.VMEM((D, width), BF16), pltpu.VMEM((width, D), BF16)],
        input_output_aliases=aliases,
        compiler_params=pltpu.CompilerParams(vmem_limit_bytes=VMEM),
        cost_estimate=pl.CostEstimate(
            flops=4 * ROWS_DEV * width * D,
            bytes_accessed=2 * PACKED * 128 * 4 + 3 * ROWS_DEV * D * 4,
            transcendentals=0,
        ),
        name="channel",
    )(*operands)


def token_kernel(
    got_ref, dense_ref, slopes_ref, icpt_ref, chan_bias_ref, columns_ref, mid_ref, bias_ref
):
    lane = lax.broadcasted_iota(I32, (16, 128), 1) // 32
    for u in range(NTB):
        for a in range(2):
            v = [got_ref[8 * p + u, :, a * 128 : (a + 1) * 128].astype(F32) for p in range(4)]
            for bit in (1, 2):
                low = (lane & bit) == 0
                new = list(v)
                for p in range(4):
                    if p & bit == 0:
                        q = p + bit
                        new[p] = jnp.where(low, v[p], pltpu.roll(v[q], 32 * bit, 1))
                        new[q] = jnp.where(low, pltpu.roll(v[p], 128 - 32 * bit, 1), v[q])
                v = new
            for q in range(4):
                r = 4 * a + q
                columns_ref[r * 16 : (r + 1) * 16, u * 128 : (u + 1) * 128] = v[q].astype(BF16)
    pre = jnp.dot(columns_ref[...], dense_ref[...], preferred_element_type=F32)
    pre = pre.reshape(SPEC, 16, TH)
    mid, terms = relaxed(pre, slopes_ref[0], slopes_ref[1], icpt_ref[0], icpt_ref[1])
    mid_ref[...] = mid.reshape(SPEC * 16, TH).astype(BF16)
    terms = terms[:, 0:8, :] + terms[:, 8:16, :]
    terms = sum(terms[:, :, k * 128 : (k + 1) * 128] for k in range(NHB)) + chan_bias_ref[...]
    by_row = jnp.sum(jnp.sum(terms, axis=1), axis=1, keepdims=True)
    row = lax.broadcasted_iota(I32, (SPEC, 128), 0)
    lane = lax.broadcasted_iota(I32, (SPEC, 128), 1)
    line = jnp.sum(jnp.where(row == lane, by_row, 0.0), axis=0, keepdims=True)
    bias_ref[...] = jnp.broadcast_to(line[None], bias_ref.shape)


def token_mlp(got, dense_out, slopes, icpt, chan_bias):
    return pl.pallas_call(
        token_kernel,
        out_shape=(
            jax.ShapeDtypeStruct((SPEC * 16, TOK), BF16),
            jax.ShapeDtypeStruct((SPEC * 16, TH), BF16),
            jax.ShapeDtypeStruct((64, 1, 128), F32),
        ),
        compiler_params=pltpu.CompilerParams(vmem_limit_bytes=VMEM),
        name="token",
    )(got, dense_out, slopes, icpt, chan_bias)


def back_kernel(columns_ref, mid_ref, dense_ref, out_ref):
    back = jnp.dot(mid_ref[...], dense_ref[...], preferred_element_type=F32)
    out_ref[...] = (columns_ref[...].astype(F32) + back).astype(BF16)


def token_back(columns, mid, dense_in):
    return pl.pallas_call(
        back_kernel,
        out_shape=jax.ShapeDtypeStruct((SPEC * 16, TOK), BF16),
        compiler_params=pltpu.CompilerParams(vmem_limit_bytes=VMEM),
        name="back",
    )(columns, mid, dense_in)


def on_device(
    lam_out,
    q_down,
    down_scale,
    q_up,
    up_scale,
    chan_slopes,
    chan_icpt,
    tok_in_blocks,
    tok_out_blocks,
    block_cells,
    tok_slopes,
    tok_icpt,
):
    core = lax.axis_index("core").astype(I32).reshape(1)
    row = lax.axis_index("rows").astype(I32).reshape(1)
    tok_dev = lam_out.shape[0]
    slices = lax.axis_size("rows")
    ahead = [(i * 2, (i + 1) % slices * 2) for i in range(slices)]
    behind = [(i * 2 + 1, (i - 1) % slices * 2 + 1) for i in range(slices)]

    def forward(words, pairs):
        return tuple(lax.ppermute(w, ("rows", "core"), pairs) for w in words)

    own = tuple(pack(chain, core, q_down, q_up, up_scale) for chain in range(2))
    first = forward(own, ahead + behind)
    _, lam, *bounds = lax.optimization_barrier((own, lam_out, chan_slopes, chan_icpt))
    keep_part, send_part = share(
        core, row, jnp.swapaxes(lam, 0, 1), *(b.reshape(2, tok_dev, CH) for b in bounds)
    )
    words, send_part = lax.optimization_barrier((first[1], send_part))
    second = forward((first[0], words), ahead + behind)
    other_part = lax.ppermute(send_part, "core", SWAP)
    words, other_part = lax.optimization_barrier((second[0], other_part))
    third = forward((words, second[1]), ahead + behind)
    carried = channel_part(0, core, *first, own[0], down_scale.reshape(1, D), keep_part, other_part)
    acc, chan_bias, *given = carried
    acc, chan_bias = channel_part(1, core, *second, *given, acc, chan_bias)
    far = forward(third[:1], ahead + behind)

    dense_in, dense_out = dense_blocks(block_cells, tok_in_blocks, tok_out_blocks)
    slopes = jnp.transpose(tok_slopes, (0, 2, 3, 1)).reshape(2, 16, TH)
    icpt = jnp.transpose(tok_icpt, (0, 2, 3, 1)).reshape(2, 16, TH)

    acc, chan_bias = channel_part(2, core, *third, *given, acc, chan_bias)
    keep, send, chan_bias = channel_part(3, core, *far, *given, acc, chan_bias)
    summed = (keep + lax.ppermute(send, "core", SWAP).astype(F32)).astype(BF16)
    got = lax.all_to_all(summed, ("x", "z"), 0, 0, tiled=True)
    columns, mid, own_bias = token_mlp(got, dense_out, slopes, icpt, chan_bias)
    all_bias = lax.all_to_all(own_bias, MP, 0, 0, tiled=True)
    lam_in = token_back(columns, mid, dense_in)
    lam_in = jnp.transpose(lam_in.reshape(SPEC, 16, TOK), (2, 0, 1))
    return (lam_in, jnp.sum(all_bias, axis=(0, 1))[:SPEC])


def solution(mesh):
    axes = Mesh(mesh.devices.reshape(8, 8, 4, 2), ("rows",) + MP)
    return jax.shard_map(
        on_device,
        mesh=axes,
        in_specs=(
            P(MP, "rows", None),
            P(None, "rows"),
            P(),
            P("rows", None),
            P("rows"),
            P(None, MP, "rows", None),
            P(None, MP, "rows", None),
            P(),
            P(),
            P(),
            P(None, None, "rows", MP),
            P(None, None, "rows", MP),
        ),
        out_specs=(P(None, "rows", MP), P("rows")),
        check_vma=False,
    )
```
